128 devices in a mesh: grp: 8 (over x, core), dev: 16 (over y, z).
Axes of the slice: x: 4, y: 4, z: 4, core: 2. Of those that a mesh axis runs over, the one named last changes fastest.
Arguments:
- ref_pos: float32 [3, 1048576], P(None, ('grp', 'dev')), may hold values from -4 to 4
- displacement: float32 [3, 1048576], P(None, ('grp', 'dev')), may hold values from -0.6 to 0.6
- velocity: float32 [3, 1048576], P(None, ('grp', 'dev')), may hold values from -6 to 6
- node_mass: float32 [1048576], P(('grp', 'dev')), may hold values from 0.5 to 2
- elem_nodes: int32 [4, 1048576], P(None, ('grp', 'dev')), may hold values from 0 to 8191
- elem_part: int32 [1048576], P(('grp', 'dev')), may hold values from 0 to 511, as said below
- elem_scale: float32 [1048576], P(('grp', 'dev')), may hold values from 0.5 to 2
- part_stiff: float32 [512], P(('grp', 'dev')), may hold values from 1 to 100
- shared: int32 [2, 262144], P(None, ('grp', 'dev')), may hold values from 0 to 8191, as said below
- seg_node: int32 [8192, 128], P(('grp', 'dev')), may hold values from 0 to 8191
- seg_mask: int32 [8192, 128], P(('grp', 'dev')), may hold values 0 or 1
- send_blk: int32 [128, 128, 5], P(('grp', 'dev')), may hold values from 0 to 63
- pair_a: int32 [65536], P(('grp', 'dev')), may hold values from 0 to 63
- pair_slot: int32 [65536], P(('grp', 'dev')), may hold values from 0 to 639
- pair_mask: int32 [65536], P(('grp', 'dev')), may hold values from 0 to 1, as said below
Outputs:
- new_displace: float32 [3, 1048576], P(None, ('grp', 'dev'))
- new_velocity: float32 [3, 1048576], P(None, ('grp', 'dev'))
The draws below stay inside these ranges and needn't reach their ends.
Inputs may be any that keep to these rules, and one draw needn't show every extreme that they name: `elem_part`: the elements of device d belong to parts d * 4 to (d + 1) * 4 - 1. `shared`: the 4096 entries of one device are different nodes; row 1 of device k and row 0 of device k + 1 of the same group name the same physical nodes, entry by entry. `pair_mask`: in each device's 512 pair slots the live ones come first; each device has 128 or more live, and some device has all 512 live.
All inputs are finite; a program needn't handle non-finite values. No bound on the sum of `seg_mask` on one device may be relied on, other than what follows from the above.
Results may differ from the reference program's by a relative error of at most 0.000062.
Values sent between devices are 32-bit elements; how exact they have to be, the bound alone decides.
No kernel may reach another device: no remote copies, remote signals or barrier semaphores. Data moves between devices by JAX's collectives and lax.ppermute only.
A program may use at most 128 MiB of HBM per device.

```python
import math
import jax
import jax.numpy as jnp
from jax import lax

NODE_DEV = 8192
SHARE = 2048
BLK_DEV = 64
PAIR_DEV = 512
SEG = 128
CAP = 5
PART_DEV = 4
ELEM_DEV = 8192
NODES = 1048576
ELEMS = 1048576
BLOCKS = 8192
PAIRS = 65536
PARTS_SIZE = 512
N_GRP = 8
N_DEV = 16
DEVICES = 128


def draw_elem_part(key, part):
    owner_device = jnp.arange(ELEMS, dtype=jnp.int32) // ELEM_DEV
    offset = jax.random.randint(key, (ELEMS,), 0, PART_DEV, dtype=jnp.int32)
    return owner_device * PART_DEV + offset


def draw_shared(key, part):
    device_count = NODES // NODE_DEV
    device_keys = jax.random.split(jax.random.fold_in(key, 11), device_count)

    def one_device(device_key):
        return jax.random.permutation(device_key, NODE_DEV)[:2 * SHARE].astype(jnp.int32)
    picked = jax.vmap(one_device)(device_keys)
    return jnp.moveaxis(picked.reshape(device_count, 2, SHARE), 1, 0).reshape(2, device_count * SHARE)


def draw_pair_mask(key, part):
    device_count = PAIRS // PAIR_DEV
    live_key, full_key = jax.random.split(jax.random.fold_in(key, 23))
    live_count = jax.random.randint(live_key, (device_count,), PAIR_DEV // 4, PAIR_DEV + 1, dtype=jnp.int32)
    full_device = jax.random.randint(full_key, (), 0, device_count, dtype=jnp.int32)
    live_count = jnp.where(jnp.arange(device_count, dtype=jnp.int32) == full_device, PAIR_DEV, live_count)
    positions = jnp.arange(PAIR_DEV, dtype=jnp.int32)
    return (positions[None, :] < live_count[:, None]).astype(jnp.int32).reshape(-1)


def touch_ends(drawn, rng, low, top_value):
    shape = drawn.shape
    spot = [jax.random.randint(jax.random.fold_in(rng, axis), (), 0, shape[axis]) for axis in range(len(shape))]
    drawn = drawn.at[tuple(spot)].set(low)
    longest = shape.index(max(shape))
    spot[longest] = (spot[longest] + 1) % shape[longest]
    return drawn.at[tuple(spot)].set(top_value)


def block_levels(own_key, extent, shards, low, high):
    def one(dim, shards_of):
        steps = jax.random.uniform(jax.random.fold_in(jax.random.fold_in(own_key, 6), dim), (shards_of,), jnp.float32, low / len(shards), high / len(shards))
        return jnp.repeat(jnp.exp(steps), extent[dim] // shards_of).reshape((-1,) + (1,) * (len(extent) - dim - 1))

    level = one(*shards[0])
    for cut in shards[1:]:
        level = level * one(*cut)
    return level


def centred(key, extent, scale, most, cuts=(), kind=jnp.bfloat16):
    result = scale * jax.random.normal(key, extent, jnp.float32)
    if cuts:
        result = result * block_levels(key, extent, cuts, -0.22, 0.18)
    return jnp.clip(result, -most, most).astype(kind)


def setup_inputs(seed: int = 0) -> dict:
    seeds = jax.random.split(jax.random.key(seed), 16)
    return {
        "ref_pos": centred(seeds[0], (3, NODES), 0.7, 4.0, ((1, 128),), jnp.float32),
        "displacement": centred(seeds[1], (3, NODES), 0.1, 0.6, ((1, 128),), jnp.float32),
        "velocity": centred(seeds[2], (3, NODES), 1.0, 6.0, ((1, 128),), jnp.float32),
        "node_mass": jnp.clip(jnp.exp(math.log(2.0) - 1.3862944 * jax.random.uniform(seeds[3], (NODES,), jnp.float32) ** block_levels(seeds[3], (NODES,), ((0, 128),), -0.2, 0.2)), 0.5, 2.0),
        "elem_nodes": touch_ends(jax.random.randint(seeds[4], (4, ELEMS), 0, NODE_DEV), jax.random.fold_in(seeds[4], 1), 0, NODE_DEV - 1).astype(jnp.int32),
        "elem_part": draw_elem_part(jax.random.fold_in(seeds[15], 71), 0),
        "elem_scale": jnp.clip(jnp.exp(math.log(2.0) - 1.3862944 * jax.random.uniform(seeds[6], (ELEMS,), jnp.float32) ** block_levels(seeds[6], (ELEMS,), ((0, 128),), -0.2, 0.2)), 0.5, 2.0),
        "part_stiff": jnp.clip(jnp.exp(math.log(100.0) - 4.6051702 * jax.random.uniform(seeds[7], (PARTS_SIZE,), jnp.float32) ** block_levels(seeds[7], (PARTS_SIZE,), ((0, 128),), -0.2, 0.2)), 1.0, 100.0),
        "shared": draw_shared(jax.random.fold_in(seeds[15], 71), 0),
        "seg_node": touch_ends(jax.random.randint(seeds[9], (BLOCKS, SEG), 0, NODE_DEV), jax.random.fold_in(seeds[9], 1), 0, NODE_DEV - 1).astype(jnp.int32),
        "seg_mask": touch_ends((jax.random.randint(seeds[10], (BLOCKS, SEG), 0, 8) < 7).astype(jnp.int32), jax.random.fold_in(seeds[10], 1), 0, 1),
        "send_blk": touch_ends(jax.random.randint(seeds[11], (DEVICES, DEVICES, CAP), 0, BLK_DEV), jax.random.fold_in(seeds[11], 1), 0, BLK_DEV - 1).astype(jnp.int32),
        "pair_a": touch_ends(jax.random.randint(seeds[12], (PAIRS,), 0, BLK_DEV), jax.random.fold_in(seeds[12], 1), 0, BLK_DEV - 1).astype(jnp.int32),
        "pair_slot": touch_ends(jax.random.randint(seeds[13], (PAIRS,), 0, DEVICES * CAP), jax.random.fold_in(seeds[13], 1), 0, (DEVICES * CAP) - 1).astype(jnp.int32),
        "pair_mask": draw_pair_mask(jax.random.fold_in(seeds[15], 71), 0),
    }


SPRINGS = ((0, 1, 1.0), (1, 2, 1.0), (2, 3, 1.0), (3, 0, 1.0), (0, 2, 0.5), (1, 3, 0.5))
COURANT = 0.5

def element_forces(displacement, elem_nodes, elem_stiff):
    corner = displacement[:, elem_nodes]
    corner_force = [jnp.zeros_like(corner[:, 0]) for corner_index in range(4)]
    for head_node, tail_node, weight in SPRINGS:
        pull_term = weight * elem_stiff * (corner[:, tail_node] - corner[:, head_node])
        corner_force[head_node] = corner_force[head_node] + pull_term
        corner_force[tail_node] = corner_force[tail_node] - pull_term
    stacked = jnp.stack(corner_force, 1)
    summed = jnp.zeros_like(displacement)
    return summed.at[:, elem_nodes.reshape(-1)].add(stacked.reshape(3, -1))

def pair_forces(near_pos, far_pos, near_mask, far_mask, live_pair):
    offset = near_pos[:, :, :, None] - far_pos[:, :, None, :]
    weights = jnp.exp(-lax.optimization_barrier(jnp.sum(offset * offset, 1)))
    weights = weights * (near_mask[:, :, None] * far_mask[:, None, :]) * live_pair[:, None, None]
    pushed = lax.optimization_barrier(jnp.sum(weights[:, None] * offset, 3))
    recoil = -lax.optimization_barrier(jnp.sum(weights[:, None] * offset, 2))
    return (pushed, recoil)

def contact_sums(own_blocks, own_mask, recv_blocks, recv_mask, pair_first, pair_second, pair_live):
    pair_count = pair_first.shape[0]
    group_width = math.gcd(pair_count, 32)
    seg_width = own_blocks.shape[2]

    def one_group(group_index):
        group_start = group_index * group_width
        first_ids = lax.dynamic_slice_in_dim(pair_first, group_start, group_width)
        second_ids = lax.dynamic_slice_in_dim(pair_second, group_start, group_width)
        live_part = lax.dynamic_slice_in_dim(pair_live, group_start, group_width)
        return pair_forces(own_blocks[first_ids], recv_blocks[second_ids], own_mask[first_ids], recv_mask[second_ids], live_part)
    pushed, recoil = lax.map(one_group, jnp.arange(pair_count // group_width, dtype=jnp.int32))
    pushed = pushed.reshape(pair_count, 3, seg_width)
    recoil = recoil.reshape(pair_count, 3, seg_width)
    own_force = jax.ops.segment_sum(pushed, pair_first, num_segments=own_blocks.shape[0])
    far_force = jax.ops.segment_sum(recoil, pair_second, num_segments=recv_blocks.shape[0])
    return (own_force, far_force)

def reference(ref_pos, displacement, velocity, node_mass, elem_nodes, elem_part, elem_scale, part_stiff, shared, seg_node, seg_mask, send_blk, pair_a, pair_slot, pair_mask):
    devices = N_GRP * N_DEV
    elem_stiff = part_stiff[elem_part] * elem_scale

    def by_device(array, per_device):
        shaped = array.reshape(array.shape[:-1] + (devices, per_device))
        return jnp.moveaxis(shaped, -2, 0)
    ref_dev = by_device(ref_pos, NODE_DEV)
    disp_dev = by_device(displacement, NODE_DEV)
    vel_dev = by_device(velocity, NODE_DEV)
    mass_dev = by_device(node_mass, NODE_DEV)
    nodes_dev = by_device(elem_nodes, ELEM_DEV)
    stiff_dev = by_device(elem_stiff, ELEM_DEV)
    shared_dev = by_device(shared, SHARE)
    seg_dev = seg_node.reshape(devices, BLK_DEV, SEG)
    mask_dev = seg_mask.astype(jnp.float32).reshape(devices, BLK_DEV, SEG)
    first_dev = pair_a.reshape(devices, PAIR_DEV)
    second_dev = pair_slot.reshape(devices, PAIR_DEV)
    live_dev = pair_mask.astype(jnp.float32).reshape(devices, PAIR_DEV)

    def local_step(pieces):
        ref_local, disp_local, mass_local, nodes_local, stiff_local, seg_local = pieces
        forces = element_forces(disp_local, nodes_local, stiff_local)
        elem_mass = lax.optimization_barrier(jnp.min(mass_local[nodes_local], 0))
        step_limit = jnp.min(COURANT * jnp.sqrt(elem_mass / stiff_local))
        position = ref_local + disp_local
        blocks = jnp.moveaxis(position[:, seg_local], 1, 0)
        return (forces, step_limit, blocks)
    forces, limits, blocks = lax.map(local_step, (ref_dev, disp_dev, mass_dev, nodes_dev, stiff_dev, seg_dev))
    time_step = jnp.min(limits)
    source_ids = jnp.arange(devices, dtype=jnp.int32)[:, None]

    def contact_step(device_index):
        chosen = send_blk[:, device_index, :]
        arrived = blocks[source_ids, chosen].reshape(devices * CAP, 3, SEG)
        arrived_mask = mask_dev[source_ids, chosen].reshape(devices * CAP, SEG)
        return contact_sums(blocks[device_index], mask_dev[device_index], arrived, arrived_mask, first_dev[device_index], second_dev[device_index], live_dev[device_index])
    own_force, far_force = lax.map(contact_step, jnp.arange(devices, dtype=jnp.int32))

    def return_step(device_index):
        slab_force = lax.dynamic_slice_in_dim(far_force, device_index * CAP, CAP, 1)
        return jax.ops.segment_sum(slab_force.reshape(devices * CAP, 3, SEG), send_blk[device_index].reshape(-1), num_segments=BLK_DEV)
    returned = lax.map(return_step, jnp.arange(devices, dtype=jnp.int32))
    seg_force = own_force + returned

    def node_step(pieces):
        force_local, seg_local, seg_local_force = pieces
        flat_force = jnp.moveaxis(seg_local_force, 1, 0).reshape(3, -1)
        return force_local.at[:, seg_local.reshape(-1)].add(flat_force)
    totals = lax.map(node_step, (forces, seg_dev, seg_force))
    shaped = totals.reshape(N_GRP, N_DEV, 3, NODE_DEV)
    share_grid = shared_dev.reshape(N_GRP, N_DEV, 2, SHARE)

    def pick_rows(force_local, index_list):
        return force_local[:, index_list]
    picker = jax.vmap(jax.vmap(pick_rows))
    right_rows = picker(shaped, share_grid[:, :, 1])
    left_rows = picker(shaped, share_grid[:, :, 0])
    zero_rows = jnp.zeros_like(right_rows[:, :1])
    from_lower = jnp.concatenate([zero_rows, right_rows[:, :-1]], 1)
    from_upper = jnp.concatenate([left_rows[:, 1:], zero_rows], 1)

    def place_rows(force_local, index_list, lower_part, upper_part):
        return force_local.at[:, index_list[0]].add(lower_part).at[:, index_list[1]].add(upper_part)
    assembled = jax.vmap(jax.vmap(place_rows))(shaped, share_grid, from_lower, from_upper)
    assembled = assembled.reshape(devices, 3, NODE_DEV)
    accelerate = assembled / mass_dev[:, None, :]
    new_velocity = vel_dev + time_step * accelerate
    new_displace = disp_dev + time_step * new_velocity
    return (jnp.moveaxis(new_displace, 0, 1).reshape(3, -1), jnp.moveaxis(new_velocity, 0, 1).reshape(3, -1))
```

```python
import math
from functools import partial

import jax
import jax.numpy as jnp
from jax import lax
from jax.experimental import pallas as pl
from jax.experimental.pallas import tpu as pltpu
from jax.sharding import PartitionSpec as P

SPRINGS = ((0, 1, 1.0), (1, 2, 1.0), (2, 3, 1.0), (3, 0, 1.0), (0, 2, 0.5), (1, 3, 0.5))
COURANT = 0.5
LOW = 256
PIECES = 3
SCALE = math.sqrt(math.log2(math.e))
PARK = 1.0e3
f32 = jnp.float32
bf16 = jnp.bfloat16


def pieces_of(x, count=PIECES):
    out = []
    for _ in range(count):
        head = x.astype(bf16)
        out.append(head)
        x = x - head.astype(f32)
    return out


def low_hot(idx):
    low = idx & (LOW - 1)
    rows = lax.broadcasted_iota(jnp.int32, (LOW, idx.shape[1]), 0)
    return jnp.where(rows == low, 1.0, 0.0).astype(bf16)


def high_mask(idx, high):
    rows = lax.broadcasted_iota(jnp.int32, (high, idx.shape[1]), 0)
    return rows == (idx >> 8)


def fill_table(tab, at, ref, row, high):
    for h in range(high):
        tab[at + h : at + h + 1, :] = ref[row : row + 1, h * LOW : (h + 1) * LOW]


def split_table(cut, tab):
    rows = tab.shape[0]
    for p, piece in enumerate(pieces_of(tab[...])):
        cut[p * rows : (p + 1) * rows, :] = piece


def pick(cut, hot, mask, comps, high):
    found = jnp.dot(cut[...], hot, preferred_element_type=f32)
    rows = comps * high
    found = (found[:rows] + found[rows : 2 * rows]) + found[2 * rows :]
    return [
        jnp.sum(jnp.where(mask, found[c * high : (c + 1) * high], 0.0), 0, keepdims=True)
        for c in range(comps)
    ]


def spread(force, mask, high):
    rows = [[], [], []]
    for value in force:
        wide = jnp.broadcast_to(value, mask.shape)
        for p, piece in enumerate(pieces_of(jnp.where(mask, wide, 0.0))):
            rows[p].append(piece)
    return jnp.concatenate(rows[0] + rows[1] + rows[2], 0)


def add_hot(left, hot):
    return lax.dot_general(left, hot, (((1,), (1,)), ((), ())), preferred_element_type=f32)


def send_body(send_ref, disp_ref, ref_ref, seg_ref, mask_ref, own_ref, out_ref, tab, cut):
    high = disp_ref.shape[1] // LOW
    blocks = seg_ref.shape[0]
    for c in range(3):
        fill_table(tab, c * high, disp_ref, c, high)
    for c in range(3):
        for h in range(high):
            at = c * high + h
            tab[at : at + 1, :] += ref_ref[c : c + 1, h * LOW : (h + 1) * LOW]
    split_table(cut, tab)
    group = 8

    def some(g, carry):
        base = pl.multiple_of(g * group, group)
        seg = seg_ref[pl.ds(base, group), :]
        idx = jnp.concatenate([seg[k : k + 1] for k in range(group)], 1)
        xyz = pick(cut, low_hot(idx), high_mask(idx, high), 3, high)
        weight = mask_ref[pl.ds(base, group), :].astype(f32)
        for k in range(group):
            for c in range(3):
                own_ref[base + k, c : c + 1, :] = xyz[c][:, k * 128 : (k + 1) * 128]
            own_ref[base + k, 3:4, :] = weight[k : k + 1]
        return carry

    lax.fori_loop(0, blocks // group, some, 0)
    peers, cap = out_ref.shape[0], out_ref.shape[1]

    def send(d, carry):
        for c in range(cap):
            out_ref[d, c] = own_ref[send_ref[d * cap + c]]
        return carry

    lax.fori_loop(0, peers, send, 0, unroll=4)


def element_body(
    first_ref, stiff_ref, disp_ref, mass_ref, nodes_ref, part_ref, scale_ref, tot_ref, lim_ref, tab, cut, acc
):
    high = disp_ref.shape[1] // LOW
    width = 256
    parts = stiff_ref.shape[0]
    for c in range(3):
        fill_table(tab, c * high, disp_ref, c, high)
    fill_table(tab, 3 * high, mass_ref, 0, high)
    split_table(cut, tab)
    acc[...] = jnp.zeros_like(acc)

    def some(g, limit):
        at = pl.ds(pl.multiple_of(g * width, width), width)
        part = part_ref[:, at] - first_ref[0]
        stiff = jnp.zeros(part.shape, f32)
        for k in range(parts):
            stiff = jnp.where(part == k, stiff_ref[k], stiff)
        stiff = stiff * scale_ref[:, at]
        nodes = nodes_ref[:, at]
        idx = jnp.concatenate([nodes[k : k + 1] for k in range(4)], 1)
        hot = low_hot(idx)
        mask = high_mask(idx, high)
        found = pick(cut, hot, mask, 4, high)
        corner = [[found[c][:, k * width : (k + 1) * width] for c in range(4)] for k in range(4)]
        mass = jnp.minimum(
            jnp.minimum(corner[0][3], corner[1][3]), jnp.minimum(corner[2][3], corner[3][3])
        )
        force = [[jnp.zeros((1, width), f32)] * 3 for _ in range(4)]
        for head, tail, weight in SPRINGS:
            pull = weight * stiff
            for c in range(3):
                term = pull * (corner[tail][c] - corner[head][c])
                force[head][c] = force[head][c] + term
                force[tail][c] = force[tail][c] - term
        joined = [jnp.concatenate([force[k][c] for k in range(4)], 1) for c in range(3)]
        acc[...] += add_hot(spread(joined, mask, high), hot)
        return jnp.minimum(limit, COURANT * jnp.sqrt(mass / stiff))

    limit = lax.fori_loop(
        0, nodes_ref.shape[1] // width, some, jnp.full((1, width), jnp.inf, f32)
    )
    rows = 3 * high
    tot_ref[...] = (acc[2 * rows :] + acc[rows : 2 * rows]) + acc[:rows]
    lim_ref[...] = jnp.broadcast_to(jnp.min(limit, 1, keepdims=True), lim_ref.shape)


def contact_body(
    near_ref, far_ref, own_ref, recv_ref, live_ref, lim_ref, own_out, far_out, wide, total, remote
):
    blocks = own_ref.shape[0]
    slots = recv_ref.shape[0]
    seg = own_ref.shape[2]
    cap = 5

    def park(block):
        weight = block[3:4]
        out = [jnp.where(weight > 0.5, block[0:1] * SCALE, PARK)]
        return out + [block[c : c + 1] * SCALE for c in range(1, 3)]

    def widen(b, carry):
        rows = park(own_ref[b])
        for c in range(3):
            wide[b, c] = jnp.broadcast_to(rows[c], (seg, seg)).T
            total[b, c] = jnp.zeros((seg, seg), f32)
        return carry

    lax.fori_loop(0, blocks, widen, 0)

    def ready(s, carry):
        block = recv_ref[s]
        remote[s, 0:1] = jnp.where(block[3:4] > 0.5, block[0:1] * SCALE, -PARK)
        for c in range(1, 3):
            remote[s, c : c + 1] = block[c : c + 1] * SCALE
        return carry

    lax.fori_loop(0, slots, ready, 0, unroll=4)
    far_out[...] = jnp.zeros_like(far_out)
    far_out[:, 15:16, :] = jnp.broadcast_to(lim_ref[...][None], (far_out.shape[0], 1, seg))
    live = jnp.sum(live_ref[...])

    def pair(p, carry):
        b = near_ref[p]
        s = far_ref[p]
        there = [jnp.broadcast_to(remote[s, c : c + 1, :], (8, seg)) for c in range(3)]
        recoil = [None] * 3
        for v in range(seg // 8):
            at = pl.ds(v * 8, 8)
            gap = [wide[b, c, at, :] - there[c] for c in range(3)]
            far = gap[0] * gap[0] + gap[1] * gap[1] + gap[2] * gap[2]
            weight = jnp.exp2(-far)
            for c in range(3):
                push = weight * gap[c]
                total[b, c, at, :] += push
                recoil[c] = push if recoil[c] is None else recoil[c] + push
        d = (s * 52429) >> 18
        row = (s - d * cap) * 3
        for c in range(3):
            far_out[d, pl.ds(row + c, 1), :] -= jnp.sum(recoil[c], 0, keepdims=True) * (1.0 / SCALE)
        return carry

    lax.fori_loop(0, live, pair, 0)

    def close(b, carry):
        for c in range(3):
            own_out[b, c : c + 1, :] = jnp.sum(total[b, c].T, 0, keepdims=True) * (1.0 / SCALE)
        return carry

    lax.fori_loop(0, blocks, close, 0)


def seg_body(
    send_ref, back_ref, own_ref, seg_ref, int_ref, share_ref, tot_ref, low_ref, up_ref, lim_ref, sums, cut, acc
):
    blocks = own_ref.shape[0]
    peers = back_ref.shape[0]
    cap = 5
    high = int_ref.shape[0] // 3
    sums[...] = jnp.zeros_like(sums)

    def take(d, carry):
        for c in range(cap):
            b = send_ref[d * cap + c]
            sums[c, b, 0:3, :] += back_ref[d, 3 * c : 3 * c + 3, :]
        return carry

    lax.fori_loop(0, peers, take, 0)
    acc[...] = jnp.zeros_like(acc)
    group = 8

    def some(g, carry):
        base = pl.multiple_of(g * group, group)
        seg = seg_ref[pl.ds(base, group), :]
        idx = jnp.concatenate([seg[k : k + 1] for k in range(group)], 1)
        blocks_in = []
        for k in range(group):
            b = base + k
            part = sums[0, b, 0:3] + sums[1, b, 0:3] + sums[2, b, 0:3] + sums[3, b, 0:3] + sums[4, b, 0:3]
            blocks_in.append(part + own_ref[b])
        force = jnp.concatenate(blocks_in, 1)
        left = spread([force[c : c + 1] for c in range(3)], high_mask(idx, high), high)
        acc[...] += add_hot(left, low_hot(idx))
        return carry

    lax.fori_loop(0, blocks // group, some, 0)
    rows = 3 * high
    tot_ref[...] = ((acc[2 * rows :] + acc[rows : 2 * rows]) + acc[:rows]) + int_ref[...]
    split_table(cut, tot_ref)
    count = share_ref.shape[1]
    for row, out in ((0, low_ref), (1, up_ref)):
        for at in range(0, count, 1024):
            idx = share_ref[row : row + 1, at : at + 1024]
            picked = pick(cut, low_hot(idx), high_mask(idx, high), 3, high)
            for c in range(3):
                out[c : c + 1, at : at + 1024] = picked[c]
    lim = jnp.min(back_ref[:, 15, :], 0, keepdims=True)
    lim_ref[...] = lim


def last_body(
    lim_ref, tot_ref, share_ref, low_ref, up_ref, vel_ref, disp_ref, mass_ref, new_disp, new_vel, acc
):
    high = tot_ref.shape[0] // 3
    count = share_ref.shape[1]
    total = jnp.zeros(acc.shape, f32)
    for row, src in ((0, low_ref), (1, up_ref)):
        for at in range(0, count, 1024):
            idx = share_ref[row : row + 1, at : at + 1024]
            force = [src[c : c + 1, at : at + 1024] for c in range(3)]
            total = total + add_hot(spread(force, high_mask(idx, high), high), low_hot(idx))
    rows = 3 * high
    acc[0:rows] = ((total[2 * rows :] + total[rows : 2 * rows]) + total[:rows]) + tot_ref[...]
    step = jnp.min(lim_ref[...], 1, keepdims=True)
    for h in range(high):
        at = slice(h * LOW, (h + 1) * LOW)
        mass = mass_ref[0:1, at]
        for c in range(3):
            vel = vel_ref[c : c + 1, at] + step * (acc[c * high + h : c * high + h + 1, :] / mass)
            new_vel[c : c + 1, at] = vel
            new_disp[c : c + 1, at] = disp_ref[c : c + 1, at] + step * vel


def vmem(count):
    return [pl.BlockSpec(memory_space=pltpu.VMEM)] * count


def smem(count):
    return [pl.BlockSpec(memory_space=pltpu.SMEM)] * count


def struct(*shape):
    return jax.ShapeDtypeStruct(shape, f32)


def send_call(send, disp, ref_pos, seg_node, seg_mask, peers):
    high = disp.shape[1] // LOW
    blocks, seg = seg_node.shape
    return pl.pallas_call(
        send_body,
        out_shape=(struct(blocks, 4, seg), struct(peers, send.shape[0] // peers, 4, seg)),
        in_specs=smem(1) + vmem(4),
        out_specs=tuple(vmem(2)),
        scratch_shapes=[
            pltpu.VMEM((3 * high, LOW), f32),
            pltpu.VMEM((PIECES * 3 * high, LOW), bf16),
        ],
    )(send, disp, ref_pos, seg_node, seg_mask)


def element_call(first, stiff, disp, mass, nodes, part, scale):
    high = disp.shape[1] // LOW
    return pl.pallas_call(
        element_body,
        out_shape=(struct(3 * high, LOW), struct(1, 128)),
        in_specs=smem(2) + vmem(5),
        out_specs=tuple(vmem(2)),
        scratch_shapes=[
            pltpu.VMEM((4 * high, LOW), f32),
            pltpu.VMEM((PIECES * 4 * high, LOW), bf16),
            pltpu.VMEM((PIECES * 3 * high, LOW), f32),
        ],
    )(first, stiff, disp, mass, nodes, part, scale)


def contact_call(pair_a, pair_slot, own, recv, live, lim, peers):
    blocks, _, seg = own.shape
    slots = recv.shape[0]
    return pl.pallas_call(
        contact_body,
        out_shape=(struct(blocks, 3, seg), struct(peers, 16, seg)),
        in_specs=smem(2) + vmem(4),
        out_specs=tuple(vmem(2)),
        scratch_shapes=[
            pltpu.VMEM((blocks, 3, seg, seg), f32),
            pltpu.VMEM((blocks, 3, seg, seg), f32),
            pltpu.VMEM((slots, 4, seg), f32),
        ],
        compiler_params=pltpu.CompilerParams(vmem_limit_bytes=56 << 20),
    )(pair_a, pair_slot, own, recv, live, lim)


def seg_call(send, back, own, seg_node, inner, shared):
    high = inner.shape[0] // 3
    count = shared.shape[1]
    return pl.pallas_call(
        seg_body,
        out_shape=(struct(3 * high, LOW), struct(3, count), struct(3, count), struct(1, 128)),
        in_specs=smem(1) + vmem(5),
        out_specs=tuple(vmem(4)),
        scratch_shapes=[
            pltpu.VMEM((5, own.shape[0], 4, 128), f32),
            pltpu.VMEM((PIECES * 3 * high, LOW), bf16),
            pltpu.VMEM((PIECES * 3 * high, LOW), f32),
        ],
    )(send, back, own, seg_node, inner, shared)


def last_call(lim, total, shared, lower, upper, vel, disp, mass):
    high = total.shape[0] // 3
    return pl.pallas_call(
        last_body,
        out_shape=(struct(*disp.shape), struct(*disp.shape)),
        in_specs=vmem(8),
        out_specs=tuple(vmem(2)),
        scratch_shapes=[pltpu.VMEM((PIECES * 3 * high, LOW), f32)],
    )(lim, total, shared, lower, upper, vel, disp, mass)


def shifted(value, axis, steps):
    count = lax.axis_size(axis)
    first, last = (max(0, -steps), min(count, count - steps))
    return lax.ppermute(value, axis, [(source, source + steps) for source in range(first, last)])


def shards(
    ref_pos,
    displacement,
    velocity,
    node_mass,
    elem_nodes,
    elem_part,
    elem_scale,
    part_stiff,
    shared,
    seg_node,
    seg_mask,
    send_blk,
    pair_a,
    pair_slot,
    pair_mask,
):
    peers = lax.axis_size("grp") * lax.axis_size("dev")
    send = send_blk.reshape(-1)
    mass = node_mass.reshape(1, -1)
    own, outgoing = send_call(send, displacement, ref_pos, seg_node, seg_mask, peers)
    arrived = lax.all_to_all(outgoing, ("grp", "dev"), split_axis=0, concat_axis=0, tiled=True)
    first = (lax.axis_index(("grp", "dev")) * part_stiff.shape[0]).reshape(1)
    inner, limit = element_call(
        first,
        part_stiff,
        displacement,
        mass,
        elem_nodes,
        elem_part.reshape(1, -1),
        elem_scale.reshape(1, -1),
    )
    own_force, far_force = contact_call(
        pair_a,
        pair_slot,
        own,
        arrived.reshape(-1, 4, own.shape[2]),
        pair_mask.reshape(-1, 128),
        limit,
        peers,
    )
    back = lax.all_to_all(far_force, ("grp", "dev"), split_axis=0, concat_axis=0, tiled=True)
    total, low_rows, up_rows, limits = seg_call(send, back, own_force, seg_node, inner, shared)
    from_lower = shifted(up_rows, "dev", 1)
    from_upper = shifted(low_rows, "dev", -1)
    return last_call(limits, total, shared, from_lower, from_upper, velocity, displacement, mass)


def solution(mesh):
    both = ("grp", "dev")
    return jax.shard_map(
        shards,
        mesh=mesh,
        in_specs=(
            P(None, both),
            P(None, both),
            P(None, both),
            P(both),
            P(None, both),
            P(both),
            P(both),
            P(both),
            P(None, both),
            P(both, None),
            P(both, None),
            P(both, None, None),
            P(both),
            P(both),
            P(both),
        ),
        out_specs=(P(None, both), P(None, both)),
        check_vma=False,
    )
```

```python
import math
from functools import partial

import jax
import jax.numpy as jnp
from jax import lax
from jax.experimental import pallas as pl
from jax.experimental.pallas import tpu as pltpu
from jax.sharding import PartitionSpec as P

SPRINGS = ((0, 1, 1.0), (1, 2, 1.0), (2, 3, 1.0), (3, 0, 1.0), (0, 2, 0.5), (1, 3, 0.5))
COURANT = 0.5
LOW = 256
PIECES = 3
WIDTH = 256
SCALE = math.sqrt(math.log2(math.e))
PARK = 1.0e3
f32 = jnp.float32
bf16 = jnp.bfloat16


def pieces_of(x, count=PIECES):
    out = []
    for _ in range(count):
        head = x.astype(bf16)
        out.append(head)
        x = x - head.astype(f32)
    return out


def low_hot(idx):
    low = jnp.broadcast_to((idx & (LOW - 1)).astype(f32), (16, idx.shape[1])).astype(bf16)
    line = lax.broadcasted_iota(jnp.int32, low.shape, 0).astype(f32).astype(bf16)
    one, zero = jnp.ones(low.shape, bf16), jnp.zeros(low.shape, bf16)
    return jnp.concatenate(
        [jnp.where(low == line + float(16 * k), one, zero) for k in range(LOW // 16)], 0
    )


def high_mask(idx, high):
    rows = lax.broadcasted_iota(jnp.int32, (high, idx.shape[1]), 0)
    return rows == (idx >> 8)


def fill_table(tab, at, ref, row, high):
    for h in range(high):
        tab[at + h : at + h + 1, :] = ref[row : row + 1, h * LOW : (h + 1) * LOW]


def split_table(cut, tab):
    rows = tab.shape[0]
    for p, piece in enumerate(pieces_of(tab[...])):
        cut[p * rows : (p + 1) * rows, :] = piece


def pick(cut, hot, mask, comps, high):
    found = jnp.dot(cut[...], hot, preferred_element_type=f32)
    rows = comps * high
    found = (found[:rows] + found[rows : 2 * rows]) + found[2 * rows :]
    return [
        jnp.sum(jnp.where(mask, found[c * high : (c + 1) * high], 0.0), 0, keepdims=True)
        for c in range(comps)
    ]


def cut_rows(force):
    return jnp.concatenate([piece.astype(f32) for piece in pieces_of(force)], 0)


def spread(ref, idx, high):
    mask = high_mask(idx, high)
    return jnp.concatenate(
        [jnp.where(mask, ref[r : r + 1, :], 0.0).astype(bf16) for r in range(3 * PIECES)], 0
    )


def add_hot(left, hot):
    return lax.dot_general(left, hot, (((1,), (1,)), ((), ())), preferred_element_type=f32)


def send_body(send_ref, disp_ref, ref_ref, seg_ref, mask_ref, own_ref, out_ref, tab, cut):
    high = disp_ref.shape[1] // LOW
    blocks = seg_ref.shape[0]
    for c in range(3):
        fill_table(tab, c * high, disp_ref, c, high)
    for c in range(3):
        for h in range(high):
            at = c * high + h
            tab[at : at + 1, :] += ref_ref[c : c + 1, h * LOW : (h + 1) * LOW]
    split_table(cut, tab)
    group = 8

    def some(g, carry):
        base = pl.multiple_of(g * group, group)
        seg = seg_ref[pl.ds(base, group), :]
        idx = jnp.concatenate([seg[k : k + 1] for k in range(group)], 1)
        xyz = pick(cut, low_hot(idx), high_mask(idx, high), 3, high)
        weight = mask_ref[pl.ds(base, group), :].astype(f32)
        for k in range(group):
            for c in range(3):
                own_ref[base + k, c : c + 1, :] = xyz[c][:, k * 128 : (k + 1) * 128]
            own_ref[base + k, 3:4, :] = weight[k : k + 1]
        return carry

    lax.fori_loop(0, blocks // group, some, 0, unroll=4)
    peers, cap = out_ref.shape[0], out_ref.shape[1]

    def send(d, carry):
        for c in range(cap):
            out_ref[d, c] = own_ref[send_ref[d * cap + c]]
        return carry

    lax.fori_loop(0, peers, send, 0, unroll=4)


def force_body(
    first_ref, stiff_ref, disp_ref, mass_ref, nodes_ref, part_ref, scale_ref, force_ref, lim_ref, tab, cut
):
    high = disp_ref.shape[1] // LOW
    width = WIDTH
    parts = stiff_ref.shape[0]
    for c in range(3):
        fill_table(tab, c * high, disp_ref, c, high)
    fill_table(tab, 3 * high, mass_ref, 0, high)
    split_table(cut, tab)

    def some(g, limit):
        at = pl.ds(pl.multiple_of(g * width, width), width)
        part = part_ref[:, at] - first_ref[0]
        stiff = jnp.zeros(part.shape, f32)
        for k in range(parts):
            stiff = jnp.where(part == k, stiff_ref[k], stiff)
        stiff = stiff * scale_ref[:, at]
        nodes = nodes_ref[:, at]
        idx = jnp.concatenate([nodes[k : k + 1] for k in range(4)], 1)
        found = pick(cut, low_hot(idx), high_mask(idx, high), 4, high)
        corner = [[found[c][:, k * width : (k + 1) * width] for c in range(4)] for k in range(4)]
        mass = jnp.minimum(
            jnp.minimum(corner[0][3], corner[1][3]), jnp.minimum(corner[2][3], corner[3][3])
        )
        force = [[jnp.zeros((1, width), f32)] * 3 for _ in range(4)]
        for head, tail, weight in SPRINGS:
            pull = weight * stiff
            for c in range(3):
                term = pull * (corner[tail][c] - corner[head][c])
                force[head][c] = force[head][c] + term
                force[tail][c] = force[tail][c] - term
        joined = [jnp.concatenate([force[k][c] for k in range(4)], 1) for c in range(3)]
        force_ref[g, 0:9] = cut_rows(jnp.concatenate(joined, 0))
        return jnp.minimum(limit, COURANT * jnp.sqrt(mass / stiff))

    limit = lax.fori_loop(
        0, nodes_ref.shape[1] // width, some, jnp.full((1, width), jnp.inf, f32), unroll=4
    )
    lim_ref[...] = jnp.broadcast_to(jnp.min(limit, 1, keepdims=True), lim_ref.shape)


def scatter_body(nodes_ref, force_ref, seg_ref, own_ref, tot_ref, acc, cut):
    high = tot_ref.shape[0] // 3
    acc[...] = jnp.zeros_like(acc)

    def some(g, carry):
        at = pl.ds(pl.multiple_of(g * WIDTH, WIDTH), WIDTH)
        nodes = nodes_ref[:, at]
        idx = jnp.concatenate([nodes[k : k + 1] for k in range(4)], 1)
        acc[...] += add_hot(spread(force_ref.at[g], idx, high), low_hot(idx))
        return carry

    lax.fori_loop(0, force_ref.shape[0], some, 0, unroll=4)
    group = 8

    def more(g, carry):
        base = pl.multiple_of(g * group, group)
        seg = seg_ref[pl.ds(base, group), :]
        idx = jnp.concatenate([seg[k : k + 1] for k in range(group)], 1)
        cut[0:9] = cut_rows(jnp.concatenate([own_ref[base + k] for k in range(group)], 1))
        acc[...] += add_hot(spread(cut, idx, high), low_hot(idx))
        return carry

    lax.fori_loop(0, seg_ref.shape[0] // group, more, 0, unroll=4)
    rows = 3 * high
    tot_ref[...] = (acc[2 * rows :] + acc[rows : 2 * rows]) + acc[:rows]


def contact_body(
    near_ref, far_ref, own_ref, recv_ref, live_ref, lim_ref, own_out, far_out, wide, total_a, total_b, remote, rows, chosen
):
    blocks = own_ref.shape[0]
    slots = recv_ref.shape[0]
    seg = own_ref.shape[2]
    cap = 5
    group = 8
    line = lax.broadcasted_iota(jnp.int32, (seg, 3 * seg), 0)
    part = lax.broadcasted_iota(jnp.int32, (seg, 3 * seg), 1) >> 7
    for k in range(group):
        at = line - 16 * k
        hit = (at == part) | (at == part + 3) | (at == part + 6)
        chosen[k] = jnp.where(hit, 1.0, 0.0).astype(bf16)
    rows[...] = jnp.zeros_like(rows)

    def scaled(block, parked):
        x = jnp.where(block[3:4] > 0.5, block[0:1] * SCALE, parked)
        return jnp.concatenate([x, block[1:3] * SCALE], 0)

    def widen(g, carry):
        for k in range(group):
            xyz = scaled(own_ref[g * group + k], PARK)
            for p, piece in enumerate(pieces_of(xyz)):
                rows[16 * k + 3 * p : 16 * k + 3 * p + 3, :] = piece.astype(f32)
        columns = rows[...].T.astype(bf16)
        for k in range(group):
            out = jnp.dot(columns, chosen[k], preferred_element_type=f32)
            for c in range(3):
                wide[g * group + k, c] = out[:, c * seg : (c + 1) * seg]
                total_a[g * group + k, c] = jnp.zeros((seg, seg), f32)
                total_b[g * group + k, c] = jnp.zeros((seg, seg), f32)
        return carry

    lax.fori_loop(0, blocks // group, widen, 0)
    def ready(s, carry):
        block = recv_ref[s]
        remote[s, 0:3] = scaled(block, -PARK)
        return carry

    lax.fori_loop(0, slots, ready, 0, unroll=8)
    far_out[...] = jnp.zeros_like(far_out)
    far_out[:, 15:16, :] = jnp.broadcast_to(lim_ref[...][None], (far_out.shape[0], 1, seg))
    live = jnp.sum(live_ref[...])

    def pair(p, total):
        b = near_ref[p]
        s = far_ref[p]
        there = [jnp.broadcast_to(remote[s, c : c + 1, :], (8, seg)) for c in range(3)]
        recoil = [None] * 3
        for v in range(seg // 8):
            at = pl.ds(v * 8, 8)
            gap = [wide[b, c, at, :] - there[c] for c in range(3)]
            far = gap[0] * gap[0] + gap[1] * gap[1] + gap[2] * gap[2]
            weight = jnp.exp2(-far)
            for c in range(3):
                push = weight * gap[c]
                total[b, c, at, :] += push
                recoil[c] = push if recoil[c] is None else recoil[c] + push
        d = (s * 52429) >> 18
        row = (s - d * cap) * 3
        for c in range(3):
            far_out[d, pl.ds(row + c, 1), :] -= jnp.sum(recoil[c], 0, keepdims=True) * (1.0 / SCALE)

    def both(q, carry):
        pair(2 * q, total_a)
        pair(2 * q + 1, total_b)
        return carry

    lax.fori_loop(0, live >> 1, both, 0)

    @pl.when((live & 1) == 1)
    def _():
        pair(live - 1, total_a)

    def close(b, carry):
        for c in range(3):
            total = total_a[b, c] + total_b[b, c]
            own_out[b, c : c + 1, :] = jnp.sum(total.T, 0, keepdims=True) * (1.0 / SCALE)
        return carry

    lax.fori_loop(0, blocks, close, 0)


def seg_body(
    send_ref, back_ref, seg_ref, int_ref, share_ref, tot_ref, low_ref, up_ref, lim_ref, sums, cut, acc, rows
):
    blocks = seg_ref.shape[0]
    peers = back_ref.shape[0]
    cap = 5
    high = int_ref.shape[0] // 3
    sums[...] = jnp.zeros_like(sums)

    def take(d, carry):
        for c in range(cap):
            b = send_ref[d * cap + c]
            sums[c, b, 0:3, :] += back_ref[d, 3 * c : 3 * c + 3, :]
        return carry

    lax.fori_loop(0, peers, take, 0)
    acc[...] = jnp.zeros_like(acc)
    group = 8

    def some(g, carry):
        base = pl.multiple_of(g * group, group)
        seg = seg_ref[pl.ds(base, group), :]
        idx = jnp.concatenate([seg[k : k + 1] for k in range(group)], 1)
        blocks_in = []
        for k in range(group):
            b = base + k
            part = sums[0, b, 0:3] + sums[1, b, 0:3] + sums[2, b, 0:3] + sums[3, b, 0:3] + sums[4, b, 0:3]
            blocks_in.append(part)
        rows[0:9] = cut_rows(jnp.concatenate(blocks_in, 1))
        acc[...] += add_hot(spread(rows, idx, high), low_hot(idx))
        return carry

    lax.fori_loop(0, blocks // group, some, 0, unroll=4)
    size = 3 * high
    tot_ref[...] = ((acc[2 * size :] + acc[size : 2 * size]) + acc[:size]) + int_ref[...]
    split_table(cut, tot_ref)
    count = share_ref.shape[1]
    for row, out in ((0, low_ref), (1, up_ref)):
        for at in range(0, count, 1024):
            idx = share_ref[row : row + 1, at : at + 1024]
            picked = pick(cut, low_hot(idx), high_mask(idx, high), 3, high)
            for c in range(3):
                out[c : c + 1, at : at + 1024] = picked[c]
    lim = jnp.min(back_ref[:, 15, :], 0, keepdims=True)
    lim_ref[...] = lim


def last_body(
    lim_ref, tot_ref, share_ref, low_ref, up_ref, vel_ref, disp_ref, mass_ref, new_disp, new_vel, acc, cut
):
    high = tot_ref.shape[0] // 3
    count = share_ref.shape[1]
    total = jnp.zeros(acc.shape, f32)
    for row, src in ((0, low_ref), (1, up_ref)):
        for at in range(0, count, 1024):
            idx = share_ref[row : row + 1, at : at + 1024]
            cut[0:9] = cut_rows(src[:, at : at + 1024])
            total = total + add_hot(spread(cut, idx, high), low_hot(idx))
    rows = 3 * high
    acc[0:rows] = ((total[2 * rows :] + total[rows : 2 * rows]) + total[:rows]) + tot_ref[...]
    step = jnp.min(lim_ref[...], 1, keepdims=True)
    for h in range(high):
        at = slice(h * LOW, (h + 1) * LOW)
        mass = mass_ref[0:1, at]
        for c in range(3):
            vel = vel_ref[c : c + 1, at] + step * (acc[c * high + h : c * high + h + 1, :] / mass)
            new_vel[c : c + 1, at] = vel
            new_disp[c : c + 1, at] = disp_ref[c : c + 1, at] + step * vel


def vmem(count):
    return [pl.BlockSpec(memory_space=pltpu.VMEM)] * count


def smem(count):
    return [pl.BlockSpec(memory_space=pltpu.SMEM)] * count


def struct(*shape):
    return jax.ShapeDtypeStruct(shape, f32)


def send_call(send, disp, ref_pos, seg_node, seg_mask, peers):
    high = disp.shape[1] // LOW
    blocks, seg = seg_node.shape
    return pl.pallas_call(
        send_body,
        out_shape=(struct(blocks, 4, seg), struct(peers, send.shape[0] // peers, 4, seg)),
        in_specs=smem(1) + vmem(4),
        out_specs=tuple(vmem(2)),
        scratch_shapes=[
            pltpu.VMEM((3 * high, LOW), f32),
            pltpu.VMEM((PIECES * 3 * high, LOW), bf16),
        ],
    )(send, disp, ref_pos, seg_node, seg_mask)


def force_call(first, stiff, disp, mass, nodes, part, scale):
    high = disp.shape[1] // LOW
    return pl.pallas_call(
        force_body,
        out_shape=(struct(nodes.shape[1] // WIDTH, 16, 4 * WIDTH), struct(1, 128)),
        in_specs=smem(2) + vmem(5),
        out_specs=tuple(vmem(2)),
        scratch_shapes=[
            pltpu.VMEM((4 * high, LOW), f32),
            pltpu.VMEM((PIECES * 4 * high, LOW), bf16),
        ],
    )(first, stiff, disp, mass, nodes, part, scale)


def scatter_call(nodes, force, seg_node, own):
    high = nodes.shape[1] // LOW
    return pl.pallas_call(
        scatter_body,
        out_shape=struct(3 * high, LOW),
        in_specs=vmem(4),
        out_specs=vmem(1)[0],
        scratch_shapes=[
            pltpu.VMEM((PIECES * 3 * high, LOW), f32),
            pltpu.VMEM((16, 1024), f32),
        ],
    )(nodes, force, seg_node, own)


def contact_call(pair_a, pair_slot, own, recv, live, lim, peers):
    blocks, _, seg = own.shape
    slots = recv.shape[0]
    return pl.pallas_call(
        contact_body,
        out_shape=(struct(blocks, 3, seg), struct(peers, 16, seg)),
        in_specs=smem(2) + vmem(4),
        out_specs=tuple(vmem(2)),
        scratch_shapes=[
            pltpu.VMEM((blocks, 3, seg, seg), f32),
            pltpu.VMEM((blocks, 3, seg, seg), f32),
            pltpu.VMEM((blocks, 3, seg, seg), f32),
            pltpu.VMEM((slots, 4, seg), f32),
            pltpu.VMEM((seg, seg), f32),
            pltpu.VMEM((8, seg, 3 * seg), bf16),
        ],
        compiler_params=pltpu.CompilerParams(vmem_limit_bytes=56 << 20),
    )(pair_a, pair_slot, own, recv, live, lim)


def seg_call(send, back, seg_node, inner, shared):
    high = inner.shape[0] // 3
    count = shared.shape[1]
    return pl.pallas_call(
        seg_body,
        out_shape=(struct(3 * high, LOW), struct(3, count), struct(3, count), struct(1, 128)),
        in_specs=smem(1) + vmem(4),
        out_specs=tuple(vmem(4)),
        scratch_shapes=[
            pltpu.VMEM((5, seg_node.shape[0], 4, 128), f32),
            pltpu.VMEM((PIECES * 3 * high, LOW), bf16),
            pltpu.VMEM((PIECES * 3 * high, LOW), f32),
            pltpu.VMEM((16, 1024), f32),
        ],
    )(send, back, seg_node, inner, shared)


def last_call(lim, total, shared, lower, upper, vel, disp, mass):
    high = total.shape[0] // 3
    return pl.pallas_call(
        last_body,
        out_shape=(struct(*disp.shape), struct(*disp.shape)),
        in_specs=vmem(8),
        out_specs=tuple(vmem(2)),
        scratch_shapes=[
            pltpu.VMEM((PIECES * 3 * high, LOW), f32),
            pltpu.VMEM((16, 1024), f32),
        ],
    )(lim, total, shared, lower, upper, vel, disp, mass)


def shifted(value, axis, steps):
    count = lax.axis_size(axis)
    first, last = (max(0, -steps), min(count, count - steps))
    return lax.ppermute(value, axis, [(source, source + steps) for source in range(first, last)])


def shards(
    ref_pos,
    displacement,
    velocity,
    node_mass,
    elem_nodes,
    elem_part,
    elem_scale,
    part_stiff,
    shared,
    seg_node,
    seg_mask,
    send_blk,
    pair_a,
    pair_slot,
    pair_mask,
):
    peers = lax.axis_size("grp") * lax.axis_size("dev")
    send = send_blk.reshape(-1)
    mass = node_mass.reshape(1, -1)
    own, outgoing = send_call(send, displacement, ref_pos, seg_node, seg_mask, peers)
    arrived = lax.all_to_all(outgoing, ("grp", "dev"), split_axis=0, concat_axis=0, tiled=True)
    first = (lax.axis_index(("grp", "dev")) * part_stiff.shape[0]).reshape(1)
    force, limit = force_call(
        first,
        part_stiff,
        displacement,
        mass,
        elem_nodes,
        elem_part.reshape(1, -1),
        elem_scale.reshape(1, -1),
    )
    own_force, far_force = contact_call(
        pair_a,
        pair_slot,
        own,
        arrived.reshape(-1, 4, own.shape[2]),
        pair_mask.reshape(-1, 128),
        limit,
        peers,
    )
    back = lax.all_to_all(far_force, ("grp", "dev"), split_axis=0, concat_axis=0, tiled=True)
    inner = scatter_call(elem_nodes, force, seg_node, own_force)
    total, low_rows, up_rows, limits = seg_call(send, back, seg_node, inner, shared)
    from_lower = shifted(up_rows, "dev", 1)
    from_upper = shifted(low_rows, "dev", -1)
    return last_call(limits, total, shared, from_lower, from_upper, velocity, displacement, mass)


def solution(mesh):
    both = ("grp", "dev")
    return jax.shard_map(
        shards,
        mesh=mesh,
        in_specs=(
            P(None, both),
            P(None, both),
            P(None, both),
            P(both),
            P(None, both),
            P(both),
            P(both),
            P(both),
            P(None, both),
            P(both, None),
            P(both, None),
            P(both, None, None),
            P(both),
            P(both),
            P(both),
        ),
        out_specs=(P(None, both), P(None, both)),
        check_vma=False,
    )
```

```python
import math
from functools import partial

import jax
import jax.numpy as jnp
from jax import lax
from jax.experimental import pallas as pl
from jax.experimental.pallas import tpu as pltpu
from jax.sharding import PartitionSpec as P

SPRINGS = ((0, 1, 1.0), (1, 2, 1.0), (2, 3, 1.0), (3, 0, 1.0), (0, 2, 0.5), (1, 3, 0.5))
COURANT = 0.5
LOW = 256
PIECES = 3
WIDTH = 256
SCALE = math.sqrt(math.log2(math.e))
PARK = 1.0e3
f32 = jnp.float32
bf16 = jnp.bfloat16


def pieces_of(x, count=PIECES):
    out = []
    for _ in range(count):
        head = x.astype(bf16)
        out.append(head)
        x = x - head.astype(f32)
    return out


def low_hot(idx):
    low = jnp.broadcast_to((idx & (LOW - 1)).astype(f32), (16, idx.shape[1])).astype(bf16)
    line = lax.broadcasted_iota(jnp.int32, low.shape, 0).astype(f32).astype(bf16)
    one, zero = jnp.ones(low.shape, bf16), jnp.zeros(low.shape, bf16)
    return jnp.concatenate(
        [jnp.where(low == line + float(16 * k), one, zero) for k in range(LOW // 16)], 0
    )


def high_mask(idx, high):
    rows = lax.broadcasted_iota(jnp.int32, (high, idx.shape[1]), 0)
    return rows == (idx >> 8)


def fill_table(tab, at, ref, row, high):
    for h in range(high):
        tab[at + h : at + h + 1, :] = ref[row : row + 1, h * LOW : (h + 1) * LOW]


def split_table(cut, tab):
    rows = tab.shape[0]
    for p, piece in enumerate(pieces_of(tab[...])):
        cut[p * rows : (p + 1) * rows, :] = piece


def pick(cut, hot, mask, comps, high):
    found = jnp.dot(cut[...], hot, preferred_element_type=f32)
    rows = comps * high
    found = (found[:rows] + found[rows : 2 * rows]) + found[2 * rows :]
    return [
        jnp.sum(jnp.where(mask, found[c * high : (c + 1) * high], 0.0), 0, keepdims=True)
        for c in range(comps)
    ]


def cut_rows(force):
    return jnp.concatenate([piece.astype(f32) for piece in pieces_of(force)], 0)


def spread(ref, idx, high):
    mask = high_mask(idx, high)
    return jnp.concatenate(
        [jnp.where(mask, ref[r : r + 1, :], 0.0).astype(bf16) for r in range(3 * PIECES)], 0
    )


def add_hot(left, hot):
    return lax.dot_general(left, hot, (((1,), (1,)), ((), ())), preferred_element_type=f32)


def send_body(send_ref, disp_ref, ref_ref, seg_ref, mask_ref, own_ref, out_ref, tab, cut):
    high = disp_ref.shape[1] // LOW
    blocks = seg_ref.shape[0]
    for c in range(3):
        fill_table(tab, c * high, disp_ref, c, high)
    for c in range(3):
        for h in range(high):
            at = c * high + h
            tab[at : at + 1, :] += ref_ref[c : c + 1, h * LOW : (h + 1) * LOW]
    split_table(cut, tab)
    group = 8

    def some(g, carry):
        base = pl.multiple_of(g * group, group)
        seg = seg_ref[pl.ds(base, group), :]
        idx = jnp.concatenate([seg[k : k + 1] for k in range(group)], 1)
        xyz = pick(cut, low_hot(idx), high_mask(idx, high), 3, high)
        weight = mask_ref[pl.ds(base, group), :].astype(f32)
        for k in range(group):
            for c in range(3):
                own_ref[base + k, c : c + 1, :] = xyz[c][:, k * 128 : (k + 1) * 128]
            own_ref[base + k, 3:4, :] = weight[k : k + 1]
        return carry

    lax.fori_loop(0, blocks // group, some, 0, unroll=4)
    peers, cap = out_ref.shape[0], out_ref.shape[1]

    def send(d, carry):
        for c in range(cap):
            out_ref[d, c] = own_ref[send_ref[d * cap + c]]
        return carry

    lax.fori_loop(0, peers, send, 0, unroll=4)


def force_body(
    first_ref, stiff_ref, disp_ref, mass_ref, nodes_ref, part_ref, scale_ref, force_ref, lim_ref, tab, cut
):
    high = disp_ref.shape[1] // LOW
    width = WIDTH
    parts = stiff_ref.shape[0]
    for c in range(3):
        fill_table(tab, c * high, disp_ref, c, high)
    fill_table(tab, 3 * high, mass_ref, 0, high)
    split_table(cut, tab)

    def some(g, limit):
        at = pl.ds(pl.multiple_of(g * width, width), width)
        part = part_ref[:, at] - first_ref[0]
        stiff = jnp.zeros(part.shape, f32)
        for k in range(parts):
            stiff = jnp.where(part == k, stiff_ref[k], stiff)
        stiff = stiff * scale_ref[:, at]
        nodes = nodes_ref[:, at]
        idx = jnp.concatenate([nodes[k : k + 1] for k in range(4)], 1)
        found = pick(cut, low_hot(idx), high_mask(idx, high), 4, high)
        corner = [[found[c][:, k * width : (k + 1) * width] for c in range(4)] for k in range(4)]
        mass = jnp.minimum(
            jnp.minimum(corner[0][3], corner[1][3]), jnp.minimum(corner[2][3], corner[3][3])
        )
        force = [[jnp.zeros((1, width), f32)] * 3 for _ in range(4)]
        for head, tail, weight in SPRINGS:
            pull = weight * stiff
            for c in range(3):
                term = pull * (corner[tail][c] - corner[head][c])
                force[head][c] = force[head][c] + term
                force[tail][c] = force[tail][c] - term
        joined = [jnp.concatenate([force[k][c] for k in range(4)], 1) for c in range(3)]
        force_ref[g, 0:9] = cut_rows(jnp.concatenate(joined, 0))
        return jnp.minimum(limit, COURANT * jnp.sqrt(mass / stiff))

    limit = lax.fori_loop(
        0, nodes_ref.shape[1] // width, some, jnp.full((1, width), jnp.inf, f32), unroll=4
    )
    lim_ref[...] = jnp.broadcast_to(jnp.min(limit, 1, keepdims=True), lim_ref.shape)


def scatter_body(nodes_ref, force_ref, seg_ref, own_ref, tot_ref, acc, cut):
    high = tot_ref.shape[0] // 3
    acc[...] = jnp.zeros_like(acc)

    def some(g, carry):
        at = pl.ds(pl.multiple_of(g * WIDTH, WIDTH), WIDTH)
        nodes = nodes_ref[:, at]
        idx = jnp.concatenate([nodes[k : k + 1] for k in range(4)], 1)
        acc[...] += add_hot(spread(force_ref.at[g], idx, high), low_hot(idx))
        return carry

    lax.fori_loop(0, force_ref.shape[0], some, 0, unroll=4)
    group = 8

    def more(g, carry):
        base = pl.multiple_of(g * group, group)
        seg = seg_ref[pl.ds(base, group), :]
        idx = jnp.concatenate([seg[k : k + 1] for k in range(group)], 1)
        cut[0:9] = cut_rows(jnp.concatenate([own_ref[base + k] for k in range(group)], 1))
        acc[...] += add_hot(spread(cut, idx, high), low_hot(idx))
        return carry

    lax.fori_loop(0, seg_ref.shape[0] // group, more, 0, unroll=4)
    rows = 3 * high
    tot_ref[...] = (acc[2 * rows :] + acc[rows : 2 * rows]) + acc[:rows]


def contact_body(
    near_ref, far_ref, own_ref, recv_ref, live_ref, lim_ref, own_out, far_out, wide, total_a, total_b, remote, rows, chosen, recoils
):
    blocks = own_ref.shape[0]
    slots = recv_ref.shape[0]
    seg = own_ref.shape[2]
    cap = 5
    group = 8
    line = lax.broadcasted_iota(jnp.int32, (seg, 3 * seg), 0)
    part = lax.broadcasted_iota(jnp.int32, (seg, 3 * seg), 1) >> 7
    for k in range(group):
        at = line - 16 * k
        hit = (at == part) | (at == part + 3) | (at == part + 6)
        chosen[k] = jnp.where(hit, 1.0, 0.0).astype(bf16)
    rows[...] = jnp.zeros_like(rows)

    def scaled(block, parked):
        x = jnp.where(block[3:4] > 0.5, block[0:1] * SCALE, parked)
        return jnp.concatenate([x, block[1:3] * SCALE], 0)

    def widen(g, carry):
        for k in range(group):
            xyz = scaled(own_ref[g * group + k], PARK)
            for p, piece in enumerate(pieces_of(xyz)):
                rows[16 * k + 3 * p : 16 * k + 3 * p + 3, :] = piece.astype(f32)
        columns = rows[...].T.astype(bf16)
        for k in range(group):
            out = jnp.dot(columns, chosen[k], preferred_element_type=f32)
            for c in range(3):
                wide[g * group + k, c] = out[:, c * seg : (c + 1) * seg]
                total_a[g * group + k, c] = jnp.zeros((seg, seg), f32)
                total_b[g * group + k, c] = jnp.zeros((seg, seg), f32)
        return carry

    lax.fori_loop(0, blocks // group, widen, 0, unroll=4)
    def ready(s, carry):
        block = recv_ref[s]
        remote[s, 0:3] = scaled(block, -PARK)
        return carry

    lax.fori_loop(0, slots, ready, 0, unroll=8)
    recoils[...] = jnp.zeros_like(recoils)
    live = jnp.sum(live_ref[...])

    def pair(p, total):
        b = near_ref[p]
        s = far_ref[p]
        there = [jnp.broadcast_to(remote[s, c : c + 1, :], (8, seg)) for c in range(3)]
        recoil = [None] * 3
        for v in range(seg // 8):
            at = pl.ds(v * 8, 8)
            gap = [wide[b, c, at, :] - there[c] for c in range(3)]
            far = gap[0] * gap[0] + gap[1] * gap[1] + gap[2] * gap[2]
            weight = jnp.exp2(-far)
            for c in range(3):
                push = weight * gap[c]
                total[b, c, at, :] += push
                recoil[c] = push if recoil[c] is None else recoil[c] + push
        for c in range(3):
            recoils[c, pl.ds(pl.multiple_of(s * 8, 8), 8), :] += recoil[c]

    def both(q, carry):
        pair(2 * q, total_a)
        pair(2 * q + 1, total_b)
        return carry

    lax.fori_loop(0, live >> 1, both, 0)

    @pl.when((live & 1) == 1)
    def _():
        pair(live - 1, total_a)

    def close(b, carry):
        for c in range(3):
            total = total_a[b, c] + total_b[b, c]
            own_out[b, c : c + 1, :] = jnp.sum(total.T, 0, keepdims=True) * (1.0 / SCALE)
        return carry

    lax.fori_loop(0, blocks, close, 0, unroll=8)
    peers = slots // cap
    stamp = jnp.broadcast_to(lim_ref[...], (8, seg))

    def finish(g, carry):
        for k in range(cap):
            for c in range(3):
                at = g * (64 * cap) + k * 8
                rows = [recoils[c, pl.ds(at + r, 8, stride=8 * cap), :] for r in range(8)]
                while len(rows) > 1:
                    rows = [x + y for x, y in zip(rows[::2], rows[1::2])]
                far_out[pl.ds(g * 128 + 3 * k + c, 8, stride=16), :] = rows[0] * (-1.0 / SCALE)
        far_out[pl.ds(g * 128 + 15, 8, stride=16), :] = stamp
        return carry

    lax.fori_loop(0, peers // 8, finish, 0, unroll=4)


def seg_body(
    send_ref, back_ref, seg_ref, int_ref, share_ref, tot_ref, low_ref, up_ref, lim_ref, sums, cut, acc, rows
):
    blocks = seg_ref.shape[0]
    peers = back_ref.shape[0]
    cap = 5
    high = int_ref.shape[0] // 3
    sums[...] = jnp.zeros_like(sums)

    def take(d, carry):
        for c in range(cap):
            b = send_ref[d * cap + c]
            sums[c, b, 0:3, :] += back_ref[d, 3 * c : 3 * c + 3, :]
        return carry

    lax.fori_loop(0, peers, take, 0)
    acc[...] = jnp.zeros_like(acc)
    group = 8

    def some(g, carry):
        base = pl.multiple_of(g * group, group)
        seg = seg_ref[pl.ds(base, group), :]
        idx = jnp.concatenate([seg[k : k + 1] for k in range(group)], 1)
        blocks_in = []
        for k in range(group):
            b = base + k
            part = sums[0, b, 0:3] + sums[1, b, 0:3] + sums[2, b, 0:3] + sums[3, b, 0:3] + sums[4, b, 0:3]
            blocks_in.append(part)
        rows[0:9] = cut_rows(jnp.concatenate(blocks_in, 1))
        acc[...] += add_hot(spread(rows, idx, high), low_hot(idx))
        return carry

    lax.fori_loop(0, blocks // group, some, 0, unroll=4)
    size = 3 * high
    tot_ref[...] = ((acc[2 * size :] + acc[size : 2 * size]) + acc[:size]) + int_ref[...]
    split_table(cut, tot_ref)
    count = share_ref.shape[1]
    for row, out in ((0, low_ref), (1, up_ref)):
        for at in range(0, count, 1024):
            idx = share_ref[row : row + 1, at : at + 1024]
            picked = pick(cut, low_hot(idx), high_mask(idx, high), 3, high)
            for c in range(3):
                out[c : c + 1, at : at + 1024] = picked[c]
    lim = jnp.min(back_ref[:, 15, :], 0, keepdims=True)
    lim_ref[...] = lim


def last_body(
    lim_ref, tot_ref, share_ref, low_ref, up_ref, vel_ref, disp_ref, mass_ref, new_disp, new_vel, acc, cut
):
    high = tot_ref.shape[0] // 3
    count = share_ref.shape[1]
    total = jnp.zeros(acc.shape, f32)
    for row, src in ((0, low_ref), (1, up_ref)):
        for at in range(0, count, 1024):
            idx = share_ref[row : row + 1, at : at + 1024]
            cut[0:9] = cut_rows(src[:, at : at + 1024])
            total = total + add_hot(spread(cut, idx, high), low_hot(idx))
    rows = 3 * high
    acc[0:rows] = ((total[2 * rows :] + total[rows : 2 * rows]) + total[:rows]) + tot_ref[...]
    step = jnp.min(lim_ref[...], 1, keepdims=True)
    for h in range(high):
        at = slice(h * LOW, (h + 1) * LOW)
        mass = mass_ref[0:1, at]
        for c in range(3):
            vel = vel_ref[c : c + 1, at] + step * (acc[c * high + h : c * high + h + 1, :] / mass)
            new_vel[c : c + 1, at] = vel
            new_disp[c : c + 1, at] = disp_ref[c : c + 1, at] + step * vel


def vmem(count):
    return [pl.BlockSpec(memory_space=pltpu.VMEM)] * count


def smem(count):
    return [pl.BlockSpec(memory_space=pltpu.SMEM)] * count


def struct(*shape):
    return jax.ShapeDtypeStruct(shape, f32)


def send_call(send, disp, ref_pos, seg_node, seg_mask, peers):
    high = disp.shape[1] // LOW
    blocks, seg = seg_node.shape
    return pl.pallas_call(
        send_body,
        out_shape=(struct(blocks, 4, seg), struct(peers, send.shape[0] // peers, 4, seg)),
        in_specs=smem(1) + vmem(4),
        out_specs=tuple(vmem(2)),
        scratch_shapes=[
            pltpu.VMEM((3 * high, LOW), f32),
            pltpu.VMEM((PIECES * 3 * high, LOW), bf16),
        ],
    )(send, disp, ref_pos, seg_node, seg_mask)


def force_call(first, stiff, disp, mass, nodes, part, scale):
    high = disp.shape[1] // LOW
    return pl.pallas_call(
        force_body,
        out_shape=(struct(nodes.shape[1] // WIDTH, 16, 4 * WIDTH), struct(1, 128)),
        in_specs=smem(2) + vmem(5),
        out_specs=tuple(vmem(2)),
        scratch_shapes=[
            pltpu.VMEM((4 * high, LOW), f32),
            pltpu.VMEM((PIECES * 4 * high, LOW), bf16),
        ],
    )(first, stiff, disp, mass, nodes, part, scale)


def scatter_call(nodes, force, seg_node, own):
    high = nodes.shape[1] // LOW
    return pl.pallas_call(
        scatter_body,
        out_shape=struct(3 * high, LOW),
        in_specs=vmem(4),
        out_specs=vmem(1)[0],
        scratch_shapes=[
            pltpu.VMEM((PIECES * 3 * high, LOW), f32),
            pltpu.VMEM((16, 1024), f32),
        ],
    )(nodes, force, seg_node, own)


def contact_call(pair_a, pair_slot, own, recv, live, lim, peers):
    blocks, _, seg = own.shape
    slots = recv.shape[0]
    return pl.pallas_call(
        contact_body,
        out_shape=(struct(blocks, 3, seg), struct(peers * 16, seg)),
        in_specs=smem(2) + vmem(4),
        out_specs=tuple(vmem(2)),
        scratch_shapes=[
            pltpu.VMEM((blocks, 3, seg, seg), f32),
            pltpu.VMEM((blocks, 3, seg, seg), f32),
            pltpu.VMEM((blocks, 3, seg, seg), f32),
            pltpu.VMEM((slots, 4, seg), f32),
            pltpu.VMEM((seg, seg), f32),
            pltpu.VMEM((8, seg, 3 * seg), bf16),
            pltpu.VMEM((3, slots * 8, seg), f32),
        ],
        compiler_params=pltpu.CompilerParams(vmem_limit_bytes=56 << 20),
    )(pair_a, pair_slot, own, recv, live, lim)


def seg_call(send, back, seg_node, inner, shared):
    high = inner.shape[0] // 3
    count = shared.shape[1]
    return pl.pallas_call(
        seg_body,
        out_shape=(struct(3 * high, LOW), struct(3, count), struct(3, count), struct(1, 128)),
        in_specs=smem(1) + vmem(4),
        out_specs=tuple(vmem(4)),
        scratch_shapes=[
            pltpu.VMEM((5, seg_node.shape[0], 4, 128), f32),
            pltpu.VMEM((PIECES * 3 * high, LOW), bf16),
            pltpu.VMEM((PIECES * 3 * high, LOW), f32),
            pltpu.VMEM((16, 1024), f32),
        ],
    )(send, back, seg_node, inner, shared)


def last_call(lim, total, shared, lower, upper, vel, disp, mass):
    high = total.shape[0] // 3
    return pl.pallas_call(
        last_body,
        out_shape=(struct(*disp.shape), struct(*disp.shape)),
        in_specs=vmem(8),
        out_specs=tuple(vmem(2)),
        scratch_shapes=[
            pltpu.VMEM((PIECES * 3 * high, LOW), f32),
            pltpu.VMEM((16, 1024), f32),
        ],
    )(lim, total, shared, lower, upper, vel, disp, mass)


def shifted(value, axis, steps):
    count = lax.axis_size(axis)
    first, last = (max(0, -steps), min(count, count - steps))
    return lax.ppermute(value, axis, [(source, source + steps) for source in range(first, last)])


def shards(
    ref_pos,
    displacement,
    velocity,
    node_mass,
    elem_nodes,
    elem_part,
    elem_scale,
    part_stiff,
    shared,
    seg_node,
    seg_mask,
    send_blk,
    pair_a,
    pair_slot,
    pair_mask,
):
    peers = lax.axis_size("grp") * lax.axis_size("dev")
    send = send_blk.reshape(-1)
    mass = node_mass.reshape(1, -1)
    own, outgoing = send_call(send, displacement, ref_pos, seg_node, seg_mask, peers)
    arrived = lax.all_to_all(outgoing, ("grp", "dev"), split_axis=0, concat_axis=0, tiled=True)
    first = (lax.axis_index(("grp", "dev")) * part_stiff.shape[0]).reshape(1)
    force, limit = force_call(
        first,
        part_stiff,
        displacement,
        mass,
        elem_nodes,
        elem_part.reshape(1, -1),
        elem_scale.reshape(1, -1),
    )
    own_force, far_force = contact_call(
        pair_a,
        pair_slot,
        own,
        arrived.reshape(-1, 4, own.shape[2]),
        pair_mask.reshape(-1, 128),
        limit,
        peers,
    )
    back = lax.all_to_all(
        far_force.reshape(peers, 16, -1), ("grp", "dev"), split_axis=0, concat_axis=0, tiled=True
    )
    inner = scatter_call(elem_nodes, force, seg_node, own_force)
    total, low_rows, up_rows, limits = seg_call(send, back, seg_node, inner, shared)
    from_lower = shifted(up_rows, "dev", 1)
    from_upper = shifted(low_rows, "dev", -1)
    return last_call(limits, total, shared, from_lower, from_upper, velocity, displacement, mass)


def solution(mesh):
    both = ("grp", "dev")
    return jax.shard_map(
        shards,
        mesh=mesh,
        in_specs=(
            P(None, both),
            P(None, both),
            P(None, both),
            P(both),
            P(None, both),
            P(both),
            P(both),
            P(both),
            P(None, both),
            P(both, None),
            P(both, None),
            P(both, None, None),
            P(both),
            P(both),
            P(both),
        ),
        out_specs=(P(None, both), P(None, both)),
        check_vma=False,
    )
```

```python
import math
from functools import partial

import jax
import jax.numpy as jnp
from jax import lax
from jax.experimental import pallas as pl
from jax.experimental.pallas import tpu as pltpu
from jax.sharding import PartitionSpec as P

SPRINGS = ((0, 1, 1.0), (1, 2, 1.0), (2, 3, 1.0), (3, 0, 1.0), (0, 2, 0.5), (1, 3, 0.5))
COURANT = 0.5
LOW = 256
PIECES = 3
WIDTH = 256
SCALE = math.sqrt(math.log2(math.e))
PARK = 1.0e3
f32 = jnp.float32
bf16 = jnp.bfloat16


def pieces_of(x, count=PIECES):
    out = []
    for _ in range(count):
        head = x.astype(bf16)
        out.append(head)
        x = x - head.astype(f32)
    return out


def low_hot(idx):
    low = jnp.broadcast_to((idx & (LOW - 1)).astype(f32), (16, idx.shape[1])).astype(bf16)
    line = lax.broadcasted_iota(jnp.int32, low.shape, 0).astype(f32).astype(bf16)
    one, zero = jnp.ones(low.shape, bf16), jnp.zeros(low.shape, bf16)
    return jnp.concatenate(
        [jnp.where(low == line + float(16 * k), one, zero) for k in range(LOW // 16)], 0
    )


def high_mask(idx, high):
    rows = lax.broadcasted_iota(jnp.int32, (high, idx.shape[1]), 0)
    return rows == (idx >> 8)


def fill_table(tab, at, ref, row, high):
    for h in range(high):
        tab[at + h : at + h + 1, :] = ref[row : row + 1, h * LOW : (h + 1) * LOW]


def split_table(cut, tab):
    rows = tab.shape[0]
    for p, piece in enumerate(pieces_of(tab[...])):
        cut[p * rows : (p + 1) * rows, :] = piece


def pick(cut, hot, mask, comps, high):
    found = jnp.dot(cut[...], hot, preferred_element_type=f32)
    rows = comps * high
    found = (found[:rows] + found[rows : 2 * rows]) + found[2 * rows :]
    return [
        jnp.sum(jnp.where(mask, found[c * high : (c + 1) * high], 0.0), 0, keepdims=True)
        for c in range(comps)
    ]


def cut_rows(force):
    return jnp.concatenate([piece.astype(f32) for piece in pieces_of(force)], 0)


def spread(ref, idx, high):
    mask = high_mask(idx, high)
    return jnp.concatenate(
        [jnp.where(mask, ref[r : r + 1, :], 0.0).astype(bf16) for r in range(3 * PIECES)], 0
    )


def add_hot(left, hot):
    return lax.dot_general(left, hot, (((1,), (1,)), ((), ())), preferred_element_type=f32)


def send_body(send_ref, disp_ref, ref_ref, seg_ref, mask_ref, own_ref, out_ref, tab, cut):
    high = disp_ref.shape[1] // LOW
    blocks = seg_ref.shape[0]
    for c in range(3):
        fill_table(tab, c * high, disp_ref, c, high)
    for c in range(3):
        for h in range(high):
            at = c * high + h
            tab[at : at + 1, :] += ref_ref[c : c + 1, h * LOW : (h + 1) * LOW]
    split_table(cut, tab)
    group = 8

    def some(g, carry):
        base = pl.multiple_of(g * group, group)
        seg = seg_ref[pl.ds(base, group), :]
        idx = jnp.concatenate([seg[k : k + 1] for k in range(group)], 1)
        xyz = pick(cut, low_hot(idx), high_mask(idx, high), 3, high)
        weight = mask_ref[pl.ds(base, group), :].astype(f32)
        for k in range(group):
            for c in range(3):
                own_ref[base + k, c : c + 1, :] = xyz[c][:, k * 128 : (k + 1) * 128]
            own_ref[base + k, 3:4, :] = weight[k : k + 1]
        return carry

    lax.fori_loop(0, blocks // group, some, 0, unroll=4)
    peers, cap = out_ref.shape[0], out_ref.shape[1]

    def send(d, carry):
        for c in range(cap):
            out_ref[d, c] = own_ref[send_ref[c * peers + d]]
        return carry

    lax.fori_loop(0, peers, send, 0, unroll=4)


def force_body(
    first_ref, stiff_ref, disp_ref, mass_ref, nodes_ref, part_ref, scale_ref, force_ref, lim_ref, tab, cut
):
    high = disp_ref.shape[1] // LOW
    width = WIDTH
    parts = stiff_ref.shape[0]
    for c in range(3):
        fill_table(tab, c * high, disp_ref, c, high)
    fill_table(tab, 3 * high, mass_ref, 0, high)
    split_table(cut, tab)

    def some(g, limit):
        at = pl.ds(pl.multiple_of(g * width, width), width)
        part = part_ref[:, at] - first_ref[0]
        stiff = jnp.zeros(part.shape, f32)
        for k in range(parts):
            stiff = jnp.where(part == k, stiff_ref[k], stiff)
        stiff = stiff * scale_ref[:, at]
        nodes = nodes_ref[:, at]
        idx = jnp.concatenate([nodes[k : k + 1] for k in range(4)], 1)
        found = pick(cut, low_hot(idx), high_mask(idx, high), 4, high)
        corner = [[found[c][:, k * width : (k + 1) * width] for c in range(4)] for k in range(4)]
        mass = jnp.minimum(
            jnp.minimum(corner[0][3], corner[1][3]), jnp.minimum(corner[2][3], corner[3][3])
        )
        force = [[jnp.zeros((1, width), f32)] * 3 for _ in range(4)]
        for head, tail, weight in SPRINGS:
            pull = weight * stiff
            for c in range(3):
                term = pull * (corner[tail][c] - corner[head][c])
                force[head][c] = force[head][c] + term
                force[tail][c] = force[tail][c] - term
        joined = [jnp.concatenate([force[k][c] for k in range(4)], 1) for c in range(3)]
        force_ref[g, 0:9] = cut_rows(jnp.concatenate(joined, 0))
        return jnp.minimum(limit, COURANT * jnp.sqrt(mass / stiff))

    limit = lax.fori_loop(
        0, nodes_ref.shape[1] // width, some, jnp.full((1, width), jnp.inf, f32), unroll=4
    )
    lim_ref[...] = jnp.broadcast_to(jnp.min(limit, 1, keepdims=True), lim_ref.shape)


def scatter_body(nodes_ref, force_ref, seg_ref, own_ref, tot_ref, acc, cut):
    high = tot_ref.shape[0] // 3
    acc[...] = jnp.zeros_like(acc)

    def some(g, carry):
        at = pl.ds(pl.multiple_of(g * WIDTH, WIDTH), WIDTH)
        nodes = nodes_ref[:, at]
        idx = jnp.concatenate([nodes[k : k + 1] for k in range(4)], 1)
        acc[...] += add_hot(spread(force_ref.at[g], idx, high), low_hot(idx))
        return carry

    lax.fori_loop(0, force_ref.shape[0], some, 0, unroll=4)
    group = 8

    def more(g, carry):
        base = pl.multiple_of(g * group, group)
        seg = seg_ref[pl.ds(base, group), :]
        idx = jnp.concatenate([seg[k : k + 1] for k in range(group)], 1)
        cut[0:9] = cut_rows(jnp.concatenate([own_ref[base + k] for k in range(group)], 1))
        acc[...] += add_hot(spread(cut, idx, high), low_hot(idx))
        return carry

    lax.fori_loop(0, seg_ref.shape[0] // group, more, 0, unroll=4)
    rows = 3 * high
    tot_ref[...] = (acc[2 * rows :] + acc[rows : 2 * rows]) + acc[:rows]


def contact_body(
    near_ref, far_ref, own_ref, recv_ref, live_ref, lim_ref, own_out, far_out, wide, total_a, total_b, remote, rows, chosen, recoils
):
    blocks = own_ref.shape[0]
    slots = recv_ref.shape[0]
    seg = own_ref.shape[2]
    cap = 5
    group = 8
    line = lax.broadcasted_iota(jnp.int32, (seg, 3 * seg), 0)
    part = lax.broadcasted_iota(jnp.int32, (seg, 3 * seg), 1) >> 7
    for k in range(group):
        at = line - 16 * k
        hit = (at == part) | (at == part + 3) | (at == part + 6)
        chosen[k] = jnp.where(hit, 1.0, 0.0).astype(bf16)
    rows[...] = jnp.zeros_like(rows)

    def scaled(block, parked):
        x = jnp.where(block[3:4] > 0.5, block[0:1] * SCALE, parked)
        return jnp.concatenate([x, block[1:3] * SCALE], 0)

    def widen(g, carry):
        for k in range(group):
            xyz = scaled(own_ref[g * group + k], PARK)
            for p, piece in enumerate(pieces_of(xyz)):
                rows[16 * k + 3 * p : 16 * k + 3 * p + 3, :] = piece.astype(f32)
        columns = rows[...].T.astype(bf16)
        for k in range(group):
            out = jnp.dot(columns, chosen[k], preferred_element_type=f32)
            for c in range(3):
                wide[g * group + k, c] = out[:, c * seg : (c + 1) * seg]
                total_a[g * group + k, c] = jnp.zeros((seg, seg), f32)
                total_b[g * group + k, c] = jnp.zeros((seg, seg), f32)
        return carry

    lax.fori_loop(0, blocks // group, widen, 0, unroll=4)
    def ready(s, carry):
        block = recv_ref[s]
        remote[s, 0:3] = scaled(block, -PARK)
        return carry

    lax.fori_loop(0, slots, ready, 0, unroll=8)
    recoils[...] = jnp.zeros_like(recoils)
    live = jnp.sum(live_ref[...])

    def pair(p, total):
        b = near_ref[p]
        s = far_ref[p]
        there = [jnp.broadcast_to(remote[s, c : c + 1, :], (8, seg)) for c in range(3)]
        recoil = [None] * 3
        for v in range(seg // 8):
            at = pl.ds(v * 8, 8)
            gap = [wide[b, c, at, :] - there[c] for c in range(3)]
            far = gap[0] * gap[0] + gap[1] * gap[1] + gap[2] * gap[2]
            weight = jnp.exp2(-far)
            for c in range(3):
                push = weight * gap[c]
                total[b, c, at, :] += push
                recoil[c] = push if recoil[c] is None else recoil[c] + push
        for c in range(3):
            recoils[c, pl.ds(pl.multiple_of(s * 8, 8), 8), :] += recoil[c]

    def four(q, carry):
        pair(4 * q, total_a)
        pair(4 * q + 1, total_b)
        pair(4 * q + 2, total_a)
        pair(4 * q + 3, total_b)
        return carry

    def one(p, carry):
        pair(p, total_a)
        return carry

    whole = live >> 2
    lax.fori_loop(0, whole, four, 0)
    lax.fori_loop(4 * whole, live, one, 0)

    def close(b, carry):
        for c in range(3):
            total = total_a[b, c] + total_b[b, c]
            own_out[b, c : c + 1, :] = jnp.sum(total.T, 0, keepdims=True) * (1.0 / SCALE)
        return carry

    lax.fori_loop(0, blocks, close, 0, unroll=8)
    peers = slots // cap
    stamp = jnp.broadcast_to(lim_ref[...], (8, seg))

    def finish(g, carry):
        for k in range(cap):
            for c in range(3):
                at = g * (64 * cap) + k * 8
                rows = [recoils[c, pl.ds(at + r, 8, stride=8 * cap), :] for r in range(8)]
                while len(rows) > 1:
                    rows = [x + y for x, y in zip(rows[::2], rows[1::2])]
                far_out[pl.ds(g * 128 + 3 * k + c, 8, stride=16), :] = rows[0] * (-1.0 / SCALE)
        far_out[pl.ds(g * 128 + 15, 8, stride=16), :] = stamp
        return carry

    lax.fori_loop(0, peers // 8, finish, 0, unroll=4)


def seg_body(
    send_ref, back_ref, seg_ref, int_ref, share_ref, tot_ref, low_ref, up_ref, lim_ref, sums, cut, acc, rows
):
    blocks = seg_ref.shape[0]
    peers = back_ref.shape[0] // 16
    cap = 5
    high = int_ref.shape[0] // 3
    line = lax.broadcasted_iota(jnp.int32, (blocks, peers), 0)
    sums[...] = jnp.zeros_like(sums)
    for c in range(cap):
        hot = jnp.where(line == send_ref[c : c + 1, :], 1.0, 0.0).astype(bf16)
        for k in range(3):
            force = back_ref[pl.ds(3 * c + k, peers, stride=16), :]
            found = jnp.dot(hot, jnp.concatenate(pieces_of(force), 1), preferred_element_type=f32)
            sums[k] += (found[:, 256:] + found[:, 128:256]) + found[:, :128]
    acc[...] = jnp.zeros_like(acc)
    group = 8

    def some(g, carry):
        base = pl.multiple_of(g * group, group)
        seg = seg_ref[pl.ds(base, group), :]
        idx = jnp.concatenate([seg[k : k + 1] for k in range(group)], 1)
        force = [sums[c, pl.ds(base, group), :] for c in range(3)]
        force = [jnp.concatenate([f[k : k + 1] for k in range(group)], 1) for f in force]
        rows[0:9] = cut_rows(jnp.concatenate(force, 0))
        acc[...] += add_hot(spread(rows, idx, high), low_hot(idx))
        return carry

    lax.fori_loop(0, blocks // group, some, 0, unroll=4)
    size = 3 * high
    tot_ref[...] = ((acc[2 * size :] + acc[size : 2 * size]) + acc[:size]) + int_ref[...]
    split_table(cut, tot_ref)
    count = share_ref.shape[1]
    for row, out in ((0, low_ref), (1, up_ref)):
        for at in range(0, count, 1024):
            idx = share_ref[row : row + 1, at : at + 1024]
            picked = pick(cut, low_hot(idx), high_mask(idx, high), 3, high)
            for c in range(3):
                out[c : c + 1, at : at + 1024] = picked[c]
    lim = jnp.min(back_ref[pl.ds(15, peers, stride=16), :], 0, keepdims=True)
    lim_ref[...] = lim


def last_body(
    lim_ref, tot_ref, share_ref, low_ref, up_ref, vel_ref, disp_ref, mass_ref, new_disp, new_vel, acc, cut
):
    high = tot_ref.shape[0] // 3
    count = share_ref.shape[1]
    total = jnp.zeros(acc.shape, f32)
    for row, src in ((0, low_ref), (1, up_ref)):
        for at in range(0, count, 1024):
            idx = share_ref[row : row + 1, at : at + 1024]
            cut[0:9] = cut_rows(src[:, at : at + 1024])
            total = total + add_hot(spread(cut, idx, high), low_hot(idx))
    rows = 3 * high
    acc[0:rows] = ((total[2 * rows :] + total[rows : 2 * rows]) + total[:rows]) + tot_ref[...]
    step = jnp.min(lim_ref[...], 1, keepdims=True)
    for h in range(high):
        at = slice(h * LOW, (h + 1) * LOW)
        mass = mass_ref[0:1, at]
        for c in range(3):
            vel = vel_ref[c : c + 1, at] + step * (acc[c * high + h : c * high + h + 1, :] / mass)
            new_vel[c : c + 1, at] = vel
            new_disp[c : c + 1, at] = disp_ref[c : c + 1, at] + step * vel


def vmem(count):
    return [pl.BlockSpec(memory_space=pltpu.VMEM)] * count


def smem(count):
    return [pl.BlockSpec(memory_space=pltpu.SMEM)] * count


def struct(*shape):
    return jax.ShapeDtypeStruct(shape, f32)


def send_call(send, disp, ref_pos, seg_node, seg_mask, peers):
    high = disp.shape[1] // LOW
    blocks, seg = seg_node.shape
    return pl.pallas_call(
        send_body,
        out_shape=(struct(blocks, 4, seg), struct(peers, send.shape[0] // peers, 4, seg)),
        in_specs=smem(1) + vmem(4),
        out_specs=tuple(vmem(2)),
        scratch_shapes=[
            pltpu.VMEM((3 * high, LOW), f32),
            pltpu.VMEM((PIECES * 3 * high, LOW), bf16),
        ],
        compiler_params=pltpu.CompilerParams(vmem_limit_bytes=24 << 20),
    )(send, disp, ref_pos, seg_node, seg_mask)


def force_call(first, stiff, disp, mass, nodes, part, scale):
    high = disp.shape[1] // LOW
    return pl.pallas_call(
        force_body,
        out_shape=(struct(nodes.shape[1] // WIDTH, 16, 4 * WIDTH), struct(1, 128)),
        in_specs=smem(2) + vmem(5),
        out_specs=tuple(vmem(2)),
        scratch_shapes=[
            pltpu.VMEM((4 * high, LOW), f32),
            pltpu.VMEM((PIECES * 4 * high, LOW), bf16),
        ],
        compiler_params=pltpu.CompilerParams(vmem_limit_bytes=24 << 20),
    )(first, stiff, disp, mass, nodes, part, scale)


def scatter_call(nodes, force, seg_node, own):
    high = nodes.shape[1] // LOW
    return pl.pallas_call(
        scatter_body,
        out_shape=struct(3 * high, LOW),
        in_specs=vmem(4),
        out_specs=vmem(1)[0],
        scratch_shapes=[
            pltpu.VMEM((PIECES * 3 * high, LOW), f32),
            pltpu.VMEM((16, 1024), f32),
        ],
        compiler_params=pltpu.CompilerParams(vmem_limit_bytes=24 << 20),
    )(nodes, force, seg_node, own)


def contact_call(pair_a, pair_slot, own, recv, live, lim, peers):
    blocks, _, seg = own.shape
    slots = recv.shape[0]
    return pl.pallas_call(
        contact_body,
        out_shape=(struct(blocks, 3, seg), struct(peers * 16, seg)),
        in_specs=smem(2) + vmem(4),
        out_specs=tuple(vmem(2)),
        scratch_shapes=[
            pltpu.VMEM((blocks, 3, seg, seg), f32),
            pltpu.VMEM((blocks, 3, seg, seg), f32),
            pltpu.VMEM((blocks, 3, seg, seg), f32),
            pltpu.VMEM((slots, 4, seg), f32),
            pltpu.VMEM((seg, seg), f32),
            pltpu.VMEM((8, seg, 3 * seg), bf16),
            pltpu.VMEM((3, slots * 8, seg), f32),
        ],
        compiler_params=pltpu.CompilerParams(vmem_limit_bytes=52 << 20),
    )(pair_a, pair_slot, own, recv, live, lim)


def seg_call(send, back, seg_node, inner, shared):
    high = inner.shape[0] // 3
    count = shared.shape[1]
    return pl.pallas_call(
        seg_body,
        out_shape=(struct(3 * high, LOW), struct(3, count), struct(3, count), struct(1, 128)),
        in_specs=vmem(5),
        out_specs=tuple(vmem(4)),
        scratch_shapes=[
            pltpu.VMEM((3, seg_node.shape[0], 128), f32),
            pltpu.VMEM((PIECES * 3 * high, LOW), bf16),
            pltpu.VMEM((PIECES * 3 * high, LOW), f32),
            pltpu.VMEM((16, 1024), f32),
        ],
        compiler_params=pltpu.CompilerParams(vmem_limit_bytes=24 << 20),
    )(send, back.reshape(-1, 128), seg_node, inner, shared)


def last_call(lim, total, shared, lower, upper, vel, disp, mass):
    high = total.shape[0] // 3
    return pl.pallas_call(
        last_body,
        out_shape=(struct(*disp.shape), struct(*disp.shape)),
        in_specs=vmem(8),
        out_specs=tuple(vmem(2)),
        scratch_shapes=[
            pltpu.VMEM((PIECES * 3 * high, LOW), f32),
            pltpu.VMEM((16, 1024), f32),
        ],
        compiler_params=pltpu.CompilerParams(vmem_limit_bytes=24 << 20),
    )(lim, total, shared, lower, upper, vel, disp, mass)


def shifted(value, axis, steps):
    count = lax.axis_size(axis)
    first, last = (max(0, -steps), min(count, count - steps))
    return lax.ppermute(value, axis, [(source, source + steps) for source in range(first, last)])


def shards(
    ref_pos,
    displacement,
    velocity,
    node_mass,
    elem_nodes,
    elem_part,
    elem_scale,
    part_stiff,
    shared,
    seg_node,
    seg_mask,
    send_blk,
    pair_a,
    pair_slot,
    pair_mask,
):
    peers = lax.axis_size("grp") * lax.axis_size("dev")
    mass = node_mass.reshape(1, -1)
    send = send_blk[0].T
    own, outgoing = send_call(send.reshape(-1), displacement, ref_pos, seg_node, seg_mask, peers)
    arrived = lax.all_to_all(outgoing, ("grp", "dev"), split_axis=0, concat_axis=0, tiled=True)
    first = (lax.axis_index(("grp", "dev")) * part_stiff.shape[0]).reshape(1)
    force, limit = force_call(
        first,
        part_stiff,
        displacement,
        mass,
        elem_nodes,
        elem_part.reshape(1, -1),
        elem_scale.reshape(1, -1),
    )
    own_force, far_force = contact_call(
        pair_a,
        pair_slot,
        own,
        arrived.reshape(-1, 4, own.shape[2]),
        pair_mask.reshape(-1, 128),
        limit,
        peers,
    )
    back = lax.all_to_all(
        far_force.reshape(peers, 16, -1), ("grp", "dev"), split_axis=0, concat_axis=0, tiled=True
    )
    inner = scatter_call(elem_nodes, force, seg_node, own_force)
    total, low_rows, up_rows, limits = seg_call(send, back, seg_node, inner, shared)
    from_lower = shifted(up_rows, "dev", 1)
    from_upper = shifted(low_rows, "dev", -1)
    return last_call(limits, total, shared, from_lower, from_upper, velocity, displacement, mass)


def solution(mesh):
    both = ("grp", "dev")
    return jax.shard_map(
        shards,
        mesh=mesh,
        in_specs=(
            P(None, both),
            P(None, both),
            P(None, both),
            P(both),
            P(None, both),
            P(both),
            P(both),
            P(both),
            P(None, both),
            P(both, None),
            P(both, None),
            P(both, None, None),
            P(both),
            P(both),
            P(both),
        ),
        out_specs=(P(None, both), P(None, both)),
        check_vma=False,
    )
```

```python
import math
from functools import partial

import jax
import jax.numpy as jnp
from jax import lax
from jax.experimental import pallas as pl
from jax.experimental.pallas import tpu as pltpu
from jax.sharding import PartitionSpec as P

SPRINGS = ((0, 1, 1.0), (1, 2, 1.0), (2, 3, 1.0), (3, 0, 1.0), (0, 2, 0.5), (1, 3, 0.5))
COURANT = 0.5
LOW = 256
PIECES = 3
FULL_VMEM = 64 << 20
SMALL_VMEM = 16 << 20
WIDTH = 256
SCALE = math.sqrt(math.log2(math.e))
PARK = 1.0e3
f32 = jnp.float32
bf16 = jnp.bfloat16


def pieces_of(x, count=PIECES):
    out = []
    for _ in range(count):
        head = x.astype(bf16)
        out.append(head)
        x = x - head.astype(f32)
    return out


def low_hot(idx):
    low = jnp.broadcast_to((idx & (LOW - 1)).astype(f32), (16, idx.shape[1])).astype(bf16)
    line = lax.broadcasted_iota(jnp.int32, low.shape, 0).astype(f32).astype(bf16)
    one, zero = jnp.ones(low.shape, bf16), jnp.zeros(low.shape, bf16)
    return jnp.concatenate(
        [jnp.where(low == line + float(16 * k), one, zero) for k in range(LOW // 16)], 0
    )


def high_mask(idx, high):
    rows = lax.broadcasted_iota(jnp.int32, (high, idx.shape[1]), 0)
    return rows == (idx >> 8)


def fill_table(tab, at, ref, row, high):
    for h in range(high):
        tab[at + h : at + h + 1, :] = ref[row : row + 1, h * LOW : (h + 1) * LOW]


def split_table(cut, tab):
    rows = tab.shape[0]
    for p, piece in enumerate(pieces_of(tab[...])):
        cut[p * rows : (p + 1) * rows, :] = piece


def pick(cut, hot, mask, comps, high):
    found = jnp.dot(cut[...], hot, preferred_element_type=f32)
    rows = comps * high
    found = (found[:rows] + found[rows : 2 * rows]) + found[2 * rows :]
    return [
        jnp.sum(jnp.where(mask, found[c * high : (c + 1) * high], 0.0), 0, keepdims=True)
        for c in range(comps)
    ]


def cut_rows(force):
    return jnp.concatenate([piece.astype(f32) for piece in pieces_of(force)], 0)


def spread(ref, idx, high):
    mask = high_mask(idx, high)
    return jnp.concatenate(
        [jnp.where(mask, ref[r : r + 1, :], 0.0).astype(bf16) for r in range(3 * PIECES)], 0
    )


def add_hot(left, hot):
    return lax.dot_general(left, hot, (((1,), (1,)), ((), ())), preferred_element_type=f32)


def send_body(send_ref, disp_ref, ref_ref, seg_ref, mask_ref, own_ref, out_ref, tab, cut):
    high = disp_ref.shape[1] // LOW
    blocks = seg_ref.shape[0]
    for c in range(3):
        fill_table(tab, c * high, disp_ref, c, high)
    for c in range(3):
        for h in range(high):
            at = c * high + h
            tab[at : at + 1, :] += ref_ref[c : c + 1, h * LOW : (h + 1) * LOW]
    split_table(cut, tab)
    group = 8

    def some(g, carry):
        base = pl.multiple_of(g * group, group)
        seg = seg_ref[pl.ds(base, group), :]
        idx = jnp.concatenate([seg[k : k + 1] for k in range(group)], 1)
        xyz = pick(cut, low_hot(idx), high_mask(idx, high), 3, high)
        weight = mask_ref[pl.ds(base, group), :].astype(f32)
        for k in range(group):
            for c in range(3):
                own_ref[base + k, c : c + 1, :] = xyz[c][:, k * 128 : (k + 1) * 128]
            own_ref[base + k, 3:4, :] = weight[k : k + 1]
        return carry

    lax.fori_loop(0, blocks // group, some, 0, unroll=4)
    peers, cap = out_ref.shape[0], out_ref.shape[1]

    def send(d, carry):
        for c in range(cap):
            out_ref[d, c] = own_ref[send_ref[c * peers + d]]
        return carry

    lax.fori_loop(0, peers, send, 0, unroll=4)


def force_body(
    first_ref, stiff_ref, disp_ref, mass_ref, nodes_ref, part_ref, scale_ref, force_ref, lim_ref, tab, cut
):
    high = disp_ref.shape[1] // LOW
    width = WIDTH
    parts = stiff_ref.shape[0]
    for c in range(3):
        fill_table(tab, c * high, disp_ref, c, high)
    fill_table(tab, 3 * high, mass_ref, 0, high)
    split_table(cut, tab)

    def some(g, limit):
        at = pl.ds(pl.multiple_of(g * width, width), width)
        part = part_ref[:, at] - first_ref[0]
        stiff = jnp.zeros(part.shape, f32)
        for k in range(parts):
            stiff = jnp.where(part == k, stiff_ref[k], stiff)
        stiff = stiff * scale_ref[:, at]
        nodes = nodes_ref[:, at]
        idx = jnp.concatenate([nodes[k : k + 1] for k in range(4)], 1)
        found = pick(cut, low_hot(idx), high_mask(idx, high), 4, high)
        corner = [[found[c][:, k * width : (k + 1) * width] for c in range(4)] for k in range(4)]
        mass = jnp.minimum(
            jnp.minimum(corner[0][3], corner[1][3]), jnp.minimum(corner[2][3], corner[3][3])
        )
        force = [[jnp.zeros((1, width), f32)] * 3 for _ in range(4)]
        for head, tail, weight in SPRINGS:
            pull = weight * stiff
            for c in range(3):
                term = pull * (corner[tail][c] - corner[head][c])
                force[head][c] = force[head][c] + term
                force[tail][c] = force[tail][c] - term
        joined = [jnp.concatenate([force[k][c] for k in range(4)], 1) for c in range(3)]
        force_ref[g, 0:9] = cut_rows(jnp.concatenate(joined, 0))
        return jnp.minimum(limit, COURANT * jnp.sqrt(mass / stiff))

    limit = lax.fori_loop(
        0, nodes_ref.shape[1] // width, some, jnp.full((1, width), jnp.inf, f32), unroll=4
    )
    lim_ref[...] = jnp.broadcast_to(jnp.min(limit, 1, keepdims=True), lim_ref.shape)


def scatter_body(
    nodes_ref, force_ref, seg_ref, own, vel_ref, disp_ref, mass_ref, tot_ref, vel_out, disp_out, inv_out, acc, cut
):
    high = tot_ref.shape[0] // 3
    for c in range(3):
        fill_table(vel_out, c * high, vel_ref, c, high)
        fill_table(disp_out, c * high, disp_ref, c, high)
    fill_table(inv_out, 0, mass_ref, 0, high)
    inv_out[...] = 1.0 / inv_out[...]
    acc[...] = jnp.zeros_like(acc)

    def some(g, carry):
        at = pl.ds(pl.multiple_of(g * WIDTH, WIDTH), WIDTH)
        nodes = nodes_ref[:, at]
        idx = jnp.concatenate([nodes[k : k + 1] for k in range(4)], 1)
        acc[...] += add_hot(spread(force_ref.at[g], idx, high), low_hot(idx))
        return carry

    lax.fori_loop(0, force_ref.shape[0], some, 0, unroll=4)
    group = 8

    def more(g, carry):
        base = pl.multiple_of(g * group, group)
        seg = seg_ref[pl.ds(base, group), :]
        idx = jnp.concatenate([seg[k : k + 1] for k in range(group)], 1)
        cut[0:9] = cut_rows(jnp.concatenate([own[base + k] for k in range(group)], 1))
        acc[...] += add_hot(spread(cut, idx, high), low_hot(idx))
        return carry

    lax.fori_loop(0, seg_ref.shape[0] // group, more, 0, unroll=4)
    rows = 3 * high
    tot_ref[...] = (acc[2 * rows :] + acc[rows : 2 * rows]) + acc[:rows]


def contact_body(
    near_ref, far_ref, own_ref, recv_ref, live_ref, lim_ref, own_out, far_out, wide, total_a, total_b, recoils, landed, near, far, rows, chosen, sems
):
    blocks = total_a.shape[0]
    slots = landed.shape[0]
    seg = landed.shape[2]
    cap = 5
    fetch = pltpu.make_async_copy(recv_ref, landed, sems.at[0])
    fetch.start()

    group = 8
    line = lax.broadcasted_iota(jnp.int32, (seg, 3 * seg), 0)
    part = lax.broadcasted_iota(jnp.int32, (seg, 3 * seg), 1) >> 7
    for k in range(group):
        at = line - 16 * k
        hit = (at == part) | (at == part + 3) | (at == part + 6)
        chosen[k] = jnp.where(hit, 1.0, 0.0).astype(bf16)
    rows[...] = jnp.zeros_like(rows)

    def widen(g, carry):
        for k in range(group):
            block = own_ref[g * group + k]
            x = jnp.where(block[3:4] > 0.5, block[0:1] * SCALE, PARK)
            xyz = jnp.concatenate([x, block[1:3] * SCALE], 0)
            for p, piece in enumerate(pieces_of(xyz)):
                rows[16 * k + 3 * p : 16 * k + 3 * p + 3, :] = piece.astype(f32)
        columns = rows[...].T.astype(bf16)
        for k in range(group):
            out = jnp.dot(columns, chosen[k], preferred_element_type=f32)
            for c in range(3):
                wide[g * group + k, c] = out[:, c * seg : (c + 1) * seg]
                total_a[g * group + k, c] = jnp.zeros((seg, seg), f32)
                total_b[g * group + k, c] = jnp.zeros((seg, seg), f32)
        return carry

    lax.fori_loop(0, blocks // group, widen, 0, unroll=4)
    recoils[...] = jnp.zeros_like(recoils)
    live = jnp.sum(live_ref[...])
    fetch.wait()

    def pair(p, total):
        b = near_ref[p]
        s = far_ref[p]
        there = [jnp.broadcast_to(landed[s, c : c + 1, :], (8, seg)) for c in range(4)]
        x = jnp.where(there[3] > 0.5, there[0] * SCALE, -PARK)
        there = [x, there[1] * SCALE, there[2] * SCALE]
        recoil = [None] * 3
        for v in range(seg // 8):
            at = pl.ds(v * 8, 8)
            gap = [wide[b, c, at, :] - there[c] for c in range(3)]
            square = gap[0] * gap[0] + gap[1] * gap[1] + gap[2] * gap[2]
            weight = jnp.exp2(-square)
            for c in range(3):
                push = weight * gap[c]
                total[b, c, at, :] += push
                recoil[c] = push if recoil[c] is None else recoil[c] + push
        for c in range(3):
            recoils[c, pl.ds(pl.multiple_of(s * 8, 8), 8), :] += recoil[c]

    def four(q, carry):
        pair(4 * q, total_a)
        pair(4 * q + 1, total_b)
        pair(4 * q + 2, total_a)
        pair(4 * q + 3, total_b)
        return carry

    def one(p, carry):
        pair(p, total_a)
        return carry

    whole = live >> 2
    lax.fori_loop(0, whole, four, 0)
    lax.fori_loop(4 * whole, live, one, 0)
    peers = slots // cap
    stamp = jnp.broadcast_to(lim_ref[...], (8, seg))

    def finish(g, carry):
        for k in range(cap):
            for c in range(3):
                at = g * (64 * cap) + k * 8
                rows = [recoils[c, pl.ds(at + r, 8, stride=8 * cap), :] for r in range(8)]
                while len(rows) > 1:
                    rows = [x + y for x, y in zip(rows[::2], rows[1::2])]
                far[pl.ds(g * 128 + 3 * k + c, 8, stride=16), :] = rows[0] * (-1.0 / SCALE)
        far[pl.ds(g * 128 + 15, 8, stride=16), :] = stamp
        return carry

    lax.fori_loop(0, peers // 8, finish, 0, unroll=4)
    give_far = pltpu.make_async_copy(far, far_out, sems.at[1])
    give_far.start()

    def close(b, carry):
        for c in range(3):
            total = total_a[b, c] + total_b[b, c]
            near[b, c : c + 1, :] = jnp.sum(total.T, 0, keepdims=True) * (1.0 / SCALE)
        return carry

    lax.fori_loop(0, blocks, close, 0, unroll=8)
    give_near = pltpu.make_async_copy(near, own_out, sems.at[2])
    give_near.start()
    give_far.wait()
    give_near.wait()


def seg_body(
    send_ref, back_ref, seg_ref, int_ref, share_ref, tot_ref, low_ref, up_ref, lim_ref, sums, cut, acc, rows
):
    blocks = seg_ref.shape[0]
    peers = back_ref.shape[0] // 16
    cap = 5
    high = int_ref.shape[0] // 3
    line = lax.broadcasted_iota(jnp.int32, (blocks, peers), 0)
    sums[...] = jnp.zeros_like(sums)
    for c in range(cap):
        hot = jnp.where(line == send_ref[c : c + 1, :], 1.0, 0.0).astype(bf16)
        for k in range(3):
            force = back_ref[pl.ds(3 * c + k, peers, stride=16), :]
            found = jnp.dot(hot, jnp.concatenate(pieces_of(force), 1), preferred_element_type=f32)
            sums[k] += (found[:, 256:] + found[:, 128:256]) + found[:, :128]
    acc[...] = jnp.zeros_like(acc)
    group = 8

    def some(g, carry):
        base = pl.multiple_of(g * group, group)
        seg = seg_ref[pl.ds(base, group), :]
        idx = jnp.concatenate([seg[k : k + 1] for k in range(group)], 1)
        force = [sums[c, pl.ds(base, group), :] for c in range(3)]
        force = [jnp.concatenate([f[k : k + 1] for k in range(group)], 1) for f in force]
        rows[0:9] = cut_rows(jnp.concatenate(force, 0))
        acc[...] += add_hot(spread(rows, idx, high), low_hot(idx))
        return carry

    lax.fori_loop(0, blocks // group, some, 0, unroll=4)
    size = 3 * high
    tot_ref[...] = ((acc[2 * size :] + acc[size : 2 * size]) + acc[:size]) + int_ref[...]
    split_table(cut, tot_ref)
    count = share_ref.shape[1]
    for row, out in ((0, low_ref), (1, up_ref)):
        for at in range(0, count, 1024):
            idx = share_ref[row : row + 1, at : at + 1024]
            picked = pick(cut, low_hot(idx), high_mask(idx, high), 3, high)
            for c in range(3):
                out[c : c + 1, at : at + 1024] = picked[c]
    lim = jnp.min(back_ref[pl.ds(15, peers, stride=16), :], 0, keepdims=True)
    lim_ref[...] = lim


def last_body(
    lim_ref, tot_ref, share_ref, low_ref, up_ref, vel_ref, disp_ref, inv_ref, new_disp, new_vel, cut
):
    high = tot_ref.shape[0] // 3
    count = share_ref.shape[1]
    total = jnp.zeros((PIECES * 3 * high, LOW), f32)
    for row, src in ((0, low_ref), (1, up_ref)):
        for k, at in enumerate(range(0, count, 1024)):
            idx = share_ref[row : row + 1, at : at + 1024]
            rows = cut.at[2 * row + k]
            rows[0:9] = cut_rows(src[:, at : at + 1024])
            total = total + add_hot(spread(rows, idx, high), low_hot(idx))
    size = 3 * high
    force = ((total[2 * size :] + total[size : 2 * size]) + total[:size]) + tot_ref[...]
    step = jnp.min(lim_ref[...], 1, keepdims=True)
    for c in range(3):
        at = slice(c * high, (c + 1) * high)
        vel = vel_ref[at] + step * (force[at] * inv_ref[...])
        disp = disp_ref[at] + step * vel
        for h in range(high):
            new_vel[c : c + 1, h * LOW : (h + 1) * LOW] = vel[h : h + 1]
            new_disp[c : c + 1, h * LOW : (h + 1) * LOW] = disp[h : h + 1]


def vmem(count):
    return [pl.BlockSpec(memory_space=pltpu.VMEM)] * count


def hbm(count):
    return [pl.BlockSpec(memory_space=pltpu.HBM)] * count


def smem(count):
    return [pl.BlockSpec(memory_space=pltpu.SMEM)] * count


def struct(*shape):
    return jax.ShapeDtypeStruct(shape, f32)


def send_call(send, disp, ref_pos, seg_node, seg_mask, peers):
    high = disp.shape[1] // LOW
    blocks, seg = seg_node.shape
    return pl.pallas_call(
        send_body,
        out_shape=(struct(blocks, 4, seg), struct(peers, send.shape[0] // peers, 4, seg)),
        in_specs=smem(1) + vmem(4),
        out_specs=tuple(vmem(2)),
        scratch_shapes=[
            pltpu.VMEM((3 * high, LOW), f32),
            pltpu.VMEM((PIECES * 3 * high, LOW), bf16),
        ],
    )(send, disp, ref_pos, seg_node, seg_mask)


def force_call(first, stiff, disp, mass, nodes, part, scale):
    high = disp.shape[1] // LOW
    return pl.pallas_call(
        force_body,
        out_shape=(struct(nodes.shape[1] // WIDTH, 16, 4 * WIDTH), struct(1, 128)),
        in_specs=smem(2) + vmem(5),
        out_specs=tuple(vmem(2)),
        scratch_shapes=[
            pltpu.VMEM((4 * high, LOW), f32),
            pltpu.VMEM((PIECES * 4 * high, LOW), bf16),
        ],
        compiler_params=pltpu.CompilerParams(vmem_limit_bytes=FULL_VMEM),
    )(first, stiff, disp, mass, nodes, part, scale)


def scatter_call(nodes, force, seg_node, own, vel, disp, mass):
    high = nodes.shape[1] // LOW
    return pl.pallas_call(
        scatter_body,
        out_shape=(struct(3 * high, LOW), struct(3 * high, LOW), struct(3 * high, LOW), struct(high, LOW)),
        in_specs=vmem(7),
        out_specs=tuple(vmem(4)),
        scratch_shapes=[
            pltpu.VMEM((PIECES * 3 * high, LOW), f32),
            pltpu.VMEM((16, 1024), f32),
        ],
        compiler_params=pltpu.CompilerParams(vmem_limit_bytes=SMALL_VMEM),
    )(nodes, force, seg_node, own, vel, disp, mass)


def contact_call(pair_a, pair_slot, own, recv, live, lim, peers):
    blocks, _, seg = own.shape
    slots = recv.shape[0]
    return pl.pallas_call(
        contact_body,
        out_shape=(struct(blocks, 3, seg), struct(peers * 16, seg)),
        in_specs=smem(2) + vmem(1) + hbm(1) + vmem(2),
        out_specs=tuple(hbm(2)),
        scratch_shapes=[
            pltpu.VMEM((blocks, 3, seg, seg), f32),
            pltpu.VMEM((blocks, 3, seg, seg), f32),
            pltpu.VMEM((blocks, 3, seg, seg), f32),
            pltpu.VMEM((3, slots * 8, seg), f32),
            pltpu.VMEM(recv.shape, f32),
            pltpu.VMEM((blocks, 3, seg), f32),
            pltpu.VMEM((peers * 16, seg), f32),
            pltpu.VMEM((seg, seg), f32),
            pltpu.VMEM((8, seg, 3 * seg), bf16),
            pltpu.SemaphoreType.DMA((3,)),
        ],
        compiler_params=pltpu.CompilerParams(vmem_limit_bytes=FULL_VMEM),
    )(pair_a, pair_slot, own, recv, live, lim)


def seg_call(send, back, seg_node, inner, shared):
    high = inner.shape[0] // 3
    count = shared.shape[1]
    return pl.pallas_call(
        seg_body,
        out_shape=(struct(3 * high, LOW), struct(3, count), struct(3, count), struct(1, 128)),
        in_specs=vmem(5),
        out_specs=tuple(vmem(4)),
        scratch_shapes=[
            pltpu.VMEM((3, seg_node.shape[0], 128), f32),
            pltpu.VMEM((PIECES * 3 * high, LOW), bf16),
            pltpu.VMEM((PIECES * 3 * high, LOW), f32),
            pltpu.VMEM((16, 1024), f32),
        ],
        compiler_params=pltpu.CompilerParams(vmem_limit_bytes=SMALL_VMEM),
    )(send, back.reshape(-1, 128), seg_node, inner, shared)


def last_call(lim, total, shared, lower, upper, vel, disp, inv):
    high = inv.shape[0]
    nodes = struct(3, high * LOW)
    return pl.pallas_call(
        last_body,
        out_shape=(nodes, nodes),
        in_specs=vmem(8),
        out_specs=tuple(vmem(2)),
        scratch_shapes=[pltpu.VMEM((4, 16, 1024), f32)],
        compiler_params=pltpu.CompilerParams(vmem_limit_bytes=SMALL_VMEM),
    )(lim, total, shared, lower, upper, vel, disp, inv)


def shifted(value, axis, steps):
    count = lax.axis_size(axis)
    first, last = (max(0, -steps), min(count, count - steps))
    return lax.ppermute(value, axis, [(source, source + steps) for source in range(first, last)])


def shards(
    ref_pos,
    displacement,
    velocity,
    node_mass,
    elem_nodes,
    elem_part,
    elem_scale,
    part_stiff,
    shared,
    seg_node,
    seg_mask,
    send_blk,
    pair_a,
    pair_slot,
    pair_mask,
):
    peers = lax.axis_size("grp") * lax.axis_size("dev")
    mass = node_mass.reshape(1, -1)
    send = send_blk[0].T
    own, outgoing = send_call(send.reshape(-1), displacement, ref_pos, seg_node, seg_mask, peers)
    arrived = lax.all_to_all(outgoing, ("grp", "dev"), split_axis=0, concat_axis=0, tiled=True)
    first = (lax.axis_index(("grp", "dev")) * part_stiff.shape[0]).reshape(1)
    force, limit = force_call(
        first,
        part_stiff,
        displacement,
        mass,
        elem_nodes,
        elem_part.reshape(1, -1),
        elem_scale.reshape(1, -1),
    )
    own_force, far_force = contact_call(
        pair_a,
        pair_slot,
        own,
        arrived.reshape(-1, 4, own.shape[2]),
        pair_mask.reshape(-1, 128),
        limit,
        peers,
    )
    back = lax.all_to_all(
        far_force.reshape(peers, 16, -1), ("grp", "dev"), split_axis=0, concat_axis=0, tiled=True
    )
    inner, vel, disp, inv = scatter_call(
        elem_nodes, force, seg_node, own_force, velocity, displacement, mass
    )
    total, low_rows, up_rows, limits = seg_call(send, back, seg_node, inner, shared)
    from_lower = shifted(up_rows, "dev", 1)
    from_upper = shifted(low_rows, "dev", -1)
    return last_call(limits, total, shared, from_lower, from_upper, vel, disp, inv)


def solution(mesh):
    both = ("grp", "dev")
    return jax.shard_map(
        shards,
        mesh=mesh,
        in_specs=(
            P(None, both),
            P(None, both),
            P(None, both),
            P(both),
            P(None, both),
            P(both),
            P(both),
            P(both),
            P(None, both),
            P(both, None),
            P(both, None),
            P(both, None, None),
            P(both),
            P(both),
            P(both),
        ),
        out_specs=(P(None, both), P(None, both)),
        check_vma=False,
    )
```

```python
import math
from functools import partial

import jax
import jax.numpy as jnp
from jax import lax
from jax.experimental import pallas as pl
from jax.experimental.pallas import tpu as pltpu
from jax.sharding import PartitionSpec as P

SPRINGS = ((0, 1, 1.0), (1, 2, 1.0), (2, 3, 1.0), (3, 0, 1.0), (0, 2, 0.5), (1, 3, 0.5))
COURANT = 0.5
LOW = 256
PIECES = 3
FULL_VMEM = 64 << 20
SMALL_VMEM = 16 << 20
WIDTH = 256
SCALE = math.sqrt(math.log2(math.e))
PARK = 1.0e3
f32 = jnp.float32
bf16 = jnp.bfloat16


def pieces_of(x, count=PIECES):
    out = []
    for _ in range(count):
        head = x.astype(bf16)
        out.append(head)
        x = x - head.astype(f32)
    return out


def low_hot(idx):
    low = jnp.broadcast_to((idx & (LOW - 1)).astype(f32), (16, idx.shape[1])).astype(bf16)
    line = lax.broadcasted_iota(jnp.int32, low.shape, 0).astype(f32).astype(bf16)
    one, zero = jnp.ones(low.shape, bf16), jnp.zeros(low.shape, bf16)
    return jnp.concatenate(
        [jnp.where(low == line + float(16 * k), one, zero) for k in range(LOW // 16)], 0
    )


def high_mask(idx, high):
    rows = lax.broadcasted_iota(jnp.int32, (high, idx.shape[1]), 0)
    return rows == (idx >> 8)


def fill_table(tab, at, ref, row, high):
    for h in range(high):
        tab[at + h : at + h + 1, :] = ref[row : row + 1, h * LOW : (h + 1) * LOW]


def split_table(cut, tab):
    rows = tab.shape[0]
    for p, piece in enumerate(pieces_of(tab[...])):
        cut[p * rows : (p + 1) * rows, :] = piece


def pick(cut, hot, mask, comps, high):
    found = jnp.dot(cut[...], hot, preferred_element_type=f32)
    rows = comps * high
    found = (found[:rows] + found[rows : 2 * rows]) + found[2 * rows :]
    return [
        jnp.sum(jnp.where(mask, found[c * high : (c + 1) * high], 0.0), 0, keepdims=True)
        for c in range(comps)
    ]


def cut_rows(force):
    return jnp.concatenate([piece.astype(f32) for piece in pieces_of(force)], 0)


def spread(ref, idx, high):
    mask = high_mask(idx, high)
    return jnp.concatenate(
        [jnp.where(mask, ref[r : r + 1, :], 0.0).astype(bf16) for r in range(3 * PIECES)], 0
    )


def add_hot(left, hot):
    return lax.dot_general(left, hot, (((1,), (1,)), ((), ())), preferred_element_type=f32)


def send_body(send_ref, disp_ref, ref_ref, seg_ref, mask_ref, own_ref, out_ref, tab, cut):
    high = disp_ref.shape[1] // LOW
    blocks = seg_ref.shape[0]
    for c in range(3):
        fill_table(tab, c * high, disp_ref, c, high)
    for c in range(3):
        for h in range(high):
            at = c * high + h
            tab[at : at + 1, :] += ref_ref[c : c + 1, h * LOW : (h + 1) * LOW]
    split_table(cut, tab)
    group = 8

    def some(g, carry):
        base = pl.multiple_of(g * group, group)
        seg = seg_ref[pl.ds(base, group), :]
        idx = jnp.concatenate([seg[k : k + 1] for k in range(group)], 1)
        xyz = pick(cut, low_hot(idx), high_mask(idx, high), 3, high)
        weight = mask_ref[pl.ds(base, group), :].astype(f32)
        for k in range(group):
            for c in range(3):
                own_ref[base + k, c : c + 1, :] = xyz[c][:, k * 128 : (k + 1) * 128]
            own_ref[base + k, 3:4, :] = weight[k : k + 1]
        return carry

    lax.fori_loop(0, blocks // group, some, 0, unroll=4)
    peers, cap = out_ref.shape[0], out_ref.shape[1]

    def send(d, carry):
        for c in range(cap):
            out_ref[d, c] = own_ref[send_ref[c, 0, d]]
        return carry

    lax.fori_loop(0, peers, send, 0, unroll=4)


def force_body(
    first_ref, stiff_ref, disp_ref, mass_ref, nodes_ref, part_ref, scale_ref, force_ref, lim_ref, tab, cut
):
    high = disp_ref.shape[1] // LOW
    width = WIDTH
    parts = stiff_ref.shape[0]
    for c in range(3):
        fill_table(tab, c * high, disp_ref, c, high)
    fill_table(tab, 3 * high, mass_ref, 0, high)
    split_table(cut, tab)

    def some(g, limit):
        at = pl.ds(pl.multiple_of(g * width, width), width)
        part = part_ref[:, at] - first_ref[0]
        stiff = jnp.zeros(part.shape, f32)
        for k in range(parts):
            stiff = jnp.where(part == k, stiff_ref[k], stiff)
        stiff = stiff * scale_ref[:, at]
        nodes = nodes_ref[:, at]
        idx = jnp.concatenate([nodes[k : k + 1] for k in range(4)], 1)
        found = pick(cut, low_hot(idx), high_mask(idx, high), 4, high)
        corner = [[found[c][:, k * width : (k + 1) * width] for c in range(4)] for k in range(4)]
        mass = jnp.minimum(
            jnp.minimum(corner[0][3], corner[1][3]), jnp.minimum(corner[2][3], corner[3][3])
        )
        force = [[jnp.zeros((1, width), f32)] * 3 for _ in range(4)]
        for head, tail, weight in SPRINGS:
            pull = weight * stiff
            for c in range(3):
                term = pull * (corner[tail][c] - corner[head][c])
                force[head][c] = force[head][c] + term
                force[tail][c] = force[tail][c] - term
        joined = [jnp.concatenate([force[k][c] for k in range(4)], 1) for c in range(3)]
        force_ref[g, 0:9] = cut_rows(jnp.concatenate(joined, 0))
        return jnp.minimum(limit, COURANT * jnp.sqrt(mass / stiff))

    limit = lax.fori_loop(
        0, nodes_ref.shape[1] // width, some, jnp.full((1, width), jnp.inf, f32), unroll=4
    )
    lim_ref[...] = jnp.broadcast_to(jnp.min(limit, 1, keepdims=True), lim_ref.shape)


def scatter_body(
    nodes_ref, force_ref, seg_ref, own, vel_ref, disp_ref, mass_ref, tot_ref, vel_out, disp_out, inv_out, acc, cut
):
    high = tot_ref.shape[0] // 3
    for c in range(3):
        fill_table(vel_out, c * high, vel_ref, c, high)
        fill_table(disp_out, c * high, disp_ref, c, high)
    fill_table(inv_out, 0, mass_ref, 0, high)
    inv_out[...] = 1.0 / inv_out[...]
    acc[...] = jnp.zeros_like(acc)

    def some(g, carry):
        at = pl.ds(pl.multiple_of(g * WIDTH, WIDTH), WIDTH)
        nodes = nodes_ref[:, at]
        idx = jnp.concatenate([nodes[k : k + 1] for k in range(4)], 1)
        acc[...] += add_hot(spread(force_ref.at[g], idx, high), low_hot(idx))
        return carry

    lax.fori_loop(0, force_ref.shape[0], some, 0, unroll=4)
    group = 8

    def more(g, carry):
        base = pl.multiple_of(g * group, group)
        seg = seg_ref[pl.ds(base, group), :]
        idx = jnp.concatenate([seg[k : k + 1] for k in range(group)], 1)
        cut[0:9] = cut_rows(jnp.concatenate([own[base + k] for k in range(group)], 1))
        acc[...] += add_hot(spread(cut, idx, high), low_hot(idx))
        return carry

    lax.fori_loop(0, seg_ref.shape[0] // group, more, 0, unroll=4)
    rows = 3 * high
    tot_ref[...] = (acc[2 * rows :] + acc[rows : 2 * rows]) + acc[:rows]


def contact_body(
    near_ref, far_ref, own_ref, recv_ref, live_ref, lim_ref, own_out, far_out, wide, total_a, total_b, recoils, landed, near, far, rows, chosen, sems
):
    blocks = total_a.shape[0]
    slots = landed.shape[0]
    seg = landed.shape[2]
    cap = 5
    fetch = pltpu.make_async_copy(recv_ref, landed, sems.at[0])
    fetch.start()

    group = 8
    line = lax.broadcasted_iota(jnp.int32, (seg, 3 * seg), 0)
    part = lax.broadcasted_iota(jnp.int32, (seg, 3 * seg), 1) >> 7
    for k in range(group):
        at = line - 16 * k
        hit = (at == part) | (at == part + 3) | (at == part + 6)
        chosen[k] = jnp.where(hit, 1.0, 0.0).astype(bf16)
    rows[...] = jnp.zeros_like(rows)

    def widen(g, carry):
        for k in range(group):
            block = own_ref[g * group + k]
            x = jnp.where(block[3:4] > 0.5, block[0:1] * SCALE, PARK)
            xyz = jnp.concatenate([x, block[1:3] * SCALE], 0)
            for p, piece in enumerate(pieces_of(xyz)):
                rows[16 * k + 3 * p : 16 * k + 3 * p + 3, :] = piece.astype(f32)
        columns = rows[...].T.astype(bf16)
        for k in range(group):
            out = jnp.dot(columns, chosen[k], preferred_element_type=f32)
            for c in range(3):
                wide[g * group + k, c] = out[:, c * seg : (c + 1) * seg]
                total_a[g * group + k, c] = jnp.zeros((seg, seg), f32)
                total_b[g * group + k, c] = jnp.zeros((seg, seg), f32)
        return carry

    lax.fori_loop(0, blocks // group, widen, 0, unroll=4)
    recoils[...] = jnp.zeros_like(recoils)
    live = jnp.sum(live_ref[...])
    fetch.wait()

    def pair(p, total):
        b = near_ref[p]
        s = far_ref[p]
        there = [jnp.broadcast_to(landed[s, c : c + 1, :], (8, seg)) for c in range(4)]
        x = jnp.where(there[3] > 0.5, there[0] * SCALE, -PARK)
        there = [x, there[1] * SCALE, there[2] * SCALE]
        recoil = [None] * 3
        for v in range(seg // 8):
            at = pl.ds(v * 8, 8)
            gap = [wide[b, c, at, :] - there[c] for c in range(3)]
            square = gap[0] * gap[0] + gap[1] * gap[1] + gap[2] * gap[2]
            weight = jnp.exp2(-square)
            for c in range(3):
                push = weight * gap[c]
                total[b, c, at, :] += push
                recoil[c] = push if recoil[c] is None else recoil[c] + push
        for c in range(3):
            recoils[c, pl.ds(pl.multiple_of(s * 8, 8), 8), :] += recoil[c]

    def four(q, carry):
        pair(8 * q, total_a)
        pair(8 * q + 1, total_b)
        pair(8 * q + 2, total_a)
        pair(8 * q + 3, total_b)
        pair(8 * q + 4, total_a)
        pair(8 * q + 5, total_b)
        pair(8 * q + 6, total_a)
        pair(8 * q + 7, total_b)
        return carry

    def one(p, carry):
        pair(p, total_a)
        return carry

    whole = live >> 3
    lax.fori_loop(0, whole, four, 0)
    lax.fori_loop(8 * whole, live, one, 0)
    peers = slots // cap
    stamp = jnp.broadcast_to(lim_ref[...], (8, seg))

    def finish(g, carry):
        for k in range(cap):
            for c in range(3):
                at = g * (64 * cap) + k * 8
                rows = [recoils[c, pl.ds(at + r, 8, stride=8 * cap), :] for r in range(8)]
                while len(rows) > 1:
                    rows = [x + y for x, y in zip(rows[::2], rows[1::2])]
                far[pl.ds(g * 128 + 3 * k + c, 8, stride=16), :] = rows[0] * (-1.0 / SCALE)
        far[pl.ds(g * 128 + 15, 8, stride=16), :] = stamp
        return carry

    lax.fori_loop(0, peers // 8, finish, 0, unroll=4)
    give_far = pltpu.make_async_copy(far, far_out, sems.at[1])
    give_far.start()

    def close(b, carry):
        total = total_a[b, 0] + total_b[b, 0]
        summed = lax.dot_general(
            jnp.ones((16, 3 * seg), bf16),
            jnp.concatenate(pieces_of(total), 1),
            (((1,), (1,)), ((), ())),
            preferred_element_type=f32,
        )
        near[b, 0:1, :] = summed[0:1] * (1.0 / SCALE)
        for c in (1, 2):
            total = total_a[b, c] + total_b[b, c]
            near[b, c : c + 1, :] = jnp.sum(total.T, 0, keepdims=True) * (1.0 / SCALE)
        return carry

    lax.fori_loop(0, blocks, close, 0, unroll=8)
    give_near = pltpu.make_async_copy(near, own_out, sems.at[2])
    give_near.start()
    give_far.wait()
    give_near.wait()


def seg_body(
    send_ref, back_ref, seg_ref, int_ref, share_ref, tot_ref, low_ref, up_ref, lim_ref, sums, cut, acc, rows
):
    blocks = seg_ref.shape[0]
    peers = back_ref.shape[0] // 16
    cap = 5
    high = int_ref.shape[0] // 3
    line = lax.broadcasted_iota(jnp.int32, (blocks, peers), 0)
    sums[...] = jnp.zeros_like(sums)
    for c in range(cap):
        hot = jnp.where(line == send_ref[c], 1.0, 0.0).astype(bf16)
        for k in range(3):
            force = back_ref[pl.ds(3 * c + k, peers, stride=16), :]
            found = jnp.dot(hot, jnp.concatenate(pieces_of(force), 1), preferred_element_type=f32)
            sums[k] += (found[:, 256:] + found[:, 128:256]) + found[:, :128]
    acc[...] = jnp.zeros_like(acc)
    group = 8

    def some(g, carry):
        base = pl.multiple_of(g * group, group)
        seg = seg_ref[pl.ds(base, group), :]
        idx = jnp.concatenate([seg[k : k + 1] for k in range(group)], 1)
        force = [sums[c, pl.ds(base, group), :] for c in range(3)]
        force = [jnp.concatenate([f[k : k + 1] for k in range(group)], 1) for f in force]
        rows[0:9] = cut_rows(jnp.concatenate(force, 0))
        acc[...] += add_hot(spread(rows, idx, high), low_hot(idx))
        return carry

    lax.fori_loop(0, blocks // group, some, 0, unroll=4)
    size = 3 * high
    tot_ref[...] = ((acc[2 * size :] + acc[size : 2 * size]) + acc[:size]) + int_ref[...]
    split_table(cut, tot_ref)
    count = share_ref.shape[1]
    for row, out in ((0, low_ref), (1, up_ref)):
        for at in range(0, count, 1024):
            idx = share_ref[row : row + 1, at : at + 1024]
            picked = pick(cut, low_hot(idx), high_mask(idx, high), 3, high)
            for c in range(3):
                out[c : c + 1, at : at + 1024] = picked[c]
    lim = jnp.min(back_ref[pl.ds(15, peers, stride=16), :], 0, keepdims=True)
    lim_ref[...] = lim


def last_body(
    lim_ref, tot_ref, share_ref, low_ref, up_ref, vel_ref, disp_ref, inv_ref, new_disp, new_vel, cut
):
    high = tot_ref.shape[0] // 3
    count = share_ref.shape[1]
    total = jnp.zeros((PIECES * 3 * high, LOW), f32)
    for row, src in ((0, low_ref), (1, up_ref)):
        for k, at in enumerate(range(0, count, 1024)):
            idx = share_ref[row : row + 1, at : at + 1024]
            rows = cut.at[2 * row + k]
            rows[0:9] = cut_rows(src[:, at : at + 1024])
            total = total + add_hot(spread(rows, idx, high), low_hot(idx))
    size = 3 * high
    force = ((total[2 * size :] + total[size : 2 * size]) + total[:size]) + tot_ref[...]
    step = jnp.min(lim_ref[...], 1, keepdims=True)
    for c in range(3):
        at = slice(c * high, (c + 1) * high)
        vel = vel_ref[at] + step * (force[at] * inv_ref[...])
        disp = disp_ref[at] + step * vel
        for h in range(high):
            new_vel[c : c + 1, h * LOW : (h + 1) * LOW] = vel[h : h + 1]
            new_disp[c : c + 1, h * LOW : (h + 1) * LOW] = disp[h : h + 1]


def vmem(count):
    return [pl.BlockSpec(memory_space=pltpu.VMEM)] * count


def hbm(count):
    return [pl.BlockSpec(memory_space=pltpu.HBM)] * count


def smem(count):
    return [pl.BlockSpec(memory_space=pltpu.SMEM)] * count


def struct(*shape):
    return jax.ShapeDtypeStruct(shape, f32)


def send_call(send, disp, ref_pos, seg_node, seg_mask, peers):
    high = disp.shape[1] // LOW
    blocks, seg = seg_node.shape
    return pl.pallas_call(
        send_body,
        out_shape=(struct(blocks, 4, seg), struct(peers, send.shape[0], 4, seg)),
        in_specs=smem(1) + vmem(4),
        out_specs=tuple(vmem(2)),
        scratch_shapes=[
            pltpu.VMEM((3 * high, LOW), f32),
            pltpu.VMEM((PIECES * 3 * high, LOW), bf16),
        ],
    )(send, disp, ref_pos, seg_node, seg_mask)


def force_call(first, stiff, disp, mass, nodes, part, scale):
    high = disp.shape[1] // LOW
    return pl.pallas_call(
        force_body,
        out_shape=(struct(nodes.shape[1] // WIDTH, 16, 4 * WIDTH), struct(1, 128)),
        in_specs=smem(2) + vmem(5),
        out_specs=tuple(vmem(2)),
        scratch_shapes=[
            pltpu.VMEM((4 * high, LOW), f32),
            pltpu.VMEM((PIECES * 4 * high, LOW), bf16),
        ],
        compiler_params=pltpu.CompilerParams(vmem_limit_bytes=FULL_VMEM),
    )(first, stiff, disp, mass, nodes, part, scale)


def scatter_call(nodes, force, seg_node, own, vel, disp, mass):
    high = nodes.shape[1] // LOW
    return pl.pallas_call(
        scatter_body,
        out_shape=(struct(3 * high, LOW), struct(3 * high, LOW), struct(3 * high, LOW), struct(high, LOW)),
        in_specs=vmem(7),
        out_specs=tuple(vmem(4)),
        scratch_shapes=[
            pltpu.VMEM((PIECES * 3 * high, LOW), f32),
            pltpu.VMEM((16, 1024), f32),
        ],
        compiler_params=pltpu.CompilerParams(vmem_limit_bytes=SMALL_VMEM),
    )(nodes, force, seg_node, own, vel, disp, mass)


def contact_call(pair_a, pair_slot, own, recv, live, lim, peers):
    blocks, _, seg = own.shape
    slots = recv.shape[0]
    return pl.pallas_call(
        contact_body,
        out_shape=(struct(blocks, 3, seg), struct(peers * 16, seg)),
        in_specs=smem(2) + vmem(1) + hbm(1) + vmem(2),
        out_specs=tuple(hbm(2)),
        scratch_shapes=[
            pltpu.VMEM((blocks, 3, seg, seg), f32),
            pltpu.VMEM((blocks, 3, seg, seg), f32),
            pltpu.VMEM((blocks, 3, seg, seg), f32),
            pltpu.VMEM((3, slots * 8, seg), f32),
            pltpu.VMEM(recv.shape, f32),
            pltpu.VMEM((blocks, 3, seg), f32),
            pltpu.VMEM((peers * 16, seg), f32),
            pltpu.VMEM((seg, seg), f32),
            pltpu.VMEM((8, seg, 3 * seg), bf16),
            pltpu.SemaphoreType.DMA((3,)),
        ],
        compiler_params=pltpu.CompilerParams(vmem_limit_bytes=FULL_VMEM),
    )(pair_a, pair_slot, own, recv, live, lim)


def seg_call(send, back, seg_node, inner, shared):
    high = inner.shape[0] // 3
    count = shared.shape[1]
    return pl.pallas_call(
        seg_body,
        out_shape=(struct(3 * high, LOW), struct(3, count), struct(3, count), struct(1, 128)),
        in_specs=vmem(5),
        out_specs=tuple(vmem(4)),
        scratch_shapes=[
            pltpu.VMEM((3, seg_node.shape[0], 128), f32),
            pltpu.VMEM((PIECES * 3 * high, LOW), bf16),
            pltpu.VMEM((PIECES * 3 * high, LOW), f32),
            pltpu.VMEM((16, 1024), f32),
        ],
        compiler_params=pltpu.CompilerParams(vmem_limit_bytes=SMALL_VMEM),
    )(send, back.reshape(-1, 128), seg_node, inner, shared)


def last_call(lim, total, shared, lower, upper, vel, disp, inv):
    high = inv.shape[0]
    nodes = struct(3, high * LOW)
    return pl.pallas_call(
        last_body,
        out_shape=(nodes, nodes),
        in_specs=vmem(8),
        out_specs=tuple(vmem(2)),
        scratch_shapes=[pltpu.VMEM((4, 16, 1024), f32)],
        compiler_params=pltpu.CompilerParams(vmem_limit_bytes=SMALL_VMEM),
    )(lim, total, shared, lower, upper, vel, disp, inv)


def shifted(value, axis, steps):
    count = lax.axis_size(axis)
    first, last = (max(0, -steps), min(count, count - steps))
    return lax.ppermute(value, axis, [(source, source + steps) for source in range(first, last)])


def shards(
    ref_pos,
    displacement,
    velocity,
    node_mass,
    elem_nodes,
    elem_part,
    elem_scale,
    part_stiff,
    shared,
    seg_node,
    seg_mask,
    send_blk,
    pair_a,
    pair_slot,
    pair_mask,
):
    peers = lax.axis_size("grp") * lax.axis_size("dev")
    mass = node_mass.reshape(1, -1)
    send = send_blk.transpose(2, 0, 1)
    own, outgoing = send_call(send, displacement, ref_pos, seg_node, seg_mask, peers)
    arrived = lax.all_to_all(outgoing, ("grp", "dev"), split_axis=0, concat_axis=0, tiled=True)
    first = (lax.axis_index(("grp", "dev")) * part_stiff.shape[0]).reshape(1)
    force, limit = force_call(
        first,
        part_stiff,
        displacement,
        mass,
        elem_nodes,
        elem_part.reshape(1, -1),
        elem_scale.reshape(1, -1),
    )
    own_force, far_force = contact_call(
        pair_a,
        pair_slot,
        own,
        arrived.reshape(-1, 4, own.shape[2]),
        pair_mask.reshape(-1, 128),
        limit,
        peers,
    )
    back = lax.all_to_all(
        far_force.reshape(peers, 16, -1), ("grp", "dev"), split_axis=0, concat_axis=0, tiled=True
    )
    inner, vel, disp, inv = scatter_call(
        elem_nodes, force, seg_node, own_force, velocity, displacement, mass
    )
    total, low_rows, up_rows, limits = seg_call(send, back, seg_node, inner, shared)
    from_lower = shifted(up_rows, "dev", 1)
    from_upper = shifted(low_rows, "dev", -1)
    return last_call(limits, total, shared, from_lower, from_upper, vel, disp, inv)


def solution(mesh):
    both = ("grp", "dev")
    return jax.shard_map(
        shards,
        mesh=mesh,
        in_specs=(
            P(None, both),
            P(None, both),
            P(None, both),
            P(both),
            P(None, both),
            P(both),
            P(both),
            P(both),
            P(None, both),
            P(both, None),
            P(both, None),
            P(both, None, None),
            P(both),
            P(both),
            P(both),
        ),
        out_specs=(P(None, both), P(None, both)),
        check_vma=False,
    )
```

```python
import math
from functools import partial

import jax
import jax.numpy as jnp
from jax import lax
from jax.experimental import pallas as pl
from jax.experimental.pallas import tpu as pltpu
from jax.sharding import PartitionSpec as P

SPRINGS = ((0, 1, 1.0), (1, 2, 1.0), (2, 3, 1.0), (3, 0, 1.0), (0, 2, 0.5), (1, 3, 0.5))
COURANT = 0.5
LOW = 256
PIECES = 3
FULL_VMEM = 64 << 20
SMALL_VMEM = 16 << 20
WIDTH = 256
SCALE = math.sqrt(math.log2(math.e))
PARK = 1.0e3
f32 = jnp.float32
bf16 = jnp.bfloat16


def pieces_of(x, count=PIECES):
    out = []
    for _ in range(count):
        head = x.astype(bf16)
        out.append(head)
        x = x - head.astype(f32)
    return out


def low_hot(idx):
    low = jnp.broadcast_to((idx & (LOW - 1)).astype(f32), (16, idx.shape[1])).astype(bf16)
    line = lax.broadcasted_iota(jnp.int32, low.shape, 0).astype(f32).astype(bf16)
    one, zero = jnp.ones(low.shape, bf16), jnp.zeros(low.shape, bf16)
    return jnp.concatenate(
        [jnp.where(low == line + float(16 * k), one, zero) for k in range(LOW // 16)], 0
    )


def high_mask(idx, high):
    rows = lax.broadcasted_iota(jnp.int32, (high, idx.shape[1]), 0)
    return rows == (idx >> 8)


def fill_table(tab, at, ref, row, high):
    for h in range(high):
        tab[at + h : at + h + 1, :] = ref[row : row + 1, h * LOW : (h + 1) * LOW]


def split_table(cut, tab):
    rows = tab.shape[0]
    for p, piece in enumerate(pieces_of(tab[...])):
        cut[p * rows : (p + 1) * rows, :] = piece


def pick(cut, hot, mask, comps, high):
    found = jnp.dot(cut[...], hot, preferred_element_type=f32)
    rows = comps * high
    found = (found[:rows] + found[rows : 2 * rows]) + found[2 * rows :]
    return [
        jnp.sum(jnp.where(mask, found[c * high : (c + 1) * high], 0.0), 0, keepdims=True)
        for c in range(comps)
    ]


def cut_rows(force):
    return jnp.concatenate([piece.astype(f32) for piece in pieces_of(force)], 0)


def spread(ref, idx, high):
    mask = high_mask(idx, high)
    return jnp.concatenate(
        [jnp.where(mask, ref[r : r + 1, :], 0.0).astype(bf16) for r in range(3 * PIECES)], 0
    )


def add_hot(left, hot):
    return lax.dot_general(left, hot, (((1,), (1,)), ((), ())), preferred_element_type=f32)


def send_body(send_ref, disp_ref, ref_ref, seg_ref, mask_ref, own_ref, out_ref, tab, cut):
    high = disp_ref.shape[1] // LOW
    blocks = seg_ref.shape[0]
    for c in range(3):
        fill_table(tab, c * high, disp_ref, c, high)
    for c in range(3):
        for h in range(high):
            at = c * high + h
            tab[at : at + 1, :] += ref_ref[c : c + 1, h * LOW : (h + 1) * LOW]
    split_table(cut, tab)
    group = 8

    def some(g, carry):
        base = pl.multiple_of(g * group, group)
        seg = seg_ref[pl.ds(base, group), :]
        idx = jnp.concatenate([seg[k : k + 1] for k in range(group)], 1)
        xyz = pick(cut, low_hot(idx), high_mask(idx, high), 3, high)
        weight = mask_ref[pl.ds(base, group), :].astype(f32)
        for k in range(group):
            for c in range(3):
                own_ref[base + k, c : c + 1, :] = xyz[c][:, k * 128 : (k + 1) * 128]
            own_ref[base + k, 3:4, :] = weight[k : k + 1]
        return carry

    lax.fori_loop(0, blocks // group, some, 0, unroll=4)
    peers, cap = out_ref.shape[0], out_ref.shape[1]

    def send(d, carry):
        for c in range(cap):
            out_ref[d, c] = own_ref[send_ref[c, 0, d]]
        return carry

    lax.fori_loop(0, peers, send, 0, unroll=4)


def force_body(
    first_ref, stiff_ref, disp_ref, mass_ref, nodes_ref, part_ref, scale_ref, force_ref, lim_ref, tab, cut
):
    high = disp_ref.shape[1] // LOW
    width = WIDTH
    parts = stiff_ref.shape[0]
    for c in range(3):
        fill_table(tab, c * high, disp_ref, c, high)
    fill_table(tab, 3 * high, mass_ref, 0, high)
    split_table(cut, tab)

    def some(g, limit):
        at = pl.ds(pl.multiple_of(g * width, width), width)
        part = part_ref[:, at] - first_ref[0]
        stiff = jnp.zeros(part.shape, f32)
        for k in range(parts):
            stiff = jnp.where(part == k, stiff_ref[k], stiff)
        stiff = stiff * scale_ref[:, at]
        nodes = nodes_ref[:, at]
        idx = jnp.concatenate([nodes[k : k + 1] for k in range(4)], 1)
        found = pick(cut, low_hot(idx), high_mask(idx, high), 4, high)
        corner = [[found[c][:, k * width : (k + 1) * width] for c in range(4)] for k in range(4)]
        mass = jnp.minimum(
            jnp.minimum(corner[0][3], corner[1][3]), jnp.minimum(corner[2][3], corner[3][3])
        )
        force = [[jnp.zeros((1, width), f32)] * 3 for _ in range(4)]
        for head, tail, weight in SPRINGS:
            pull = weight * stiff
            for c in range(3):
                term = pull * (corner[tail][c] - corner[head][c])
                force[head][c] = force[head][c] + term
                force[tail][c] = force[tail][c] - term
        joined = [jnp.concatenate([force[k][c] for k in range(4)], 1) for c in range(3)]
        force_ref[g, 0:9] = cut_rows(jnp.concatenate(joined, 0))
        return jnp.minimum(limit, COURANT * jnp.sqrt(mass / stiff))

    limit = lax.fori_loop(
        0, nodes_ref.shape[1] // width, some, jnp.full((1, width), jnp.inf, f32), unroll=4
    )
    lim_ref[...] = jnp.broadcast_to(jnp.min(limit, 1, keepdims=True), lim_ref.shape)


def scatter_body(
    nodes_ref, force_ref, seg_ref, own, vel_ref, disp_ref, mass_ref, tot_ref, vel_out, disp_out, inv_out, acc, cut
):
    high = tot_ref.shape[0] // 3
    for c in range(3):
        fill_table(vel_out, c * high, vel_ref, c, high)
        fill_table(disp_out, c * high, disp_ref, c, high)
    fill_table(inv_out, 0, mass_ref, 0, high)
    inv_out[...] = 1.0 / inv_out[...]
    acc[...] = jnp.zeros_like(acc)

    def some(g, carry):
        at = pl.ds(pl.multiple_of(g * WIDTH, WIDTH), WIDTH)
        nodes = nodes_ref[:, at]
        idx = jnp.concatenate([nodes[k : k + 1] for k in range(4)], 1)
        acc[...] += add_hot(spread(force_ref.at[g], idx, high), low_hot(idx))
        return carry

    lax.fori_loop(0, force_ref.shape[0], some, 0, unroll=4)
    group = 8

    def more(g, carry):
        base = pl.multiple_of(g * group, group)
        seg = seg_ref[pl.ds(base, group), :]
        idx = jnp.concatenate([seg[k : k + 1] for k in range(group)], 1)
        cut[0:9] = cut_rows(jnp.concatenate([own[base + k] for k in range(group)], 1))
        acc[...] += add_hot(spread(cut, idx, high), low_hot(idx))
        return carry

    lax.fori_loop(0, seg_ref.shape[0] // group, more, 0, unroll=4)
    rows = 3 * high
    tot_ref[...] = (acc[2 * rows :] + acc[rows : 2 * rows]) + acc[:rows]


def contact_body(
    near_ref, far_ref, own_ref, recv_ref, live_ref, lim_ref, own_out, far_out, wide, total_a, total_b, recoils, landed, near, far, rows, chosen, sems
):
    blocks = total_a.shape[0]
    slots = landed.shape[0]
    seg = landed.shape[2]
    cap = 5
    fetch = pltpu.make_async_copy(recv_ref, landed, sems.at[0])
    fetch.start()

    group = 8
    line = lax.broadcasted_iota(jnp.int32, (16, 3 * seg), 0)
    part = lax.broadcasted_iota(jnp.int32, (16, 3 * seg), 1) >> 7
    hit = (line == part) | (line == part + 3) | (line == part + 6)
    hit = jnp.where(hit, 1.0, 0.0).astype(bf16)
    chosen[...] = jnp.zeros_like(chosen)
    for k in range(group):
        chosen[k, 16 * k : 16 * k + 16, :] = hit
    rows[...] = jnp.zeros_like(rows)

    def widen(g, carry):
        for k in range(group):
            block = own_ref[g * group + k]
            x = jnp.where(block[3:4] > 0.5, block[0:1] * SCALE, PARK)
            xyz = jnp.concatenate([x, block[1:3] * SCALE], 0)
            for p, piece in enumerate(pieces_of(xyz)):
                rows[16 * k + 3 * p : 16 * k + 3 * p + 3, :] = piece.astype(f32)
        columns = rows[...].T.astype(bf16)
        for k in range(group):
            out = jnp.dot(columns, chosen[k], preferred_element_type=f32)
            for c in range(3):
                wide[g * group + k, c] = out[:, c * seg : (c + 1) * seg]
                total_a[g * group + k, c] = jnp.zeros((seg, seg), f32)
                total_b[g * group + k, c] = jnp.zeros((seg, seg), f32)
        return carry

    lax.fori_loop(0, blocks // group, widen, 0, unroll=4)
    recoils[...] = jnp.zeros_like(recoils)
    live = jnp.sum(live_ref[...])
    fetch.wait()

    def pair(p, total):
        b = near_ref[p]
        s = far_ref[p]
        there = [jnp.broadcast_to(landed[s, c : c + 1, :], (8, seg)) for c in range(4)]
        x = jnp.where(there[3] > 0.5, there[0] * SCALE, -PARK)
        there = [x, there[1] * SCALE, there[2] * SCALE]
        recoil = [None] * 3
        for v in range(seg // 8):
            at = pl.ds(v * 8, 8)
            gap = [wide[b, c, at, :] - there[c] for c in range(3)]
            square = gap[0] * gap[0] + gap[1] * gap[1] + gap[2] * gap[2]
            weight = jnp.exp2(-square)
            for c in range(3):
                push = weight * gap[c]
                total[b, c, at, :] += push
                recoil[c] = push if recoil[c] is None else recoil[c] + push
        for c in range(3):
            recoils[c, pl.ds(pl.multiple_of(s * 8, 8), 8), :] += recoil[c]

    def four(q, carry):
        pair(8 * q, total_a)
        pair(8 * q + 1, total_b)
        pair(8 * q + 2, total_a)
        pair(8 * q + 3, total_b)
        pair(8 * q + 4, total_a)
        pair(8 * q + 5, total_b)
        pair(8 * q + 6, total_a)
        pair(8 * q + 7, total_b)
        return carry

    def one(p, carry):
        pair(p, total_a)
        return carry

    whole = live >> 3
    lax.fori_loop(0, whole, four, 0)
    lax.fori_loop(8 * whole, live, one, 0)
    peers = slots // cap
    stamp = jnp.broadcast_to(lim_ref[...], (8, seg))

    def finish(g, carry):
        for k in range(cap):
            for c in range(3):
                at = g * (64 * cap) + k * 8
                rows = [recoils[c, pl.ds(at + r, 8, stride=8 * cap), :] for r in range(8)]
                while len(rows) > 1:
                    rows = [x + y for x, y in zip(rows[::2], rows[1::2])]
                far[pl.ds(g * 128 + 3 * k + c, 8, stride=16), :] = rows[0] * (-1.0 / SCALE)
        far[pl.ds(g * 128 + 15, 8, stride=16), :] = stamp
        return carry

    lax.fori_loop(0, peers // 8, finish, 0, unroll=4)
    give_far = pltpu.make_async_copy(far, far_out, sems.at[1])
    give_far.start()

    def close(b, carry):
        total = total_a[b, 0] + total_b[b, 0]
        summed = lax.dot_general(
            jnp.ones((16, 3 * seg), bf16),
            jnp.concatenate(pieces_of(total), 1),
            (((1,), (1,)), ((), ())),
            preferred_element_type=f32,
        )
        near[b, 0:1, :] = summed[0:1] * (1.0 / SCALE)
        for c in (1, 2):
            total = total_a[b, c] + total_b[b, c]
            near[b, c : c + 1, :] = jnp.sum(total.T, 0, keepdims=True) * (1.0 / SCALE)
        return carry

    lax.fori_loop(0, blocks, close, 0, unroll=16)
    give_near = pltpu.make_async_copy(near, own_out, sems.at[2])
    give_near.start()
    give_far.wait()
    give_near.wait()


def seg_body(
    send_ref, back_ref, seg_ref, int_ref, share_ref, tot_ref, low_ref, up_ref, lim_ref, sums, cut, acc, rows
):
    blocks = seg_ref.shape[0]
    peers = back_ref.shape[0] // 16
    cap = 5
    high = int_ref.shape[0] // 3
    line = lax.broadcasted_iota(jnp.int32, (blocks, peers), 0)
    hot = jnp.concatenate(
        [jnp.where(line == send_ref[c], 1.0, 0.0).astype(bf16) for c in range(cap)], 1
    )
    for k in range(3):
        force = jnp.concatenate(
            [back_ref[pl.ds(3 * c + k, peers, stride=16), :] for c in range(cap)], 0
        )
        found = jnp.dot(hot, jnp.concatenate(pieces_of(force), 1), preferred_element_type=f32)
        sums[k] = (found[:, 256:] + found[:, 128:256]) + found[:, :128]
    acc[...] = jnp.zeros_like(acc)
    group = 8

    def some(g, carry):
        base = pl.multiple_of(g * group, group)
        seg = seg_ref[pl.ds(base, group), :]
        idx = jnp.concatenate([seg[k : k + 1] for k in range(group)], 1)
        force = [sums[c, pl.ds(base, group), :] for c in range(3)]
        force = [jnp.concatenate([f[k : k + 1] for k in range(group)], 1) for f in force]
        rows[0:9] = cut_rows(jnp.concatenate(force, 0))
        acc[...] += add_hot(spread(rows, idx, high), low_hot(idx))
        return carry

    lax.fori_loop(0, blocks // group, some, 0, unroll=4)
    size = 3 * high
    tot_ref[...] = ((acc[2 * size :] + acc[size : 2 * size]) + acc[:size]) + int_ref[...]
    split_table(cut, tot_ref)
    count = share_ref.shape[1]
    for row, out in ((0, low_ref), (1, up_ref)):
        for at in range(0, count, 1024):
            idx = share_ref[row : row + 1, at : at + 1024]
            picked = pick(cut, low_hot(idx), high_mask(idx, high), 3, high)
            for c in range(3):
                out[c : c + 1, at : at + 1024] = picked[c]
    lim = jnp.min(back_ref[pl.ds(15, peers, stride=16), :], 0, keepdims=True)
    lim_ref[...] = lim


def last_body(
    lim_ref, tot_ref, share_ref, low_ref, up_ref, vel_ref, disp_ref, inv_ref, new_disp, new_vel, cut
):
    high = tot_ref.shape[0] // 3
    count = share_ref.shape[1]
    total = jnp.zeros((PIECES * 3 * high, LOW), f32)
    for row, src in ((0, low_ref), (1, up_ref)):
        for k, at in enumerate(range(0, count, 1024)):
            idx = share_ref[row : row + 1, at : at + 1024]
            rows = cut.at[2 * row + k]
            rows[0:9] = cut_rows(src[:, at : at + 1024])
            total = total + add_hot(spread(rows, idx, high), low_hot(idx))
    size = 3 * high
    force = ((total[2 * size :] + total[size : 2 * size]) + total[:size]) + tot_ref[...]
    step = jnp.min(lim_ref[...], 1, keepdims=True)
    for c in range(3):
        at = slice(c * high, (c + 1) * high)
        vel = vel_ref[at] + step * (force[at] * inv_ref[...])
        disp = disp_ref[at] + step * vel
        for h in range(high):
            new_vel[c : c + 1, h * LOW : (h + 1) * LOW] = vel[h : h + 1]
            new_disp[c : c + 1, h * LOW : (h + 1) * LOW] = disp[h : h + 1]


def vmem(count):
    return [pl.BlockSpec(memory_space=pltpu.VMEM)] * count


def hbm(count):
    return [pl.BlockSpec(memory_space=pltpu.HBM)] * count


def smem(count):
    return [pl.BlockSpec(memory_space=pltpu.SMEM)] * count


def struct(*shape):
    return jax.ShapeDtypeStruct(shape, f32)


def send_call(send, disp, ref_pos, seg_node, seg_mask, peers):
    high = disp.shape[1] // LOW
    blocks, seg = seg_node.shape
    return pl.pallas_call(
        send_body,
        out_shape=(struct(blocks, 4, seg), struct(peers, send.shape[0], 4, seg)),
        in_specs=smem(1) + vmem(4),
        out_specs=tuple(vmem(2)),
        scratch_shapes=[
            pltpu.VMEM((3 * high, LOW), f32),
            pltpu.VMEM((PIECES * 3 * high, LOW), bf16),
        ],
    )(send, disp, ref_pos, seg_node, seg_mask)


def force_call(first, stiff, disp, mass, nodes, part, scale):
    high = disp.shape[1] // LOW
    return pl.pallas_call(
        force_body,
        out_shape=(struct(nodes.shape[1] // WIDTH, 16, 4 * WIDTH), struct(1, 128)),
        in_specs=smem(2) + vmem(5),
        out_specs=tuple(vmem(2)),
        scratch_shapes=[
            pltpu.VMEM((4 * high, LOW), f32),
            pltpu.VMEM((PIECES * 4 * high, LOW), bf16),
        ],
        compiler_params=pltpu.CompilerParams(vmem_limit_bytes=FULL_VMEM),
    )(first, stiff, disp, mass, nodes, part, scale)


def scatter_call(nodes, force, seg_node, own, vel, disp, mass):
    high = nodes.shape[1] // LOW
    return pl.pallas_call(
        scatter_body,
        out_shape=(struct(3 * high, LOW), struct(3 * high, LOW), struct(3 * high, LOW), struct(high, LOW)),
        in_specs=vmem(7),
        out_specs=tuple(vmem(4)),
        scratch_shapes=[
            pltpu.VMEM((PIECES * 3 * high, LOW), f32),
            pltpu.VMEM((16, 1024), f32),
        ],
        compiler_params=pltpu.CompilerParams(vmem_limit_bytes=SMALL_VMEM),
    )(nodes, force, seg_node, own, vel, disp, mass)


def contact_call(pair_a, pair_slot, own, recv, live, lim, peers):
    blocks, _, seg = own.shape
    slots = recv.shape[0]
    return pl.pallas_call(
        contact_body,
        out_shape=(struct(blocks, 3, seg), struct(peers * 16, seg)),
        in_specs=smem(2) + vmem(1) + hbm(1) + vmem(2),
        out_specs=tuple(hbm(2)),
        scratch_shapes=[
            pltpu.VMEM((blocks, 3, seg, seg), f32),
            pltpu.VMEM((blocks, 3, seg, seg), f32),
            pltpu.VMEM((blocks, 3, seg, seg), f32),
            pltpu.VMEM((3, slots * 8, seg), f32),
            pltpu.VMEM(recv.shape, f32),
            pltpu.VMEM((blocks, 3, seg), f32),
            pltpu.VMEM((peers * 16, seg), f32),
            pltpu.VMEM((seg, seg), f32),
            pltpu.VMEM((8, seg, 3 * seg), bf16),
            pltpu.SemaphoreType.DMA((3,)),
        ],
        compiler_params=pltpu.CompilerParams(vmem_limit_bytes=FULL_VMEM),
    )(pair_a, pair_slot, own, recv, live, lim)


def seg_call(send, back, seg_node, inner, shared):
    high = inner.shape[0] // 3
    count = shared.shape[1]
    return pl.pallas_call(
        seg_body,
        out_shape=(struct(3 * high, LOW), struct(3, count), struct(3, count), struct(1, 128)),
        in_specs=vmem(5),
        out_specs=tuple(vmem(4)),
        scratch_shapes=[
            pltpu.VMEM((3, seg_node.shape[0], 128), f32),
            pltpu.VMEM((PIECES * 3 * high, LOW), bf16),
            pltpu.VMEM((PIECES * 3 * high, LOW), f32),
            pltpu.VMEM((16, 1024), f32),
        ],
        compiler_params=pltpu.CompilerParams(vmem_limit_bytes=SMALL_VMEM),
    )(send, back.reshape(-1, 128), seg_node, inner, shared)


def last_call(lim, total, shared, lower, upper, vel, disp, inv):
    high = inv.shape[0]
    nodes = struct(3, high * LOW)
    return pl.pallas_call(
        last_body,
        out_shape=(nodes, nodes),
        in_specs=vmem(8),
        out_specs=tuple(vmem(2)),
        scratch_shapes=[pltpu.VMEM((4, 16, 1024), f32)],
        compiler_params=pltpu.CompilerParams(vmem_limit_bytes=SMALL_VMEM),
    )(lim, total, shared, lower, upper, vel, disp, inv)


def shifted(value, axis, steps):
    count = lax.axis_size(axis)
    first, last = (max(0, -steps), min(count, count - steps))
    return lax.ppermute(value, axis, [(source, source + steps) for source in range(first, last)])


def shards(
    ref_pos,
    displacement,
    velocity,
    node_mass,
    elem_nodes,
    elem_part,
    elem_scale,
    part_stiff,
    shared,
    seg_node,
    seg_mask,
    send_blk,
    pair_a,
    pair_slot,
    pair_mask,
):
    peers = lax.axis_size("grp") * lax.axis_size("dev")
    mass = node_mass.reshape(1, -1)
    send = send_blk.transpose(2, 0, 1)
    own, outgoing = send_call(send, displacement, ref_pos, seg_node, seg_mask, peers)
    arrived = lax.all_to_all(outgoing, ("grp", "dev"), split_axis=0, concat_axis=0, tiled=True)
    first = (lax.axis_index(("grp", "dev")) * part_stiff.shape[0]).reshape(1)
    force, limit = force_call(
        first,
        part_stiff,
        displacement,
        mass,
        elem_nodes,
        elem_part.reshape(1, -1),
        elem_scale.reshape(1, -1),
    )
    own_force, far_force = contact_call(
        pair_a,
        pair_slot,
        own,
        arrived.reshape(-1, 4, own.shape[2]),
        pair_mask.reshape(-1, 128),
        limit,
        peers,
    )
    back = lax.all_to_all(
        far_force.reshape(peers, 16, -1), ("grp", "dev"), split_axis=0, concat_axis=0, tiled=True
    )
    inner, vel, disp, inv = scatter_call(
        elem_nodes, force, seg_node, own_force, velocity, displacement, mass
    )
    total, low_rows, up_rows, limits = seg_call(send, back, seg_node, inner, shared)
    from_lower = shifted(up_rows, "dev", 1)
    from_upper = shifted(low_rows, "dev", -1)
    return last_call(limits, total, shared, from_lower, from_upper, vel, disp, inv)


def solution(mesh):
    both = ("grp", "dev")
    return jax.shard_map(
        shards,
        mesh=mesh,
        in_specs=(
            P(None, both),
            P(None, both),
            P(None, both),
            P(both),
            P(None, both),
            P(both),
            P(both),
            P(both),
            P(None, both),
            P(both, None),
            P(both, None),
            P(both, None, None),
            P(both),
            P(both),
            P(both),
        ),
        out_specs=(P(None, both), P(None, both)),
        check_vma=False,
    )
```

```python
import math
from functools import partial

import jax
import jax.numpy as jnp
from jax import lax
from jax.experimental import pallas as pl
from jax.experimental.pallas import tpu as pltpu
from jax.sharding import PartitionSpec as P

SPRINGS = ((0, 1, 1.0), (1, 2, 1.0), (2, 3, 1.0), (3, 0, 1.0), (0, 2, 0.5), (1, 3, 0.5))
COURANT = 0.5
LOW = 256
PIECES = 3
FULL_VMEM = 64 << 20
SMALL_VMEM = 16 << 20
WIDTH = 256
SCALE = math.sqrt(math.log2(math.e))
PARK = 1.0e3
f32 = jnp.float32
bf16 = jnp.bfloat16


def pieces_of(x, count=PIECES):
    out = []
    for _ in range(count):
        head = x.astype(bf16)
        out.append(head)
        x = x - head.astype(f32)
    return out


def low_hot(idx):
    low = jnp.broadcast_to((idx & (LOW - 1)).astype(f32), (16, idx.shape[1])).astype(bf16)
    line = lax.broadcasted_iota(jnp.int32, low.shape, 0).astype(f32).astype(bf16)
    one, zero = jnp.ones(low.shape, bf16), jnp.zeros(low.shape, bf16)
    return jnp.concatenate(
        [jnp.where(low == line + float(16 * k), one, zero) for k in range(LOW // 16)], 0
    )


def high_mask(idx, high):
    rows = lax.broadcasted_iota(jnp.int32, (high, idx.shape[1]), 0)
    return rows == (idx >> 8)


def fill_table(tab, at, ref, row, high):
    for h in range(high):
        tab[at + h : at + h + 1, :] = ref[row : row + 1, h * LOW : (h + 1) * LOW]


def split_table(cut, tab):
    rows = tab.shape[0]
    for p, piece in enumerate(pieces_of(tab[...])):
        cut[p * rows : (p + 1) * rows, :] = piece


def pick(cut, hot, mask, comps, high):
    found = jnp.dot(cut[...], hot, preferred_element_type=f32)
    rows = comps * high
    found = (found[:rows] + found[rows : 2 * rows]) + found[2 * rows :]
    return [
        jnp.sum(jnp.where(mask, found[c * high : (c + 1) * high], 0.0), 0, keepdims=True)
        for c in range(comps)
    ]


def cut_rows(force):
    return jnp.concatenate([piece.astype(f32) for piece in pieces_of(force)], 0)


def spread(ref, idx, high):
    mask = high_mask(idx, high)
    return jnp.concatenate(
        [jnp.where(mask, ref[r : r + 1, :], 0.0).astype(bf16) for r in range(3 * PIECES)], 0
    )


def add_hot(left, hot):
    return lax.dot_general(left, hot, (((1,), (1,)), ((), ())), preferred_element_type=f32)


def send_body(send_ref, disp_ref, ref_ref, seg_ref, mask_ref, own_ref, out_ref, tab, cut):
    high = disp_ref.shape[1] // LOW
    blocks = seg_ref.shape[0]
    for c in range(3):
        fill_table(tab, c * high, disp_ref, c, high)
    for c in range(3):
        for h in range(high):
            at = c * high + h
            tab[at : at + 1, :] += ref_ref[c : c + 1, h * LOW : (h + 1) * LOW]
    split_table(cut, tab)
    group = 8

    def some(g, carry):
        base = pl.multiple_of(g * group, group)
        seg = seg_ref[pl.ds(base, group), :]
        idx = jnp.concatenate([seg[k : k + 1] for k in range(group)], 1)
        xyz = pick(cut, low_hot(idx), high_mask(idx, high), 3, high)
        weight = mask_ref[pl.ds(base, group), :].astype(f32)
        for k in range(group):
            for c in range(3):
                own_ref[base + k, c : c + 1, :] = xyz[c][:, k * 128 : (k + 1) * 128]
            own_ref[base + k, 3:4, :] = weight[k : k + 1]
        return carry

    lax.fori_loop(0, blocks // group, some, 0, unroll=8)
    peers, cap = out_ref.shape[0], out_ref.shape[1]

    def send(d, carry):
        for c in range(cap):
            out_ref[d, c] = own_ref[send_ref[c, 0, d]]
        return carry

    lax.fori_loop(0, peers, send, 0, unroll=8)


def force_body(
    first_ref, stiff_ref, disp_ref, mass_ref, nodes_ref, part_ref, scale_ref, force_ref, lim_ref, tab, cut
):
    high = disp_ref.shape[1] // LOW
    width = WIDTH
    parts = stiff_ref.shape[0]
    for c in range(3):
        fill_table(tab, c * high, disp_ref, c, high)
    fill_table(tab, 3 * high, mass_ref, 0, high)
    split_table(cut, tab)

    def some(g, limit):
        at = pl.ds(pl.multiple_of(g * width, width), width)
        part = part_ref[:, at] - first_ref[0]
        stiff = jnp.zeros(part.shape, f32)
        for k in range(parts):
            stiff = jnp.where(part == k, stiff_ref[k], stiff)
        stiff = stiff * scale_ref[:, at]
        nodes = nodes_ref[:, at]
        idx = jnp.concatenate([nodes[k : k + 1] for k in range(4)], 1)
        found = pick(cut, low_hot(idx), high_mask(idx, high), 4, high)
        corner = [[found[c][:, k * width : (k + 1) * width] for c in range(4)] for k in range(4)]
        mass = jnp.minimum(
            jnp.minimum(corner[0][3], corner[1][3]), jnp.minimum(corner[2][3], corner[3][3])
        )
        force = [[jnp.zeros((1, width), f32)] * 3 for _ in range(4)]
        for head, tail, weight in SPRINGS:
            pull = weight * stiff
            for c in range(3):
                term = pull * (corner[tail][c] - corner[head][c])
                force[head][c] = force[head][c] + term
                force[tail][c] = force[tail][c] - term
        joined = [jnp.concatenate([force[k][c] for k in range(4)], 1) for c in range(3)]
        force_ref[g, 0:9] = cut_rows(jnp.concatenate(joined, 0))
        return jnp.minimum(limit, COURANT * jnp.sqrt(mass / stiff))

    limit = lax.fori_loop(
        0, nodes_ref.shape[1] // width, some, jnp.full((1, width), jnp.inf, f32), unroll=4
    )
    lim_ref[...] = jnp.broadcast_to(jnp.min(limit, 1, keepdims=True), lim_ref.shape)


def scatter_body(
    nodes_ref, force_ref, seg_ref, own, vel_ref, disp_ref, mass_ref, tot_ref, vel_out, disp_out, inv_out, acc, cut
):
    high = tot_ref.shape[0] // 3
    for c in range(3):
        fill_table(vel_out, c * high, vel_ref, c, high)
        fill_table(disp_out, c * high, disp_ref, c, high)
    fill_table(inv_out, 0, mass_ref, 0, high)
    inv_out[...] = 1.0 / inv_out[...]
    acc[...] = jnp.zeros_like(acc)

    def some(g, carry):
        at = pl.ds(pl.multiple_of(g * WIDTH, WIDTH), WIDTH)
        nodes = nodes_ref[:, at]
        idx = jnp.concatenate([nodes[k : k + 1] for k in range(4)], 1)
        acc[...] += add_hot(spread(force_ref.at[g], idx, high), low_hot(idx))
        return carry

    lax.fori_loop(0, force_ref.shape[0], some, 0, unroll=4)
    group = 8

    def more(g, carry):
        base = pl.multiple_of(g * group, group)
        seg = seg_ref[pl.ds(base, group), :]
        idx = jnp.concatenate([seg[k : k + 1] for k in range(group)], 1)
        cut[0:9] = cut_rows(jnp.concatenate([own[base + k] for k in range(group)], 1))
        acc[...] += add_hot(spread(cut, idx, high), low_hot(idx))
        return carry

    lax.fori_loop(0, seg_ref.shape[0] // group, more, 0, unroll=4)
    rows = 3 * high
    tot_ref[...] = (acc[2 * rows :] + acc[rows : 2 * rows]) + acc[:rows]


def contact_body(
    near_ref, far_ref, own_ref, recv_ref, live_ref, lim_ref, own_out, far_out, wide, total_a, total_b, recoils, landed, near, far, rows, chosen, sems
):
    blocks = total_a.shape[0]
    slots = landed.shape[0]
    seg = landed.shape[2]
    cap = 5
    fetch = pltpu.make_async_copy(recv_ref, landed, sems.at[0])
    fetch.start()

    group = 8
    line = lax.broadcasted_iota(jnp.int32, (16, 3 * seg), 0)
    part = lax.broadcasted_iota(jnp.int32, (16, 3 * seg), 1) >> 7
    hit = (line == part) | (line == part + 3) | (line == part + 6)
    hit = jnp.where(hit, 1.0, 0.0).astype(bf16)
    chosen[...] = jnp.zeros_like(chosen)
    for k in range(group):
        chosen[k, 16 * k : 16 * k + 16, :] = hit
    rows[...] = jnp.zeros_like(rows)

    def widen(g, carry):
        for k in range(group):
            block = own_ref[g * group + k]
            x = jnp.where(block[3:4] > 0.5, block[0:1] * SCALE, PARK)
            xyz = jnp.concatenate([x, block[1:3] * SCALE], 0)
            for p, piece in enumerate(pieces_of(xyz)):
                rows[16 * k + 3 * p : 16 * k + 3 * p + 3, :] = piece.astype(f32)
        columns = rows[...].T.astype(bf16)
        for k in range(group):
            out = jnp.dot(columns, chosen[k], preferred_element_type=f32)
            for c in range(3):
                wide[g * group + k, c] = out[:, c * seg : (c + 1) * seg]
                total_a[g * group + k, c] = jnp.zeros((seg, seg), f32)
                total_b[g * group + k, c] = jnp.zeros((seg, seg), f32)
        return carry

    lax.fori_loop(0, blocks // group, widen, 0, unroll=4)
    recoils[...] = jnp.zeros_like(recoils)
    live = jnp.sum(live_ref[...])
    fetch.wait()

    def pair(p, total):
        b = near_ref[p]
        s = far_ref[p]
        there = [jnp.broadcast_to(landed[s, c : c + 1, :], (8, seg)) for c in range(4)]
        x = jnp.where(there[3] > 0.5, there[0] * SCALE, -PARK)
        there = [x, there[1] * SCALE, there[2] * SCALE]
        recoil = [None] * 3
        for v in range(seg // 8):
            at = pl.ds(v * 8, 8)
            gap = [wide[b, c, at, :] - there[c] for c in range(3)]
            square = gap[0] * gap[0] + gap[1] * gap[1] + gap[2] * gap[2]
            weight = jnp.exp2(-square)
            for c in range(3):
                push = weight * gap[c]
                total[b, c, at, :] += push
                recoil[c] = push if recoil[c] is None else recoil[c] + push
        for c in range(3):
            recoils[c, pl.ds(pl.multiple_of(s * 8, 8), 8), :] += recoil[c]

    def four(q, carry):
        pair(8 * q, total_a)
        pair(8 * q + 1, total_b)
        pair(8 * q + 2, total_a)
        pair(8 * q + 3, total_b)
        pair(8 * q + 4, total_a)
        pair(8 * q + 5, total_b)
        pair(8 * q + 6, total_a)
        pair(8 * q + 7, total_b)
        return carry

    def one(p, carry):
        pair(p, total_a)
        return carry

    whole = live >> 3
    lax.fori_loop(0, whole, four, 0)
    lax.fori_loop(8 * whole, live, one, 0)
    peers = slots // cap
    stamp = jnp.broadcast_to(lim_ref[...], (8, seg))

    def finish(g, carry):
        for k in range(cap):
            for c in range(3):
                at = g * (64 * cap) + k * 8
                rows = [recoils[c, pl.ds(at + r, 8, stride=8 * cap), :] for r in range(8)]
                while len(rows) > 1:
                    rows = [x + y for x, y in zip(rows[::2], rows[1::2])]
                far[pl.ds(g * 128 + 3 * k + c, 8, stride=16), :] = rows[0] * (-1.0 / SCALE)
        far[pl.ds(g * 128 + 15, 8, stride=16), :] = stamp
        return carry

    lax.fori_loop(0, peers // 8, finish, 0, unroll=4)
    give_far = pltpu.make_async_copy(far, far_out, sems.at[1])
    give_far.start()

    def close(b, carry):
        total = total_a[b, 0] + total_b[b, 0]
        summed = lax.dot_general(
            jnp.ones((16, 3 * seg), bf16),
            jnp.concatenate(pieces_of(total), 1),
            (((1,), (1,)), ((), ())),
            preferred_element_type=f32,
        )
        near[b, 0:1, :] = summed[0:1] * (1.0 / SCALE)
        for c in (1, 2):
            total = total_a[b, c] + total_b[b, c]
            near[b, c : c + 1, :] = jnp.sum(total.T, 0, keepdims=True) * (1.0 / SCALE)
        return carry

    lax.fori_loop(0, blocks, close, 0, unroll=16)
    give_near = pltpu.make_async_copy(near, own_out, sems.at[2])
    give_near.start()
    give_far.wait()
    give_near.wait()


def seg_body(
    send_ref, back_ref, seg_ref, int_ref, share_ref, tot_ref, low_ref, up_ref, lim_ref, sums, cut, acc, rows
):
    blocks = seg_ref.shape[0]
    peers = back_ref.shape[0] // 16
    cap = 5
    high = int_ref.shape[0] // 3
    line = lax.broadcasted_iota(jnp.int32, (blocks, peers), 0)
    hot = jnp.concatenate(
        [jnp.where(line == send_ref[c], 1.0, 0.0).astype(bf16) for c in range(cap)], 1
    )
    for k in range(3):
        force = jnp.concatenate(
            [back_ref[pl.ds(3 * c + k, peers, stride=16), :] for c in range(cap)], 0
        )
        found = jnp.dot(hot, jnp.concatenate(pieces_of(force), 1), preferred_element_type=f32)
        sums[k] = (found[:, 256:] + found[:, 128:256]) + found[:, :128]
    acc[...] = jnp.zeros_like(acc)
    group = 8

    def some(g, carry):
        base = pl.multiple_of(g * group, group)
        seg = seg_ref[pl.ds(base, group), :]
        idx = jnp.concatenate([seg[k : k + 1] for k in range(group)], 1)
        force = [sums[c, pl.ds(base, group), :] for c in range(3)]
        force = [jnp.concatenate([f[k : k + 1] for k in range(group)], 1) for f in force]
        rows[0:9] = cut_rows(jnp.concatenate(force, 0))
        acc[...] += add_hot(spread(rows, idx, high), low_hot(idx))
        return carry

    lax.fori_loop(0, blocks // group, some, 0, unroll=8)
    size = 3 * high
    tot_ref[...] = ((acc[2 * size :] + acc[size : 2 * size]) + acc[:size]) + int_ref[...]
    split_table(cut, tot_ref)
    count = share_ref.shape[1]
    for row, out in ((0, low_ref), (1, up_ref)):
        for at in range(0, count, 1024):
            idx = share_ref[row : row + 1, at : at + 1024]
            picked = pick(cut, low_hot(idx), high_mask(idx, high), 3, high)
            for c in range(3):
                out[c : c + 1, at : at + 1024] = picked[c]
    lim = jnp.min(back_ref[pl.ds(15, peers, stride=16), :], 0, keepdims=True)
    lim_ref[...] = lim


def last_body(
    lim_ref, tot_ref, share_ref, low_ref, up_ref, vel_ref, disp_ref, inv_ref, new_disp, new_vel, cut
):
    high = tot_ref.shape[0] // 3
    count = share_ref.shape[1]
    total = jnp.zeros((PIECES * 3 * high, LOW), f32)
    for row, src in ((0, low_ref), (1, up_ref)):
        for k, at in enumerate(range(0, count, 1024)):
            idx = share_ref[row : row + 1, at : at + 1024]
            rows = cut.at[2 * row + k]
            rows[0:9] = cut_rows(src[:, at : at + 1024])
            total = total + add_hot(spread(rows, idx, high), low_hot(idx))
    size = 3 * high
    force = ((total[2 * size :] + total[size : 2 * size]) + total[:size]) + tot_ref[...]
    step = jnp.min(lim_ref[...], 1, keepdims=True)
    for c in range(3):
        at = slice(c * high, (c + 1) * high)
        vel = vel_ref[at] + step * (force[at] * inv_ref[...])
        disp = disp_ref[at] + step * vel
        for h in range(high):
            new_vel[c : c + 1, h * LOW : (h + 1) * LOW] = vel[h : h + 1]
            new_disp[c : c + 1, h * LOW : (h + 1) * LOW] = disp[h : h + 1]


def vmem(count):
    return [pl.BlockSpec(memory_space=pltpu.VMEM)] * count


def hbm(count):
    return [pl.BlockSpec(memory_space=pltpu.HBM)] * count


def smem(count):
    return [pl.BlockSpec(memory_space=pltpu.SMEM)] * count


def struct(*shape):
    return jax.ShapeDtypeStruct(shape, f32)


def send_call(send, disp, ref_pos, seg_node, seg_mask, peers):
    high = disp.shape[1] // LOW
    blocks, seg = seg_node.shape
    return pl.pallas_call(
        send_body,
        out_shape=(struct(blocks, 4, seg), struct(peers, send.shape[0], 4, seg)),
        in_specs=smem(1) + vmem(4),
        out_specs=tuple(vmem(2)),
        scratch_shapes=[
            pltpu.VMEM((3 * high, LOW), f32),
            pltpu.VMEM((PIECES * 3 * high, LOW), bf16),
        ],
    )(send, disp, ref_pos, seg_node, seg_mask)


def force_call(first, stiff, disp, mass, nodes, part, scale):
    high = disp.shape[1] // LOW
    return pl.pallas_call(
        force_body,
        out_shape=(struct(nodes.shape[1] // WIDTH, 16, 4 * WIDTH), struct(1, 128)),
        in_specs=smem(2) + vmem(5),
        out_specs=tuple(vmem(2)),
        scratch_shapes=[
            pltpu.VMEM((4 * high, LOW), f32),
            pltpu.VMEM((PIECES * 4 * high, LOW), bf16),
        ],
        compiler_params=pltpu.CompilerParams(vmem_limit_bytes=FULL_VMEM),
    )(first, stiff, disp, mass, nodes, part, scale)


def scatter_call(nodes, force, seg_node, own, vel, disp, mass):
    high = nodes.shape[1] // LOW
    return pl.pallas_call(
        scatter_body,
        out_shape=(struct(3 * high, LOW), struct(3 * high, LOW), struct(3 * high, LOW), struct(high, LOW)),
        in_specs=vmem(7),
        out_specs=tuple(vmem(4)),
        scratch_shapes=[
            pltpu.VMEM((PIECES * 3 * high, LOW), f32),
            pltpu.VMEM((16, 1024), f32),
        ],
        compiler_params=pltpu.CompilerParams(vmem_limit_bytes=SMALL_VMEM),
    )(nodes, force, seg_node, own, vel, disp, mass)


def contact_call(pair_a, pair_slot, own, recv, live, lim, peers):
    blocks, _, seg = own.shape
    slots = recv.shape[0]
    return pl.pallas_call(
        contact_body,
        out_shape=(struct(blocks, 3, seg), struct(peers * 16, seg)),
        in_specs=smem(2) + vmem(1) + hbm(1) + vmem(2),
        out_specs=tuple(hbm(2)),
        scratch_shapes=[
            pltpu.VMEM((blocks, 3, seg, seg), f32),
            pltpu.VMEM((blocks, 3, seg, seg), f32),
            pltpu.VMEM((blocks, 3, seg, seg), f32),
            pltpu.VMEM((3, slots * 8, seg), f32),
            pltpu.VMEM(recv.shape, f32),
            pltpu.VMEM((blocks, 3, seg), f32),
            pltpu.VMEM((peers * 16, seg), f32),
            pltpu.VMEM((seg, seg), f32),
            pltpu.VMEM((8, seg, 3 * seg), bf16),
            pltpu.SemaphoreType.DMA((3,)),
        ],
        compiler_params=pltpu.CompilerParams(vmem_limit_bytes=FULL_VMEM),
    )(pair_a, pair_slot, own, recv, live, lim)


def seg_call(send, back, seg_node, inner, shared):
    high = inner.shape[0] // 3
    count = shared.shape[1]
    return pl.pallas_call(
        seg_body,
        out_shape=(struct(3 * high, LOW), struct(3, count), struct(3, count), struct(1, 128)),
        in_specs=vmem(5),
        out_specs=tuple(vmem(4)),
        scratch_shapes=[
            pltpu.VMEM((3, seg_node.shape[0], 128), f32),
            pltpu.VMEM((PIECES * 3 * high, LOW), bf16),
            pltpu.VMEM((PIECES * 3 * high, LOW), f32),
            pltpu.VMEM((16, 1024), f32),
        ],
        compiler_params=pltpu.CompilerParams(vmem_limit_bytes=SMALL_VMEM),
    )(send, back.reshape(-1, 128), seg_node, inner, shared)


def last_call(lim, total, shared, lower, upper, vel, disp, inv):
    high = inv.shape[0]
    nodes = struct(3, high * LOW)
    return pl.pallas_call(
        last_body,
        out_shape=(nodes, nodes),
        in_specs=vmem(8),
        out_specs=tuple(vmem(2)),
        scratch_shapes=[pltpu.VMEM((4, 16, 1024), f32)],
        compiler_params=pltpu.CompilerParams(vmem_limit_bytes=SMALL_VMEM),
    )(lim, total, shared, lower, upper, vel, disp, inv)


def shifted(value, axis, steps):
    count = lax.axis_size(axis)
    first, last = (max(0, -steps), min(count, count - steps))
    return lax.ppermute(value, axis, [(source, source + steps) for source in range(first, last)])


def shards(
    ref_pos,
    displacement,
    velocity,
    node_mass,
    elem_nodes,
    elem_part,
    elem_scale,
    part_stiff,
    shared,
    seg_node,
    seg_mask,
    send_blk,
    pair_a,
    pair_slot,
    pair_mask,
):
    peers = lax.axis_size("grp") * lax.axis_size("dev")
    mass = node_mass.reshape(1, -1)
    send = send_blk.transpose(2, 0, 1)
    own, outgoing = send_call(send, displacement, ref_pos, seg_node, seg_mask, peers)
    arrived = lax.all_to_all(outgoing, ("grp", "dev"), split_axis=0, concat_axis=0, tiled=True)
    first = (lax.axis_index(("grp", "dev")) * part_stiff.shape[0]).reshape(1)
    force, limit = force_call(
        first,
        part_stiff,
        displacement,
        mass,
        elem_nodes,
        elem_part.reshape(1, -1),
        elem_scale.reshape(1, -1),
    )
    own_force, far_force = contact_call(
        pair_a,
        pair_slot,
        own,
        arrived.reshape(-1, 4, own.shape[2]),
        pair_mask.reshape(-1, 128),
        limit,
        peers,
    )
    back = lax.all_to_all(
        far_force.reshape(peers, 16, -1), ("grp", "dev"), split_axis=0, concat_axis=0, tiled=True
    )
    inner, vel, disp, inv = scatter_call(
        elem_nodes, force, seg_node, own_force, velocity, displacement, mass
    )
    total, low_rows, up_rows, limits = seg_call(send, back, seg_node, inner, shared)
    from_lower = shifted(up_rows, "dev", 1)
    from_upper = shifted(low_rows, "dev", -1)
    return last_call(limits, total, shared, from_lower, from_upper, vel, disp, inv)


def solution(mesh):
    both = ("grp", "dev")
    return jax.shard_map(
        shards,
        mesh=mesh,
        in_specs=(
            P(None, both),
            P(None, both),
            P(None, both),
            P(both),
            P(None, both),
            P(both),
            P(both),
            P(both),
            P(None, both),
            P(both, None),
            P(both, None),
            P(both, None, None),
            P(both),
            P(both),
            P(both),
        ),
        out_specs=(P(None, both), P(None, both)),
        check_vma=False,
    )
```

```python
import math
from functools import partial

import jax
import jax.numpy as jnp
from jax import lax
from jax.experimental import pallas as pl
from jax.experimental.pallas import tpu as pltpu
from jax.sharding import PartitionSpec as P

SPRINGS = ((0, 1, 1.0), (1, 2, 1.0), (2, 3, 1.0), (3, 0, 1.0), (0, 2, 0.5), (1, 3, 0.5))
COURANT = 0.5
LOW = 256
PIECES = 3
FULL_VMEM = 64 << 20
SMALL_VMEM = 16 << 20
WIDTH = 256
SCALE = math.sqrt(math.log2(math.e))
PARK = 1.0e3
f32 = jnp.float32
bf16 = jnp.bfloat16


def pieces_of(x, count=PIECES):
    out = []
    for _ in range(count):
        head = x.astype(bf16)
        out.append(head)
        x = x - head.astype(f32)
    return out


def low_hot(idx):
    low = jnp.broadcast_to((idx & (LOW - 1)).astype(f32), (16, idx.shape[1])).astype(bf16)
    line = lax.broadcasted_iota(jnp.int32, low.shape, 0).astype(f32).astype(bf16)
    one, zero = jnp.ones(low.shape, bf16), jnp.zeros(low.shape, bf16)
    return jnp.concatenate(
        [jnp.where(low == line + float(16 * k), one, zero) for k in range(LOW // 16)], 0
    )


def high_mask(idx, high):
    rows = lax.broadcasted_iota(jnp.int32, (high, idx.shape[1]), 0)
    return rows == (idx >> 8)


def fill_table(tab, at, ref, row, high):
    for h in range(high):
        tab[at + h : at + h + 1, :] = ref[row : row + 1, h * LOW : (h + 1) * LOW]


def split_table(cut, tab):
    rows = tab.shape[0]
    for p, piece in enumerate(pieces_of(tab[...])):
        cut[p * rows : (p + 1) * rows, :] = piece


def pick(cut, hot, mask, comps, high):
    found = jnp.dot(cut[...], hot, preferred_element_type=f32)
    rows = comps * high
    found = (found[:rows] + found[rows : 2 * rows]) + found[2 * rows :]
    return [
        jnp.sum(jnp.where(mask, found[c * high : (c + 1) * high], 0.0), 0, keepdims=True)
        for c in range(comps)
    ]


def cut_rows(force):
    return jnp.concatenate([piece.astype(f32) for piece in pieces_of(force)], 0)


def spread(ref, idx, high):
    mask = high_mask(idx, high)
    return jnp.concatenate(
        [jnp.where(mask, ref[r : r + 1, :], 0.0).astype(bf16) for r in range(3 * PIECES)], 0
    )


def add_hot(left, hot):
    return lax.dot_general(left, hot, (((1,), (1,)), ((), ())), preferred_element_type=f32)


def send_body(send_ref, disp_ref, ref_ref, seg_ref, mask_ref, own_ref, out_ref, tab, cut):
    high = disp_ref.shape[1] // LOW
    blocks = seg_ref.shape[0]
    for c in range(3):
        fill_table(tab, c * high, disp_ref, c, high)
    for c in range(3):
        for h in range(high):
            at = c * high + h
            tab[at : at + 1, :] += ref_ref[c : c + 1, h * LOW : (h + 1) * LOW]
    split_table(cut, tab)
    group = 8

    def some(g, carry):
        base = pl.multiple_of(g * group, group)
        seg = seg_ref[pl.ds(base, group), :]
        idx = jnp.concatenate([seg[k : k + 1] for k in range(group)], 1)
        xyz = pick(cut, low_hot(idx), high_mask(idx, high), 3, high)
        weight = mask_ref[pl.ds(base, group), :].astype(f32)
        for k in range(group):
            for c in range(3):
                own_ref[base + k, c : c + 1, :] = xyz[c][:, k * 128 : (k + 1) * 128]
            own_ref[base + k, 3:4, :] = weight[k : k + 1]
        return carry

    lax.fori_loop(0, blocks // group, some, 0, unroll=8)
    peers, cap = out_ref.shape[0], out_ref.shape[1]

    def send(d, carry):
        for c in range(cap):
            out_ref[d, c] = own_ref[send_ref[c, 0, d]]
        return carry

    lax.fori_loop(0, peers, send, 0, unroll=8)


def force_body(
    first_ref, stiff_ref, disp_ref, mass_ref, nodes_ref, part_ref, scale_ref, force_ref, lim_ref, tab, cut
):
    high = disp_ref.shape[1] // LOW
    width = WIDTH
    parts = stiff_ref.shape[0]
    for c in range(3):
        fill_table(tab, c * high, disp_ref, c, high)
    fill_table(tab, 3 * high, mass_ref, 0, high)
    split_table(cut, tab)

    def some(g, limit):
        at = pl.ds(pl.multiple_of(g * width, width), width)
        part = part_ref[:, at] - first_ref[0]
        stiff = jnp.zeros(part.shape, f32)
        for k in range(parts):
            stiff = jnp.where(part == k, stiff_ref[k], stiff)
        stiff = stiff * scale_ref[:, at]
        nodes = nodes_ref[:, at]
        idx = jnp.concatenate([nodes[k : k + 1] for k in range(4)], 1)
        found = pick(cut, low_hot(idx), high_mask(idx, high), 4, high)
        corner = [[found[c][:, k * width : (k + 1) * width] for c in range(4)] for k in range(4)]
        mass = jnp.minimum(
            jnp.minimum(corner[0][3], corner[1][3]), jnp.minimum(corner[2][3], corner[3][3])
        )
        force = [[jnp.zeros((1, width), f32)] * 3 for _ in range(4)]
        for head, tail, weight in SPRINGS:
            pull = weight * stiff
            for c in range(3):
                term = pull * (corner[tail][c] - corner[head][c])
                force[head][c] = force[head][c] + term
                force[tail][c] = force[tail][c] - term
        joined = [jnp.concatenate([force[k][c] for k in range(4)], 1) for c in range(3)]
        force_ref[g, 0:9] = cut_rows(jnp.concatenate(joined, 0))
        return jnp.minimum(limit, COURANT * jnp.sqrt(mass / stiff))

    limit = lax.fori_loop(
        0, nodes_ref.shape[1] // width, some, jnp.full((1, width), jnp.inf, f32), unroll=4
    )
    lim_ref[...] = jnp.broadcast_to(jnp.min(limit, 1, keepdims=True), lim_ref.shape)


def scatter_body(
    nodes_ref, force_ref, seg_ref, own, vel_ref, disp_ref, mass_ref, tot_ref, vel_out, disp_out, inv_out, acc, cut
):
    high = tot_ref.shape[0] // 3
    for c in range(3):
        fill_table(vel_out, c * high, vel_ref, c, high)
        fill_table(disp_out, c * high, disp_ref, c, high)
    fill_table(inv_out, 0, mass_ref, 0, high)
    inv_out[...] = 1.0 / inv_out[...]
    acc[...] = jnp.zeros_like(acc)

    def some(g, carry):
        at = pl.ds(pl.multiple_of(g * WIDTH, WIDTH), WIDTH)
        nodes = nodes_ref[:, at]
        idx = jnp.concatenate([nodes[k : k + 1] for k in range(4)], 1)
        acc[...] += add_hot(spread(force_ref.at[g], idx, high), low_hot(idx))
        return carry

    lax.fori_loop(0, force_ref.shape[0], some, 0, unroll=4)
    group = 8

    def more(g, carry):
        base = pl.multiple_of(g * group, group)
        seg = seg_ref[pl.ds(base, group), :]
        idx = jnp.concatenate([seg[k : k + 1] for k in range(group)], 1)
        cut[0:9] = cut_rows(jnp.concatenate([own[base + k] for k in range(group)], 1))
        acc[...] += add_hot(spread(cut, idx, high), low_hot(idx))
        return carry

    lax.fori_loop(0, seg_ref.shape[0] // group, more, 0, unroll=4)
    rows = 3 * high
    tot_ref[...] = (acc[2 * rows :] + acc[rows : 2 * rows]) + acc[:rows]


def contact_body(
    near_ref, far_ref, own_ref, recv_ref, live_ref, lim_ref, own_out, far_out, wide, total_a, total_b, recoils, landed, near, far, rows, chosen, sems
):
    blocks = total_a.shape[0]
    slots = landed.shape[0]
    seg = landed.shape[2]
    cap = 5
    fetch = pltpu.make_async_copy(recv_ref, landed, sems.at[0])
    fetch.start()

    group = 8
    line = lax.broadcasted_iota(jnp.int32, (16, 3 * seg), 0)
    part = lax.broadcasted_iota(jnp.int32, (16, 3 * seg), 1) >> 7
    hit = (line == part) | (line == part + 3) | (line == part + 6)
    hit = jnp.where(hit, 1.0, 0.0).astype(bf16)
    chosen[...] = jnp.zeros_like(chosen)
    for k in range(group):
        chosen[k, 16 * k : 16 * k + 16, :] = hit
    rows[...] = jnp.zeros_like(rows)

    def widen(g, carry):
        for k in range(group):
            block = own_ref[g * group + k]
            x = jnp.where(block[3:4] > 0.5, block[0:1] * SCALE, PARK)
            xyz = jnp.concatenate([x, block[1:3] * SCALE], 0)
            for p, piece in enumerate(pieces_of(xyz)):
                rows[16 * k + 3 * p : 16 * k + 3 * p + 3, :] = piece.astype(f32)
        columns = rows[...].T.astype(bf16)
        for k in range(group):
            out = jnp.dot(columns, chosen[k], preferred_element_type=f32)
            for c in range(3):
                wide[g * group + k, c] = out[:, c * seg : (c + 1) * seg]
                total_a[g * group + k, c] = jnp.zeros((seg, seg), f32)
                total_b[g * group + k, c] = jnp.zeros((seg, seg), f32)
        return carry

    lax.fori_loop(0, blocks // group, widen, 0, unroll=4)
    recoils[...] = jnp.zeros_like(recoils)
    live = jnp.sum(live_ref[...])
    fetch.wait()

    def pair(p, total):
        b = near_ref[p]
        s = far_ref[p]
        there = [jnp.broadcast_to(landed[s, c : c + 1, :], (8, seg)) for c in range(4)]
        x = jnp.where(there[3] > 0.5, there[0] * SCALE, -PARK)
        there = [x, there[1] * SCALE, there[2] * SCALE]
        recoil = [None] * 3
        for v in range(seg // 8):
            at = pl.ds(v * 8, 8)
            gap = [wide[b, c, at, :] - there[c] for c in range(3)]
            square = gap[0] * gap[0] + gap[1] * gap[1] + gap[2] * gap[2]
            weight = jnp.exp2(-square)
            for c in range(3):
                push = weight * gap[c]
                total[b, c, at, :] += push
                recoil[c] = push if recoil[c] is None else recoil[c] + push
        for c in range(3):
            recoils[c, pl.ds(pl.multiple_of(s * 8, 8), 8), :] += recoil[c]

    def four(q, carry):
        pair(8 * q, total_a)
        pair(8 * q + 1, total_b)
        pair(8 * q + 2, total_a)
        pair(8 * q + 3, total_b)
        pair(8 * q + 4, total_a)
        pair(8 * q + 5, total_b)
        pair(8 * q + 6, total_a)
        pair(8 * q + 7, total_b)
        return carry

    def one(p, carry):
        pair(p, total_a)
        return carry

    whole = live >> 3
    lax.fori_loop(0, whole, four, 0)
    lax.fori_loop(8 * whole, live, one, 0)
    peers = slots // cap
    stamp = jnp.broadcast_to(lim_ref[...], (8, seg))

    def finish(g, carry):
        for k in range(cap):
            for c in range(3):
                at = g * (64 * cap) + k * 8
                rows = [recoils[c, pl.ds(at + r, 8, stride=8 * cap), :] for r in range(8)]
                while len(rows) > 1:
                    rows = [x + y for x, y in zip(rows[::2], rows[1::2])]
                far[pl.ds(g * 128 + 3 * k + c, 8, stride=16), :] = rows[0] * (-1.0 / SCALE)
        far[pl.ds(g * 128 + 15, 8, stride=16), :] = stamp
        return carry

    lax.fori_loop(0, peers // 8, finish, 0, unroll=4)
    give_far = pltpu.make_async_copy(far, far_out, sems.at[1])
    give_far.start()

    def close(b, carry):
        total = total_a[b, 0] + total_b[b, 0]
        summed = lax.dot_general(
            jnp.ones((16, 3 * seg), bf16),
            jnp.concatenate(pieces_of(total), 1),
            (((1,), (1,)), ((), ())),
            preferred_element_type=f32,
        )
        near[b, 0:1, :] = summed[0:1] * (1.0 / SCALE)
        for c in (1, 2):
            total = total_a[b, c] + total_b[b, c]
            near[b, c : c + 1, :] = jnp.sum(total.T, 0, keepdims=True) * (1.0 / SCALE)
        return carry

    lax.fori_loop(0, blocks, close, 0, unroll=16)
    give_near = pltpu.make_async_copy(near, own_out, sems.at[2])
    give_near.start()
    give_far.wait()
    give_near.wait()


def seg_body(
    send_ref, back_ref, seg_ref, int_ref, share_ref, tot_ref, low_ref, up_ref, lim_ref, sums, cut, acc, rows
):
    blocks = seg_ref.shape[0]
    peers = back_ref.shape[0] // 16
    cap = 5
    high = int_ref.shape[0] // 3
    line = lax.broadcasted_iota(jnp.int32, (blocks, peers), 0)
    hot = jnp.concatenate(
        [jnp.where(line == send_ref[c], 1.0, 0.0).astype(bf16) for c in range(cap)], 1
    )
    for k in range(3):
        force = jnp.concatenate(
            [back_ref[pl.ds(3 * c + k, peers, stride=16), :] for c in range(cap)], 0
        )
        found = jnp.dot(hot, jnp.concatenate(pieces_of(force), 1), preferred_element_type=f32)
        sums[k] = (found[:, 256:] + found[:, 128:256]) + found[:, :128]
    acc[...] = jnp.zeros_like(acc)
    group = 8

    def some(g, carry):
        base = pl.multiple_of(g * group, group)
        seg = seg_ref[pl.ds(base, group), :]
        idx = jnp.concatenate([seg[k : k + 1] for k in range(group)], 1)
        force = [sums[c, pl.ds(base, group), :] for c in range(3)]
        force = [jnp.concatenate([f[k : k + 1] for k in range(group)], 1) for f in force]
        rows[0:9] = cut_rows(jnp.concatenate(force, 0))
        acc[...] += add_hot(spread(rows, idx, high), low_hot(idx))
        return carry

    lax.fori_loop(0, blocks // group, some, 0, unroll=4)
    size = 3 * high
    tot_ref[...] = ((acc[2 * size :] + acc[size : 2 * size]) + acc[:size]) + int_ref[...]
    split_table(cut, tot_ref)
    count = share_ref.shape[1]
    for row, out in ((0, low_ref), (1, up_ref)):
        for at in range(0, count, 1024):
            idx = share_ref[row : row + 1, at : at + 1024]
            picked = pick(cut, low_hot(idx), high_mask(idx, high), 3, high)
            for c in range(3):
                out[c : c + 1, at : at + 1024] = picked[c]
    lim = jnp.min(back_ref[pl.ds(15, peers, stride=16), :], 0, keepdims=True)
    lim_ref[...] = lim


def last_body(
    lim_ref, tot_ref, share_ref, low_ref, up_ref, vel_ref, disp_ref, inv_ref, new_disp, new_vel, cut
):
    high = tot_ref.shape[0] // 3
    count = share_ref.shape[1]
    total = jnp.zeros((PIECES * 3 * high, LOW), f32)
    for row, src in ((0, low_ref), (1, up_ref)):
        for k, at in enumerate(range(0, count, 1024)):
            idx = share_ref[row : row + 1, at : at + 1024]
            rows = cut.at[2 * row + k]
            rows[0:9] = cut_rows(src[:, at : at + 1024])
            total = total + add_hot(spread(rows, idx, high), low_hot(idx))
    size = 3 * high
    force = ((total[2 * size :] + total[size : 2 * size]) + total[:size]) + tot_ref[...]
    step = jnp.min(lim_ref[...], 1, keepdims=True)
    for c in range(3):
        at = slice(c * high, (c + 1) * high)
        vel = vel_ref[at] + step * (force[at] * inv_ref[...])
        disp = disp_ref[at] + step * vel
        for h in range(high):
            new_vel[c : c + 1, h * LOW : (h + 1) * LOW] = vel[h : h + 1]
            new_disp[c : c + 1, h * LOW : (h + 1) * LOW] = disp[h : h + 1]


def vmem(count):
    return [pl.BlockSpec(memory_space=pltpu.VMEM)] * count


def hbm(count):
    return [pl.BlockSpec(memory_space=pltpu.HBM)] * count


def smem(count):
    return [pl.BlockSpec(memory_space=pltpu.SMEM)] * count


def struct(*shape):
    return jax.ShapeDtypeStruct(shape, f32)


def send_call(send, disp, ref_pos, seg_node, seg_mask, peers):
    high = disp.shape[1] // LOW
    blocks, seg = seg_node.shape
    return pl.pallas_call(
        send_body,
        out_shape=(struct(blocks, 4, seg), struct(peers, send.shape[0], 4, seg)),
        in_specs=smem(1) + vmem(4),
        out_specs=tuple(vmem(2)),
        scratch_shapes=[
            pltpu.VMEM((3 * high, LOW), f32),
            pltpu.VMEM((PIECES * 3 * high, LOW), bf16),
        ],
    )(send, disp, ref_pos, seg_node, seg_mask)


def force_call(first, stiff, disp, mass, nodes, part, scale):
    high = disp.shape[1] // LOW
    return pl.pallas_call(
        force_body,
        out_shape=(struct(nodes.shape[1] // WIDTH, 16, 4 * WIDTH), struct(1, 128)),
        in_specs=smem(2) + vmem(5),
        out_specs=tuple(vmem(2)),
        scratch_shapes=[
            pltpu.VMEM((4 * high, LOW), f32),
            pltpu.VMEM((PIECES * 4 * high, LOW), bf16),
        ],
        compiler_params=pltpu.CompilerParams(vmem_limit_bytes=FULL_VMEM),
    )(first, stiff, disp, mass, nodes, part, scale)


def scatter_call(nodes, force, seg_node, own, vel, disp, mass):
    high = nodes.shape[1] // LOW
    return pl.pallas_call(
        scatter_body,
        out_shape=(struct(3 * high, LOW), struct(3 * high, LOW), struct(3 * high, LOW), struct(high, LOW)),
        in_specs=vmem(7),
        out_specs=tuple(vmem(4)),
        scratch_shapes=[
            pltpu.VMEM((PIECES * 3 * high, LOW), f32),
            pltpu.VMEM((16, 1024), f32),
        ],
        compiler_params=pltpu.CompilerParams(vmem_limit_bytes=SMALL_VMEM),
    )(nodes, force, seg_node, own, vel, disp, mass)


def contact_call(pair_a, pair_slot, own, recv, live, lim, peers):
    blocks, _, seg = own.shape
    slots = recv.shape[0]
    return pl.pallas_call(
        contact_body,
        out_shape=(struct(blocks, 3, seg), struct(peers * 16, seg)),
        in_specs=smem(2) + vmem(1) + hbm(1) + vmem(2),
        out_specs=tuple(hbm(2)),
        scratch_shapes=[
            pltpu.VMEM((blocks, 3, seg, seg), f32),
            pltpu.VMEM((blocks, 3, seg, seg), f32),
            pltpu.VMEM((blocks, 3, seg, seg), f32),
            pltpu.VMEM((3, slots * 8, seg), f32),
            pltpu.VMEM(recv.shape, f32),
            pltpu.VMEM((blocks, 3, seg), f32),
            pltpu.VMEM((peers * 16, seg), f32),
            pltpu.VMEM((seg, seg), f32),
            pltpu.VMEM((8, seg, 3 * seg), bf16),
            pltpu.SemaphoreType.DMA((3,)),
        ],
        compiler_params=pltpu.CompilerParams(vmem_limit_bytes=FULL_VMEM),
    )(pair_a, pair_slot, own, recv, live, lim)


def seg_call(send, back, seg_node, inner, shared):
    high = inner.shape[0] // 3
    count = shared.shape[1]
    return pl.pallas_call(
        seg_body,
        out_shape=(struct(3 * high, LOW), struct(3, count), struct(3, count), struct(1, 128)),
        in_specs=vmem(5),
        out_specs=tuple(vmem(4)),
        scratch_shapes=[
            pltpu.VMEM((3, seg_node.shape[0], 128), f32),
            pltpu.VMEM((PIECES * 3 * high, LOW), bf16),
            pltpu.VMEM((PIECES * 3 * high, LOW), f32),
            pltpu.VMEM((16, 1024), f32),
        ],
        compiler_params=pltpu.CompilerParams(vmem_limit_bytes=SMALL_VMEM),
    )(send, back.reshape(-1, 128), seg_node, inner, shared)


def last_call(lim, total, shared, lower, upper, vel, disp, inv):
    high = inv.shape[0]
    nodes = struct(3, high * LOW)
    return pl.pallas_call(
        last_body,
        out_shape=(nodes, nodes),
        in_specs=vmem(8),
        out_specs=tuple(vmem(2)),
        scratch_shapes=[pltpu.VMEM((4, 16, 1024), f32)],
        compiler_params=pltpu.CompilerParams(vmem_limit_bytes=SMALL_VMEM),
    )(lim, total, shared, lower, upper, vel, disp, inv)


def shifted(value, axis, steps):
    count = lax.axis_size(axis)
    first, last = (max(0, -steps), min(count, count - steps))
    return lax.ppermute(value, axis, [(source, source + steps) for source in range(first, last)])


def shards(
    ref_pos,
    displacement,
    velocity,
    node_mass,
    elem_nodes,
    elem_part,
    elem_scale,
    part_stiff,
    shared,
    seg_node,
    seg_mask,
    send_blk,
    pair_a,
    pair_slot,
    pair_mask,
):
    peers = lax.axis_size("grp") * lax.axis_size("dev")
    mass = node_mass.reshape(1, -1)
    send = send_blk.transpose(2, 0, 1)
    own, outgoing = send_call(send, displacement, ref_pos, seg_node, seg_mask, peers)
    arrived = lax.all_to_all(outgoing, ("grp", "dev"), split_axis=0, concat_axis=0, tiled=True)
    first = (lax.axis_index(("grp", "dev")) * part_stiff.shape[0]).reshape(1)
    force, limit = force_call(
        first,
        part_stiff,
        displacement,
        mass,
        elem_nodes,
        elem_part.reshape(1, -1),
        elem_scale.reshape(1, -1),
    )
    own_force, far_force = contact_call(
        pair_a,
        pair_slot,
        own,
        arrived.reshape(-1, 4, own.shape[2]),
        pair_mask.reshape(-1, 128),
        limit,
        peers,
    )
    back = lax.all_to_all(
        far_force.reshape(peers, 16, -1), ("grp", "dev"), split_axis=0, concat_axis=0, tiled=True
    )
    inner, vel, disp, inv = scatter_call(
        elem_nodes, force, seg_node, own_force, velocity, displacement, mass
    )
    total, low_rows, up_rows, limits = seg_call(send, back, seg_node, inner, shared)
    from_lower = shifted(up_rows, "dev", 1)
    from_upper = shifted(low_rows, "dev", -1)
    return last_call(limits, total, shared, from_lower, from_upper, vel, disp, inv)


def solution(mesh):
    both = ("grp", "dev")
    return jax.shard_map(
        shards,
        mesh=mesh,
        in_specs=(
            P(None, both),
            P(None, both),
            P(None, both),
            P(both),
            P(None, both),
            P(both),
            P(both),
            P(both),
            P(None, both),
            P(both, None),
            P(both, None),
            P(both, None, None),
            P(both),
            P(both),
            P(both),
        ),
        out_specs=(P(None, both), P(None, both)),
        check_vma=False,
    )
```

```python
import math
from functools import partial

import jax
import jax.numpy as jnp
from jax import lax
from jax.experimental import pallas as pl
from jax.experimental.pallas import tpu as pltpu
from jax.sharding import PartitionSpec as P

SPRINGS = ((0, 1, 1.0), (1, 2, 1.0), (2, 3, 1.0), (3, 0, 1.0), (0, 2, 0.5), (1, 3, 0.5))
COURANT = 0.5
LOW = 256
PIECES = 3
FULL_VMEM = 64 << 20
SMALL_VMEM = 16 << 20
WIDTH = 256
SCALE = math.sqrt(math.log2(math.e))
PARK = 1.0e3
f32 = jnp.float32
bf16 = jnp.bfloat16


def pieces_of(x, count=PIECES):
    out = []
    for _ in range(count):
        head = x.astype(bf16)
        out.append(head)
        x = x - head.astype(f32)
    return out


def low_hot(idx):
    low = jnp.broadcast_to((idx & (LOW - 1)).astype(f32), (16, idx.shape[1])).astype(bf16)
    line = lax.broadcasted_iota(jnp.int32, low.shape, 0).astype(f32).astype(bf16)
    one, zero = jnp.ones(low.shape, bf16), jnp.zeros(low.shape, bf16)
    return jnp.concatenate(
        [jnp.where(low == line + float(16 * k), one, zero) for k in range(LOW // 16)], 0
    )


def high_mask(idx, high):
    rows = lax.broadcasted_iota(jnp.int32, (high, idx.shape[1]), 0)
    return rows == (idx >> 8)


def fill_table(tab, at, ref, row, high):
    for h in range(high):
        tab[at + h : at + h + 1, :] = ref[row : row + 1, h * LOW : (h + 1) * LOW]


def split_table(cut, tab):
    rows = tab.shape[0]
    for p, piece in enumerate(pieces_of(tab[...])):
        cut[p * rows : (p + 1) * rows, :] = piece


def pick(cut, hot, mask, comps, high):
    found = jnp.dot(cut[...], hot, preferred_element_type=f32)
    rows = comps * high
    found = (found[:rows] + found[rows : 2 * rows]) + found[2 * rows :]
    return [
        jnp.sum(jnp.where(mask, found[c * high : (c + 1) * high], 0.0), 0, keepdims=True)
        for c in range(comps)
    ]


def cut_rows(force):
    return jnp.concatenate([piece.astype(f32) for piece in pieces_of(force)], 0)


def spread(ref, idx, high):
    mask = high_mask(idx, high)
    return jnp.concatenate(
        [jnp.where(mask, ref[r : r + 1, :], 0.0).astype(bf16) for r in range(3 * PIECES)], 0
    )


def add_hot(left, hot):
    return lax.dot_general(left, hot, (((1,), (1,)), ((), ())), preferred_element_type=f32)


def send_body(send_ref, disp_ref, ref_ref, seg_ref, mask_ref, own_ref, out_ref, tab, cut):
    high = disp_ref.shape[1] // LOW
    blocks = seg_ref.shape[0]
    for c in range(3):
        fill_table(tab, c * high, disp_ref, c, high)
    for c in range(3):
        for h in range(high):
            at = c * high + h
            tab[at : at + 1, :] += ref_ref[c : c + 1, h * LOW : (h + 1) * LOW]
    split_table(cut, tab)
    group = 8

    def some(g, carry):
        base = pl.multiple_of(g * group, group)
        seg = seg_ref[pl.ds(base, group), :]
        idx = jnp.concatenate([seg[k : k + 1] for k in range(group)], 1)
        xyz = pick(cut, low_hot(idx), high_mask(idx, high), 3, high)
        weight = mask_ref[pl.ds(base, group), :].astype(f32)
        for k in range(group):
            for c in range(3):
                own_ref[base + k, c : c + 1, :] = xyz[c][:, k * 128 : (k + 1) * 128]
            own_ref[base + k, 3:4, :] = weight[k : k + 1]
        return carry

    lax.fori_loop(0, blocks // group, some, 0, unroll=8)
    peers, cap = out_ref.shape[0], out_ref.shape[1]

    def send(d, carry):
        for c in range(cap):
            out_ref[d, c] = own_ref[send_ref[c, 0, d]]
        return carry

    lax.fori_loop(0, peers, send, 0, unroll=16)


def force_body(
    first_ref, stiff_ref, disp_ref, mass_ref, nodes_ref, part_ref, scale_ref, force_ref, lim_ref, tab, cut
):
    high = disp_ref.shape[1] // LOW
    width = WIDTH
    parts = stiff_ref.shape[0]
    for c in range(3):
        fill_table(tab, c * high, disp_ref, c, high)
    fill_table(tab, 3 * high, mass_ref, 0, high)
    split_table(cut, tab)

    def some(g, limit):
        at = pl.ds(pl.multiple_of(g * width, width), width)
        part = part_ref[:, at] - first_ref[0]
        stiff = jnp.zeros(part.shape, f32)
        for k in range(parts):
            stiff = jnp.where(part == k, stiff_ref[k], stiff)
        stiff = stiff * scale_ref[:, at]
        nodes = nodes_ref[:, at]
        idx = jnp.concatenate([nodes[k : k + 1] for k in range(4)], 1)
        found = pick(cut, low_hot(idx), high_mask(idx, high), 4, high)
        corner = [[found[c][:, k * width : (k + 1) * width] for c in range(4)] for k in range(4)]
        mass = jnp.minimum(
            jnp.minimum(corner[0][3], corner[1][3]), jnp.minimum(corner[2][3], corner[3][3])
        )
        force = [[jnp.zeros((1, width), f32)] * 3 for _ in range(4)]
        for head, tail, weight in SPRINGS:
            pull = weight * stiff
            for c in range(3):
                term = pull * (corner[tail][c] - corner[head][c])
                force[head][c] = force[head][c] + term
                force[tail][c] = force[tail][c] - term
        joined = [jnp.concatenate([force[k][c] for k in range(4)], 1) for c in range(3)]
        force_ref[g, 0:9] = cut_rows(jnp.concatenate(joined, 0))
        return jnp.minimum(limit, COURANT * jnp.sqrt(mass / stiff))

    limit = lax.fori_loop(
        0, nodes_ref.shape[1] // width, some, jnp.full((1, width), jnp.inf, f32), unroll=4
    )
    lim_ref[...] = jnp.broadcast_to(jnp.min(limit, 1, keepdims=True), lim_ref.shape)


def scatter_body(
    nodes_ref, force_ref, seg_ref, own, vel_ref, disp_ref, mass_ref, tot_ref, vel_out, disp_out, inv_out, acc, cut
):
    high = tot_ref.shape[0] // 3
    for c in range(3):
        fill_table(vel_out, c * high, vel_ref, c, high)
        fill_table(disp_out, c * high, disp_ref, c, high)
    fill_table(inv_out, 0, mass_ref, 0, high)
    inv_out[...] = 1.0 / inv_out[...]
    acc[...] = jnp.zeros_like(acc)

    def some(g, carry):
        at = pl.ds(pl.multiple_of(g * WIDTH, WIDTH), WIDTH)
        nodes = nodes_ref[:, at]
        idx = jnp.concatenate([nodes[k : k + 1] for k in range(4)], 1)
        acc[...] += add_hot(spread(force_ref.at[g], idx, high), low_hot(idx))
        return carry

    lax.fori_loop(0, force_ref.shape[0], some, 0, unroll=4)
    group = 8

    def more(g, carry):
        base = pl.multiple_of(g * group, group)
        seg = seg_ref[pl.ds(base, group), :]
        idx = jnp.concatenate([seg[k : k + 1] for k in range(group)], 1)
        cut[0:9] = cut_rows(jnp.concatenate([own[base + k] for k in range(group)], 1))
        acc[...] += add_hot(spread(cut, idx, high), low_hot(idx))
        return carry

    lax.fori_loop(0, seg_ref.shape[0] // group, more, 0, unroll=4)
    rows = 3 * high
    tot_ref[...] = (acc[2 * rows :] + acc[rows : 2 * rows]) + acc[:rows]


def contact_body(
    near_ref, far_ref, own_ref, recv_ref, live_ref, lim_ref, own_out, far_out, wide, total_a, total_b, recoils, landed, near, far, rows, chosen, sems
):
    blocks = total_a.shape[0]
    slots = landed.shape[0]
    seg = landed.shape[2]
    cap = 5
    fetch = pltpu.make_async_copy(recv_ref, landed, sems.at[0])
    fetch.start()

    group = 8
    line = lax.broadcasted_iota(jnp.int32, (16, 3 * seg), 0)
    part = lax.broadcasted_iota(jnp.int32, (16, 3 * seg), 1) >> 7
    hit = (line == part) | (line == part + 3) | (line == part + 6)
    hit = jnp.where(hit, 1.0, 0.0).astype(bf16)
    chosen[...] = jnp.zeros_like(chosen)
    for k in range(group):
        chosen[k, 16 * k : 16 * k + 16, :] = hit
    rows[...] = jnp.zeros_like(rows)

    def widen(g, carry):
        for k in range(group):
            block = own_ref[g * group + k]
            x = jnp.where(block[3:4] > 0.5, block[0:1] * SCALE, PARK)
            xyz = jnp.concatenate([x, block[1:3] * SCALE], 0)
            for p, piece in enumerate(pieces_of(xyz)):
                rows[16 * k + 3 * p : 16 * k + 3 * p + 3, :] = piece.astype(f32)
        columns = rows[...].T.astype(bf16)
        for k in range(group):
            out = jnp.dot(columns, chosen[k], preferred_element_type=f32)
            for c in range(3):
                wide[g * group + k, c] = out[:, c * seg : (c + 1) * seg]
                total_a[g * group + k, c] = jnp.zeros((seg, seg), f32)
                total_b[g * group + k, c] = jnp.zeros((seg, seg), f32)
        return carry

    lax.fori_loop(0, blocks // group, widen, 0, unroll=4)
    recoils[...] = jnp.zeros_like(recoils)
    live = jnp.sum(live_ref[...])
    fetch.wait()

    def pair(p, total):
        b = near_ref[p]
        s = far_ref[p]
        there = [jnp.broadcast_to(landed[s, c : c + 1, :], (8, seg)) for c in range(4)]
        x = jnp.where(there[3] > 0.5, there[0] * SCALE, -PARK)
        there = [x, there[1] * SCALE, there[2] * SCALE]
        recoil = [None] * 3
        for v in range(seg // 8):
            at = pl.ds(v * 8, 8)
            gap = [wide[b, c, at, :] - there[c] for c in range(3)]
            square = gap[0] * gap[0] + gap[1] * gap[1] + gap[2] * gap[2]
            weight = jnp.exp2(-square)
            for c in range(3):
                push = weight * gap[c]
                total[b, c, at, :] += push
                recoil[c] = push if recoil[c] is None else recoil[c] + push
        for c in range(3):
            recoils[c, pl.ds(pl.multiple_of(s * 8, 8), 8), :] += recoil[c]

    def four(q, carry):
        pair(8 * q, total_a)
        pair(8 * q + 1, total_b)
        pair(8 * q + 2, total_a)
        pair(8 * q + 3, total_b)
        pair(8 * q + 4, total_a)
        pair(8 * q + 5, total_b)
        pair(8 * q + 6, total_a)
        pair(8 * q + 7, total_b)
        return carry

    def one(p, carry):
        pair(p, total_a)
        return carry

    whole = live >> 3
    lax.fori_loop(0, whole, four, 0)
    lax.fori_loop(8 * whole, live, one, 0)
    peers = slots // cap
    stamp = jnp.broadcast_to(lim_ref[...], (8, seg))

    def finish(g, carry):
        for k in range(cap):
            for c in range(3):
                at = g * (64 * cap) + k * 8
                rows = [recoils[c, pl.ds(at + r, 8, stride=8 * cap), :] for r in range(8)]
                while len(rows) > 1:
                    rows = [x + y for x, y in zip(rows[::2], rows[1::2])]
                far[pl.ds(g * 128 + 3 * k + c, 8, stride=16), :] = rows[0] * (-1.0 / SCALE)
        far[pl.ds(g * 128 + 15, 8, stride=16), :] = stamp
        return carry

    lax.fori_loop(0, peers // 8, finish, 0, unroll=4)
    give_far = pltpu.make_async_copy(far, far_out, sems.at[1])
    give_far.start()

    def close(b, carry):
        total = total_a[b, 0] + total_b[b, 0]
        summed = lax.dot_general(
            jnp.ones((16, 3 * seg), bf16),
            jnp.concatenate(pieces_of(total), 1),
            (((1,), (1,)), ((), ())),
            preferred_element_type=f32,
        )
        near[b, 0:1, :] = summed[0:1] * (1.0 / SCALE)
        for c in (1, 2):
            total = total_a[b, c] + total_b[b, c]
            near[b, c : c + 1, :] = jnp.sum(total.T, 0, keepdims=True) * (1.0 / SCALE)
        return carry

    lax.fori_loop(0, blocks, close, 0, unroll=16)
    give_near = pltpu.make_async_copy(near, own_out, sems.at[2])
    give_near.start()
    give_far.wait()
    give_near.wait()


def seg_body(
    send_ref, back_ref, seg_ref, int_ref, share_ref, tot_ref, low_ref, up_ref, lim_ref, sums, cut, acc, rows
):
    blocks = seg_ref.shape[0]
    peers = back_ref.shape[0] // 16
    cap = 5
    high = int_ref.shape[0] // 3
    line = lax.broadcasted_iota(jnp.int32, (blocks, peers), 0)
    hot = jnp.concatenate(
        [jnp.where(line == send_ref[c], 1.0, 0.0).astype(bf16) for c in range(cap)], 1
    )
    for k in range(3):
        force = jnp.concatenate(
            [back_ref[pl.ds(3 * c + k, peers, stride=16), :] for c in range(cap)], 0
        )
        found = jnp.dot(hot, jnp.concatenate(pieces_of(force), 1), preferred_element_type=f32)
        sums[k] = (found[:, 256:] + found[:, 128:256]) + found[:, :128]
    acc[...] = jnp.zeros_like(acc)
    group = 8

    def some(g, carry):
        base = pl.multiple_of(g * group, group)
        seg = seg_ref[pl.ds(base, group), :]
        idx = jnp.concatenate([seg[k : k + 1] for k in range(group)], 1)
        force = [sums[c, pl.ds(base, group), :] for c in range(3)]
        force = [jnp.concatenate([f[k : k + 1] for k in range(group)], 1) for f in force]
        rows[0:9] = cut_rows(jnp.concatenate(force, 0))
        acc[...] += add_hot(spread(rows, idx, high), low_hot(idx))
        return carry

    lax.fori_loop(0, blocks // group, some, 0, unroll=4)
    size = 3 * high
    tot_ref[...] = ((acc[2 * size :] + acc[size : 2 * size]) + acc[:size]) + int_ref[...]
    split_table(cut, tot_ref)
    count = share_ref.shape[1]
    for row, out in ((0, low_ref), (1, up_ref)):
        for at in range(0, count, 1024):
            idx = share_ref[row : row + 1, at : at + 1024]
            picked = pick(cut, low_hot(idx), high_mask(idx, high), 3, high)
            for c in range(3):
                out[c : c + 1, at : at + 1024] = picked[c]
    lim = jnp.min(back_ref[pl.ds(15, peers, stride=16), :], 0, keepdims=True)
    lim_ref[...] = lim


def last_body(
    lim_ref, tot_ref, share_ref, low_ref, up_ref, vel_ref, disp_ref, inv_ref, new_disp, new_vel, cut
):
    high = tot_ref.shape[0] // 3
    count = share_ref.shape[1]
    total = jnp.zeros((PIECES * 3 * high, LOW), f32)
    for row, src in ((0, low_ref), (1, up_ref)):
        for k, at in enumerate(range(0, count, 1024)):
            idx = share_ref[row : row + 1, at : at + 1024]
            rows = cut.at[2 * row + k]
            rows[0:9] = cut_rows(src[:, at : at + 1024])
            total = total + add_hot(spread(rows, idx, high), low_hot(idx))
    size = 3 * high
    force = ((total[2 * size :] + total[size : 2 * size]) + total[:size]) + tot_ref[...]
    step = jnp.min(lim_ref[...], 1, keepdims=True)
    for c in range(3):
        at = slice(c * high, (c + 1) * high)
        vel = vel_ref[at] + step * (force[at] * inv_ref[...])
        disp = disp_ref[at] + step * vel
        for h in range(high):
            new_vel[c : c + 1, h * LOW : (h + 1) * LOW] = vel[h : h + 1]
            new_disp[c : c + 1, h * LOW : (h + 1) * LOW] = disp[h : h + 1]


def vmem(count):
    return [pl.BlockSpec(memory_space=pltpu.VMEM)] * count


def hbm(count):
    return [pl.BlockSpec(memory_space=pltpu.HBM)] * count


def smem(count):
    return [pl.BlockSpec(memory_space=pltpu.SMEM)] * count


def struct(*shape):
    return jax.ShapeDtypeStruct(shape, f32)


def send_call(send, disp, ref_pos, seg_node, seg_mask, peers):
    high = disp.shape[1] // LOW
    blocks, seg = seg_node.shape
    return pl.pallas_call(
        send_body,
        out_shape=(struct(blocks, 4, seg), struct(peers, send.shape[0], 4, seg)),
        in_specs=smem(1) + vmem(4),
        out_specs=tuple(vmem(2)),
        scratch_shapes=[
            pltpu.VMEM((3 * high, LOW), f32),
            pltpu.VMEM((PIECES * 3 * high, LOW), bf16),
        ],
    )(send, disp, ref_pos, seg_node, seg_mask)


def force_call(first, stiff, disp, mass, nodes, part, scale):
    high = disp.shape[1] // LOW
    return pl.pallas_call(
        force_body,
        out_shape=(struct(nodes.shape[1] // WIDTH, 16, 4 * WIDTH), struct(1, 128)),
        in_specs=smem(2) + vmem(5),
        out_specs=tuple(vmem(2)),
        scratch_shapes=[
            pltpu.VMEM((4 * high, LOW), f32),
            pltpu.VMEM((PIECES * 4 * high, LOW), bf16),
        ],
        compiler_params=pltpu.CompilerParams(vmem_limit_bytes=FULL_VMEM),
    )(first, stiff, disp, mass, nodes, part, scale)


def scatter_call(nodes, force, seg_node, own, vel, disp, mass):
    high = nodes.shape[1] // LOW
    return pl.pallas_call(
        scatter_body,
        out_shape=(struct(3 * high, LOW), struct(3 * high, LOW), struct(3 * high, LOW), struct(high, LOW)),
        in_specs=vmem(7),
        out_specs=tuple(vmem(4)),
        scratch_shapes=[
            pltpu.VMEM((PIECES * 3 * high, LOW), f32),
            pltpu.VMEM((16, 1024), f32),
        ],
        compiler_params=pltpu.CompilerParams(vmem_limit_bytes=SMALL_VMEM),
    )(nodes, force, seg_node, own, vel, disp, mass)


def contact_call(pair_a, pair_slot, own, recv, live, lim, peers):
    blocks, _, seg = own.shape
    slots = recv.shape[0]
    return pl.pallas_call(
        contact_body,
        out_shape=(struct(blocks, 3, seg), struct(peers * 16, seg)),
        in_specs=smem(2) + vmem(1) + hbm(1) + vmem(2),
        out_specs=tuple(hbm(2)),
        scratch_shapes=[
            pltpu.VMEM((blocks, 3, seg, seg), f32),
            pltpu.VMEM((blocks, 3, seg, seg), f32),
            pltpu.VMEM((blocks, 3, seg, seg), f32),
            pltpu.VMEM((3, slots * 8, seg), f32),
            pltpu.VMEM(recv.shape, f32),
            pltpu.VMEM((blocks, 3, seg), f32),
            pltpu.VMEM((peers * 16, seg), f32),
            pltpu.VMEM((seg, seg), f32),
            pltpu.VMEM((8, seg, 3 * seg), bf16),
            pltpu.SemaphoreType.DMA((3,)),
        ],
        compiler_params=pltpu.CompilerParams(vmem_limit_bytes=FULL_VMEM),
    )(pair_a, pair_slot, own, recv, live, lim)


def seg_call(send, back, seg_node, inner, shared):
    high = inner.shape[0] // 3
    count = shared.shape[1]
    return pl.pallas_call(
        seg_body,
        out_shape=(struct(3 * high, LOW), struct(3, count), struct(3, count), struct(1, 128)),
        in_specs=vmem(5),
        out_specs=tuple(vmem(4)),
        scratch_shapes=[
            pltpu.VMEM((3, seg_node.shape[0], 128), f32),
            pltpu.VMEM((PIECES * 3 * high, LOW), bf16),
            pltpu.VMEM((PIECES * 3 * high, LOW), f32),
            pltpu.VMEM((16, 1024), f32),
        ],
        compiler_params=pltpu.CompilerParams(vmem_limit_bytes=SMALL_VMEM),
    )(send, back.reshape(-1, 128), seg_node, inner, shared)


def last_call(lim, total, shared, lower, upper, vel, disp, inv):
    high = inv.shape[0]
    nodes = struct(3, high * LOW)
    return pl.pallas_call(
        last_body,
        out_shape=(nodes, nodes),
        in_specs=vmem(8),
        out_specs=tuple(vmem(2)),
        scratch_shapes=[pltpu.VMEM((4, 16, 1024), f32)],
        compiler_params=pltpu.CompilerParams(vmem_limit_bytes=SMALL_VMEM),
    )(lim, total, shared, lower, upper, vel, disp, inv)


def shifted(value, axis, steps):
    count = lax.axis_size(axis)
    first, last = (max(0, -steps), min(count, count - steps))
    return lax.ppermute(value, axis, [(source, source + steps) for source in range(first, last)])


def shards(
    ref_pos,
    displacement,
    velocity,
    node_mass,
    elem_nodes,
    elem_part,
    elem_scale,
    part_stiff,
    shared,
    seg_node,
    seg_mask,
    send_blk,
    pair_a,
    pair_slot,
    pair_mask,
):
    peers = lax.axis_size("grp") * lax.axis_size("dev")
    mass = node_mass.reshape(1, -1)
    send = send_blk.transpose(2, 0, 1)
    own, outgoing = send_call(send, displacement, ref_pos, seg_node, seg_mask, peers)
    arrived = lax.all_to_all(outgoing, ("grp", "dev"), split_axis=0, concat_axis=0, tiled=True)
    first = (lax.axis_index(("grp", "dev")) * part_stiff.shape[0]).reshape(1)
    force, limit = force_call(
        first,
        part_stiff,
        displacement,
        mass,
        elem_nodes,
        elem_part.reshape(1, -1),
        elem_scale.reshape(1, -1),
    )
    own_force, far_force = contact_call(
        pair_a,
        pair_slot,
        own,
        arrived.reshape(-1, 4, own.shape[2]),
        pair_mask.reshape(-1, 128),
        limit,
        peers,
    )
    back = lax.all_to_all(
        far_force.reshape(peers, 16, -1), ("grp", "dev"), split_axis=0, concat_axis=0, tiled=True
    )
    inner, vel, disp, inv = scatter_call(
        elem_nodes, force, seg_node, own_force, velocity, displacement, mass
    )
    total, low_rows, up_rows, limits = seg_call(send, back, seg_node, inner, shared)
    from_lower = shifted(up_rows, "dev", 1)
    from_upper = shifted(low_rows, "dev", -1)
    return last_call(limits, total, shared, from_lower, from_upper, vel, disp, inv)


def solution(mesh):
    both = ("grp", "dev")
    return jax.shard_map(
        shards,
        mesh=mesh,
        in_specs=(
            P(None, both),
            P(None, both),
            P(None, both),
            P(both),
            P(None, both),
            P(both),
            P(both),
            P(both),
            P(None, both),
            P(both, None),
            P(both, None),
            P(both, None, None),
            P(both),
            P(both),
            P(both),
        ),
        out_specs=(P(None, both), P(None, both)),
        check_vma=False,
    )
```
